32 devices in a mesh: island: 8 (over z, x), fsdp: 4 (over y, core).
Axes of the slice: x: 2, y: 2, z: 4, core: 2. Of those that a mesh axis runs over, the one named last changes fastest.
Arguments:
- local_weights: bfloat16 [8, 4096, 512], P('island', 'fsdp'), may hold values from -6 to 6
- adam_first: bfloat16 [8, 4096, 512], P('island', 'fsdp'), may hold values from -6 to 6
- adam_second: bfloat16 [8, 4096, 512], P('island', 'fsdp'), may hold values from 0.5 to 4
- global_weights: float32 [4096, 512], P('fsdp'), may hold values from -6 to 6
- outer_momentum: float32 [4096, 512], P('fsdp'), may hold values from -3 to 3
- inputs: bfloat16 [8, 512, 4096], P('island', 'fsdp'), may hold values from -6 to 6
- key_cotangent: bfloat16 [8, 512, 512], P('island', 'fsdp'), may hold values from -24 to 24
Outputs:
- new_local: bfloat16 [8, 4096, 512], P('island', 'fsdp')
- new_first: bfloat16 [8, 4096, 512], P('island', 'fsdp')
- new_second: bfloat16 [8, 4096, 512], P('island', 'fsdp')
- new_global: float32 [4096, 512], P('fsdp')
- new_momentum: float32 [4096, 512], P('fsdp')
The draws below stay inside these ranges and needn't reach their ends.
All inputs are finite; a program needn't handle non-finite values.
Results may differ from the reference program's by a relative error of at most 0.0065.
Values may be sent and summed in bfloat16 or wider, within the bound.
A program may use at most 64 MiB of HBM per device.

```python
import math
import jax
import jax.numpy as jnp
from jax import lax

D = 4096
KV_HEADS = 4
HEAD_DIM = 128
TOK_DEV = 128
KEY_WIDTH = 512
ISLAND_TOKENS = 512
N_ISLAND = 8
N_FSDP = 4


def level_of(rng, shape, cuts, smallest, top_value):
    gain = 1.0
    for dim, blocks in cuts:
        draws = jax.random.uniform(jax.random.fold_in(jax.random.fold_in(rng, 6), dim), (blocks,), jnp.float32, smallest / len(cuts), top_value / len(cuts))
        gain = gain * jnp.repeat(jnp.exp(draws), shape[dim] // blocks).reshape((-1,) + (1,) * (len(shape) - 1 - dim))
    return gain


def centred(own_key, extent, width, most, split=(), dtype=jnp.bfloat16):
    result = width * jax.random.normal(own_key, extent, jnp.float32)
    if split:
        result = result * level_of(own_key, extent, split, -0.22, 0.18)
    return jnp.clip(result, -most, most).astype(dtype)


def setup_inputs(seed: int = 0) -> dict:
    key_list = jax.random.split(jax.random.key(seed), 8)
    local_weights = centred(key_list[0], (N_ISLAND, D, KEY_WIDTH), 1.0, 6.0, ((0, 8), (1, 4)))
    adam_first = centred(key_list[1], (N_ISLAND, D, KEY_WIDTH), 1.0, 6.0, ((0, 8), (1, 4)))
    adam_second = jnp.clip(jnp.exp(math.log(4.0) - 2.0794415 * jax.random.uniform(key_list[2], (N_ISLAND, D, KEY_WIDTH), jnp.float32) ** level_of(key_list[2], (N_ISLAND, D, KEY_WIDTH), ((0, 8), (1, 4)), -0.2, 0.2)), 0.5, 4.0).astype(jnp.bfloat16)
    global_weights = centred(key_list[3], (D, KEY_WIDTH), 1.0, 6.0, ((0, 4),), jnp.float32)
    outer_momentum = centred(key_list[4], (D, KEY_WIDTH), 0.5, 3.0, ((0, 4),), jnp.float32)
    inputs = centred(key_list[5], (N_ISLAND, ISLAND_TOKENS, D), 1.0, 6.0, ((0, 8), (1, 4)))
    key_cotangent = centred(key_list[6], (N_ISLAND, ISLAND_TOKENS, KEY_WIDTH), 4.0, 24.0, ((0, 8), (1, 4)))
    return dict(local_weights=local_weights, adam_first=adam_first, adam_second=adam_second, global_weights=global_weights, outer_momentum=outer_momentum, inputs=inputs, key_cotangent=key_cotangent)


beta_one = 0.9
beta_two = 0.95
inner_rate = 0.02
weight_decay = 0.1
adam_epsilon = 1e-08
norm_epsilon = 1e-06
outer_rate = 0.7
outer_beta = 0.9
merge_weight = 0.5

def key_backward(keys, upstream):
    shaped = keys.reshape(keys.shape[0], KV_HEADS, HEAD_DIM)
    cotan_heads = upstream.reshape(keys.shape[0], KV_HEADS, HEAD_DIM)
    squares = lax.optimization_barrier(jnp.mean(shaped * shaped, axis=-1, keepdims=True))
    inverse = lax.rsqrt(squares + norm_epsilon)
    normed = shaped * inverse
    projected = lax.optimization_barrier(jnp.mean(cotan_heads * normed, axis=-1, keepdims=True))
    return (inverse * (cotan_heads - normed * projected)).reshape(keys.shape)

def reference(local_weights, adam_first, adam_second, global_weights, outer_momentum, inputs, key_cotangent):
    summed = lax.optimization_barrier(jnp.sum(local_weights.astype(jnp.float32), axis=0))
    outer_grad = global_weights - summed / N_ISLAND
    new_momentum = outer_beta * outer_momentum + outer_grad
    new_global = global_weights - outer_rate * (outer_grad + outer_beta * new_momentum)
    scale = float(D) ** (-0.5)

    def island_update(packed):
        weights, first_moment, second_moment, tokens, upstream = packed
        keys = jnp.dot(tokens, weights, preferred_element_type=jnp.float32) * scale
        key_grad = (key_backward(keys, upstream.astype(jnp.float32)) * scale).astype(jnp.bfloat16)
        blocks = jnp.einsum('ntd,ntk->ndk', tokens.reshape(N_FSDP, TOK_DEV, D).astype(jnp.float32), key_grad.reshape(N_FSDP, TOK_DEV, KEY_WIDTH).astype(jnp.float32))
        rounded = lax.optimization_barrier(blocks.astype(jnp.bfloat16))
        gradient = lax.optimization_barrier(jnp.sum(rounded.astype(jnp.float32), axis=0))
        first_new = beta_one * first_moment.astype(jnp.float32) + (1.0 - beta_one) * gradient
        second_new = beta_two * second_moment.astype(jnp.float32) + (1.0 - beta_two) * gradient * gradient
        current = weights.astype(jnp.float32)
        inner = current - inner_rate * (first_new / (jnp.sqrt(second_new) + adam_epsilon) + weight_decay * current)
        merged = merge_weight * inner + (1.0 - merge_weight) * new_global
        return (merged.astype(jnp.bfloat16), first_new.astype(jnp.bfloat16), second_new.astype(jnp.bfloat16))
    new_local, new_first, new_second = lax.map(island_update, (local_weights, adam_first, adam_second, inputs, key_cotangent))
    return (new_local, new_first, new_second, new_global, new_momentum)
```

```python
import functools

import jax
import jax.numpy as jnp
from jax import lax
from jax.experimental import pallas as pl
from jax.experimental.pallas import tpu as pltpu
from jax.sharding import PartitionSpec as P

HEAD_DIM = 128
MESH = pl.DeviceIdType.MESH

beta_one = 0.9
beta_two = 0.95
inner_rate = 0.02
weight_decay = 0.1
adam_epsilon = 1e-08
norm_epsilon = 1e-06
outer_rate = 0.7
outer_beta = 0.9
merge_weight = 0.5


def chunk_count(rows, islands):
    for chunks in (8, 4, 2, 1):
        if islands & (islands - 1) == 0 and rows % (islands * chunks * 16) == 0:
            return chunks
    return 0


def head_backward(keys, upstream, scale):
    squares = jnp.mean(keys * keys, axis=-1, keepdims=True)
    inverse = lax.rsqrt(squares + norm_epsilon)
    normed = keys * inverse
    projected = jnp.mean(upstream * normed, axis=-1, keepdims=True)
    return (inverse * (upstream - normed * projected) * scale).astype(jnp.bfloat16)


def exchange(islands, shards, chunks, scale, *refs):
    w_hbm, x_hbm, cot_hbm = refs[:3]
    if chunks:
        (grad, mean, w, x, cot, lsem, wp, xin, xp, psend, precv, kgin, kgp, kg, own,
         ysem, psem, ksem, csem, fsem, landed, part, gathered, hsem) = refs[3:]
    else:
        (grad, w, x, cot, lsem, wp, xin, xp, psend, precv, kgin, kgp, kg, own,
         ysem, psem, ksem, csem, fsem) = refs[3:]
    rows, width = w.shape
    chips = shards // 2
    island = lax.axis_index("island")
    shard = lax.axis_index("fsdp")
    core = lax.rem(shard, 2)
    chip = shard // 2
    partner = (island, chip * 2 + 1 - core)

    def peer(step):
        return (island, lax.rem(chip + step, chips) * 2 + core)

    def back(step):
        return (island, lax.rem(chip + chips - step, chips) * 2 + core)

    targets = [partner] + [peer(step) for step in range(1, chips)]
    if chunks:
        levels = islands.bit_length() - 1
        sides = [lax.rem(island // 2**bit, 2) for bit in range(levels)]
        mates = [(island + (1 - 2 * sides[bit]) * 2**bit, shard) for bit in range(levels)]
        targets += mates

    loads = [
        pltpu.make_async_copy(source, place, lsem.at[index])
        for index, (source, place) in enumerate(((w_hbm, w), (x_hbm, x), (cot_hbm, cot)))
    ]
    for load in loads:
        load.start()

    barrier = pltpu.get_barrier_semaphore()
    for target in targets:
        pl.semaphore_signal(barrier, inc=1, device_id=target, device_id_type=MESH)
    pl.semaphore_wait(barrier, len(targets))

    def remote(src, dst, sems, where, target):
        return pltpu.make_async_remote_copy(
            src_ref=src,
            dst_ref=dst,
            send_sem=sems.at[(0,) + where],
            recv_sem=sems.at[(1,) + where],
            device_id=target,
            device_id_type=MESH,
        )

    def columns(start):
        return pl.ds(pl.multiple_of(start, rows), rows)

    copies = []

    def begin(copy):
        copy.start()
        copies.append(copy)
        return copy

    y1 = []
    for step in range(1, chips):
        there = lax.rem(chip + step, chips)
        y1.append(begin(remote(
            x_hbm.at[:, pl.ds(pl.multiple_of(there * 2 * rows, 2 * rows), 2 * rows)],
            xin.at[step - 1], ysem, (step - 1,), peer(step))))
    halves, returns = {}, {}
    if chunks:
        span = rows // chunks
        orders = [
            [1, 0] + list(range(2, levels)) if levels > 1 and q % 2 == 1 else list(range(levels))
            for q in range(chunks)
        ]
        starts = []
        for q in range(chunks):
            begins = [q * span]
            for level, bit in enumerate(orders[q]):
                begins.append(begins[level] + sides[bit] * (span >> (level + 1)))
            starts.append(begins)

    def segment(q, level):
        return pl.ds(pl.multiple_of(starts[q][level], span >> level), span >> level)

    def landing(level):
        return pl.ds(span - (span >> level), span >> (level + 1))

    def send_half(q, level):
        bit, size = orders[q][level], span >> (level + 1)
        away = starts[q][level] + (1 - sides[bit]) * size
        source = part if level else w_hbm
        halves[q, level] = begin(remote(
            source.at[pl.ds(pl.multiple_of(away, size), size)],
            landed.at[q, landing(level)], hsem, (q, level), mates[bit]))

    def send_back(q, level):
        place = segment(q, level + 1)
        returns[q, level] = begin(remote(
            gathered.at[place], gathered.at[place], hsem, (q, levels + level),
            mates[orders[q][level]]))

    for q in range(chunks):
        send_half(q, 0)
    wcopy = begin(remote(w_hbm, wp, csem, (0,), partner))
    xcopy = [begin(remote(
        x_hbm.at[:, columns((chip * 2 + 1 - core) * rows)], xp.at[0], csem, (1,), partner))]

    def step_of(q, stage):
        if stage < levels:
            halves[q, stage].wait_recv()
            place = segment(q, stage + 1)
            held = (part if stage else w)[place, :].astype(jnp.float32)
            total = held + landed[q, landing(stage), :].astype(jnp.float32)
            if stage + 1 < levels:
                part[place, :] = total.astype(jnp.bfloat16)
                send_half(q, stage + 1)
            else:
                gathered[place, :] = (total / islands).astype(jnp.bfloat16)
                send_back(q, levels - 1)
        else:
            level = 2 * levels - 1 - stage
            returns[q, level].wait_recv()
            if level:
                send_back(q, level - 1)

    def product(left, right):
        return jnp.dot(left, right, preferred_element_type=jnp.float32)

    stages = []
    for q in range(chunks):
        for stage in range(2 * levels):
            late = (q // 2) * 6.0 / chunks
            stages.append((stage + late, q, stage))
    stages.sort()

    def advance(until):
        while stages and stages[0][0] <= until:
            step_of(*stages.pop(0)[1:])

    for load in loads:
        load.wait()
    advance(0.5)
    wcopy.wait_recv()
    own[...] = product(x[:, columns(shard * rows)], w[...]) + product(
        x[:, columns((chip * 2 + 1 - core) * rows)], wp[...])
    advance(3.3)

    y3 = []
    for step in range(1, chips):
        y1[step - 1].wait_recv()
        xcopy.append(begin(remote(
            xin.at[step - 1, :, columns((1 - core) * rows)], xp.at[step], csem, (step + 1,), partner)))
        psend[step - 1] = (product(xin[step - 1, :, columns(core * rows)], w[...]) + product(
            xin[step - 1, :, columns((1 - core) * rows)], wp[...])).astype(jnp.bfloat16)
        y3.append(begin(remote(
            psend.at[step - 1], precv.at[step - 1], psem, (step - 1,), back(step))))
    advance(5.1)

    keys = own[...]
    for step in range(1, chips):
        y3[step - 1].wait_recv()
        keys += precv[step - 1].astype(jnp.float32)
    keys = keys * scale
    for head in range(width // HEAD_DIM):
        lanes = slice(head * HEAD_DIM, (head + 1) * HEAD_DIM)
        kg[:, lanes] = head_backward(keys[:, lanes], cot[:, lanes].astype(jnp.float32), scale)
    y4 = [
        begin(remote(kg, kgin.at[step - 1], ksem, (step - 1,), peer(step)))
        for step in range(1, chips)
    ]
    forwards = [begin(remote(kg, kgp.at[0], fsem, (0,), partner))]

    tile = min(256, rows)

    def add_block(read, upstream, first=False):
        @pl.loop(0, rows // tile)
        def _(t):
            start = pl.multiple_of(t * tile, tile)
            term = lax.dot_general(
                read(start), upstream[...], (((0,), (0,)), ((), ())),
                preferred_element_type=jnp.float32,
            ).astype(jnp.bfloat16).astype(jnp.float32)
            place = pl.ds(start, tile)
            grad[place, :] = term if first else grad[place, :] + term

    def lane(base):
        def at(start):
            return pl.ds(pl.multiple_of(base + start, tile), tile)
        return at

    mine = lane(shard * rows)
    add_block(lambda start: x[:, mine(start)], kg, first=True)
    forwards[0].wait_recv()
    xcopy[0].wait_recv()
    add_block(lambda start: xp[0, :, pl.ds(start, tile)], kgp.at[0])
    advance(6.4)
    inner = lane(core * rows)
    for step in range(1, chips):
        y4[step - 1].wait_recv()
        forwards.append(begin(remote(
            kgin.at[step - 1], kgp.at[step], fsem, (step,), partner)))
        add_block(lambda start: xin[step - 1, :, inner(start)], kgin.at[step - 1])
    advance(6.9)
    for step in range(1, chips):
        xcopy[step].wait_recv()
        forwards[step].wait_recv()
        add_block(lambda start: xp[step, :, pl.ds(start, tile)], kgp.at[step])
    advance(1000)
    if chunks:
        mean[...] = gathered[...]
    for copy in copies:
        copy.wait_send()


def token_splits(count):
    if count % 64 == 0:
        return (count // 2, count // 4, count // 4)
    return (count,)


def pieces_of(rows, islands, shards):
    if shards != 4 or islands != 2 * shards:
        return 0
    for pieces in (8, 4, 2, 1):
        if rows % (2 * pieces * 16) == 0:
            return pieces
    return 0


def window(islands, pieces, splits, scale, *refs):
    w_hbm, m_hbm, s_hbm, gw_hbm, om_hbm, x_hbm, cot_hbm = refs[:7]
    nl, nf, ns, ng, nm = refs[7:12]
    (wc, xc, xin, cot, own, psend, precv, kg, kgin, grad, half_inner, m, s, gw, om, mean,
     rsin, pin, qin, pout, res,
     lsem, lxsem, lcsem, rssem, keepsem, xosem, wsem, cosem, yxsem, xfsem, ypsem, yksem, fksem,
     fisem, zpsem, zqsem, zrsem, agsem, dlsem) = refs[12:]
    rows, width = mean.shape
    half = rows // 2
    size = half // pieces
    count = 2 * pieces
    f32, bf16 = jnp.float32, jnp.bfloat16

    island = lax.axis_index("island")
    shard = lax.axis_index("fsdp")
    core = lax.rem(shard, 2)
    chip = shard // 2
    side = lax.rem(island, 2)
    level = island // 2
    inside = level * (3 - level) // 2

    partner = (island, chip * 2 + 1 - core)

    def across(c):
        return (island, (1 - chip) * 2 + c)

    def beside(c):
        return (island + 1 - 2 * side, chip * 2 + c)

    pair = ((level + 1 - 2 * lax.rem(level, 2)) * 2 + side, shard)
    middle = ((3 - level) * 2 + side, shard)

    offsets = [sum(splits[:i]) for i in range(len(splits))]

    def block(c, i):
        return pl.ds(2 * offsets[i] + c * splits[i], splits[i])

    def both(i):
        return pl.ds(2 * offsets[i], 2 * splits[i])

    def source(i):
        return pl.ds(offsets[i], splits[i])

    def lanes(start, extent):
        return pl.ds(pl.multiple_of(start, rows), extent)

    my_lanes = lanes(chip * 2 * rows, 2 * rows)
    core_rows = core * rows

    barrier = pltpu.get_barrier_semaphore()

    def greet(target):
        pl.semaphore_signal(barrier, inc=1, device_id=target, device_id_type=MESH)

    greet(partner)
    greet(beside(1))
    greet(across(0))

    @pl.when(core == 0)
    def _():
        greet(across(1))

    @pl.when(core == 1)
    def _():
        greet(beside(0))
        greet(pair)

    @pl.when((core == 1) & (inside == 1))
    def _():
        greet(middle)

    tokens = []
    wload = pltpu.make_async_copy(
        w_hbm, wc.at[pl.ds(pl.multiple_of(core_rows, rows), rows)], lsem.at[0])
    wload.start()
    for i in range(len(splits)):
        place = pl.ds(pl.multiple_of(2 * offsets[i] + core * splits[i], splits[i]), splits[i])
        tokens.append(pltpu.make_async_copy(
            x_hbm.at[source(i), my_lanes], xc.at[place], lxsem.at[i]))
        tokens.append(pltpu.make_async_copy(cot_hbm.at[source(i)], cot.at[place], lcsem.at[i]))
    for load in tokens:
        load.start()

    pl.semaphore_wait(barrier, 4 + core * (1 + inside))

    def remote(src, dst, sems, index, target):
        return pltpu.make_async_remote_copy(
            src_ref=src, dst_ref=dst, send_sem=sems.at[0, index], recv_sem=sems.at[1, index],
            device_id=target, device_id_type=MESH)

    def token_send(c, i):
        return remote(
            x_hbm.at[source(i), lanes((1 - chip) * 2 * rows, 2 * rows)],
            xin.at[block(c, i)], yxsem, 2 * i + c, across(0))

    def kept(j):
        return pl.multiple_of(side * half + j * size, size)

    def given(j):
        return pl.multiple_of((1 - side) * half + j * size, size)

    def scatter_send(c, j):
        return remote(
            w_hbm.at[pl.ds(given(j), size)], rsin.at[2 * j + c], rssem, 2 * j + c, beside(1))

    keep_send = remote(
        w_hbm.at[pl.ds(pl.multiple_of(side * half, half), half)],
        wc.at[pl.ds(pl.multiple_of(side * half, half), half)], keepsem, 0, partner)
    weight_send = remote(w_hbm, wc.at[pl.ds(rows, rows)], wsem, 0, partner)

    def own_tokens_up(i):
        return remote(
            x_hbm.at[source(i), lanes((chip * 2 + 1) * rows, rows)],
            xc.at[block(0, i), pl.ds(rows, rows)], xosem, i, partner)

    def own_tokens_down(i):
        return remote(x_hbm.at[source(i), my_lanes], xc.at[block(1, i)], xosem, i, partner)

    def cotangent_down(i):
        return remote(cot_hbm.at[source(i)], cot.at[block(1, i)], cosem, i, partner)

    def tokens_forward(i):
        place = xin.at[both(i), pl.ds(rows, rows)]
        return remote(place, place, xfsem, i, partner)

    def partial_send(i):
        return remote(psend.at[both(i)], precv.at[both(i)], ypsem, i, across(0))

    def upstream_across(i):
        return remote(kg.at[both(i)], kgin.at[both(i)], yksem, i, across(0))

    def upstream_down(i):
        return remote(kg.at[both(i)], kg.at[both(i)], fksem, i, partner)

    def upstream_forward(i):
        return remote(kgin.at[both(i)], kgin.at[both(i)], fisem, i, partner)

    def outer_send(k):
        return remote(pout.at[k], pin.at[k], zpsem, k, pair)

    def middle_send(k):
        return remote(pout.at[k], qin.at[k], zqsem, k, middle)

    def result_send(k):
        return remote(res.at[k], res.at[k], zrsem, k, pair)

    def gather_send(k):
        return remote(
            res.at[k], mean.at[pl.ds(kept(k // 2), size)], agsem, k, beside(k % 2))

    def deliver_send(j):
        return remote(res.at[2 * j], mean.at[pl.ds(kept(j), size)], dlsem, j, partner)

    def gather_recv(k):
        return remote(
            res.at[k], mean.at[pl.ds(given(k // 2), size)], agsem, k, beside(k % 2))

    state_loads = [
        pltpu.make_async_copy(place, dst, lsem.at[1 + index])
        for index, (place, dst) in enumerate(((m_hbm, m), (s_hbm, s), (gw_hbm, gw), (om_hbm, om)))
    ]

    def own_gradient(base):
        tile = min(256, rows)

        @pl.loop(0, rows // tile)
        def _(t):
            start = pl.multiple_of(t * tile, tile)
            grad[pl.ds(start, tile), :] = lax.dot_general(
                xc[:, pl.ds(pl.multiple_of(base + start, tile), tile)], kg[...],
                (((0,), (0,)), ((), ())), preferred_element_type=f32)

    def gradient_tile(base, start, tile):
        grad[pl.ds(start, tile), :] += lax.dot_general(
            xin[:, pl.ds(pl.multiple_of(base + start, tile), tile)], kgin[...],
            (((0,), (0,)), ((), ())), preferred_element_type=f32)
        step = min(32, tile)

        @pl.loop(0, tile // step)
        def _(u):
            place = pl.ds(pl.multiple_of(start + u * step, step), step)
            gradient = grad[place, :]
            first_new = beta_one * m[place, :].astype(f32) + (1.0 - beta_one) * gradient
            second_new = (
                beta_two * s[place, :].astype(f32) + (1.0 - beta_two) * gradient * gradient)
            nf[place, :] = first_new.astype(bf16)
            ns[place, :] = second_new.astype(bf16)
            current = wc[pl.ds(pl.multiple_of(base + start + u * step, step), step), :].astype(f32)
            inner = current - inner_rate * (
                first_new / (jnp.sqrt(second_new) + adam_epsilon) + weight_decay * current)
            half_inner[place, :] = merge_weight * inner

    def inner_update(base):
        tile = min(256, rows)

        @pl.loop(0, rows // tile)
        def _(t):
            gradient_tile(base, pl.multiple_of(t * tile, tile), tile)

    def outer_update(start, extent):
        step = min(32, extent)

        @pl.loop(0, extent // step)
        def _(u):
            place = pl.ds(pl.multiple_of(start + u * step, step), step)
            weights = gw[place, :]
            outer_grad = weights - mean[place, :].astype(f32)
            momentum = outer_beta * om[place, :] + outer_grad
            updated = weights - outer_rate * (outer_grad + outer_beta * momentum)
            nm[place, :] = momentum
            ng[place, :] = updated
            nl[place, :] = (half_inner[place, :] + (1.0 - merge_weight) * updated).astype(bf16)

    def matmul(out, place, left, convert):
        part = min(256, width)

        @pl.loop(0, width // part)
        def _(n):
            columns = pl.ds(pl.multiple_of(n * part, part), part)
            value = jnp.dot(left[...], wc[:, columns], preferred_element_type=f32)
            out[place, columns] = value.astype(bf16) if convert else value

    steps = range(len(splits))

    @pl.when(core == 0)
    def _():
        sends = []

        def begin(copy):
            copy.start()
            sends.append(copy)

        begin(token_send(0, 0))
        begin(scatter_send(0, 0))
        begin(keep_send)
        for j in range(1, pieces):
            begin(scatter_send(0, j))
        for i in steps[1:]:
            begin(token_send(0, i))
        for i in steps:
            begin(own_tokens_up(i))
        for load in state_loads:
            load.start()
        wload.wait()
        for load in tokens:
            load.wait()
        weight_send.wait_recv()
        for i in steps:
            own_tokens_down(i).wait_recv()
        matmul(own, slice(None), xc, False)
        for i in steps:
            token_send(0, i).wait_recv()
            token_send(1, i).wait_recv()
            begin(tokens_forward(i))
            matmul(psend, both(i), xin.at[both(i)], True)
            begin(partial_send(i))
        for i in steps:
            cotangent_down(i).wait_recv()
        for i in steps:
            partial_send(i).wait_recv()
            for head in range(width // HEAD_DIM):
                columns = slice(head * HEAD_DIM, (head + 1) * HEAD_DIM)
                keys = (own[both(i), columns] + precv[both(i), columns].astype(f32)) * scale
                kg[both(i), columns] = head_backward(
                    keys, cot[both(i), columns].astype(f32), scale)
            begin(upstream_across(i))
            begin(upstream_down(i))
        own_gradient(0)
        for i in steps:
            upstream_across(i).wait_recv()
            begin(upstream_forward(i))
        for load in state_loads:
            load.wait()
        inner_update(0)
        for j in range(pieces):
            deliver_send(j).wait_recv()
            outer_update(kept(j), size)
            gather_recv(2 * j).wait_recv()
            outer_update(given(j), size)
        for copy in sends:
            copy.wait_send()

    @pl.when(core == 1)
    def _():
        sends = []

        def begin(copy):
            copy.start()
            sends.append(copy)

        def held(k):
            place = pl.ds(pl.multiple_of((k % 2) * rows + kept(k // 2), size), size)
            return wc[place, :].astype(f32) + rsin[k].astype(f32)

        def hand_out(k):
            gather_send(k).start()
            if k % 2:
                mean[pl.ds(kept(k // 2), size), :] = res[k]
            else:
                deliver_send(k // 2).start()

        begin(token_send(1, 0))
        for j in range(pieces):
            begin(scatter_send(1, j))
        for i in steps[1:]:
            begin(token_send(1, i))
        begin(weight_send)
        for i in steps:
            begin(own_tokens_down(i))
            begin(cotangent_down(i))
        for load in state_loads:
            load.start()
        wload.wait()
        for load in tokens:
            load.wait()
        keep_send.wait_recv()

        @pl.when(inside == 0)
        def _():
            for k in range(count):
                scatter_send(k % 2, k // 2).wait_recv()
                pout[k] = held(k).astype(bf16)
                outer_send(k).start()
            for k in range(count):
                result_send(k).wait_recv()
                hand_out(k)
            for k in range(count):
                outer_send(k).wait_send()

        @pl.when(inside == 1)
        def _():
            lag = min(4, count)
            for k in range(count + lag):
                if k < count:
                    scatter_send(k % 2, k // 2).wait_recv()
                    outer_send(k).wait_recv()
                    pout[k] = (held(k) + pin[k].astype(f32)).astype(bf16)
                    middle_send(k).start()
                if k >= lag:
                    q = k - lag
                    middle_send(q).wait_recv()
                    total = pout[q].astype(f32) + qin[q].astype(f32)
                    res[q] = (total / islands).astype(bf16)
                    result_send(q).start()
                    hand_out(q)
            for k in range(count):
                middle_send(k).wait_send()
                result_send(k).wait_send()

        for i in steps:
            own_tokens_up(i).wait_recv()
            upstream_down(i).wait_recv()
        own_gradient(rows)
        for i in steps:
            tokens_forward(i).wait_recv()
            upstream_forward(i).wait_recv()
        for load in state_loads:
            load.wait()
        inner_update(rows)
        for j in range(pieces):
            outer_update(kept(j), size)
        for j in range(pieces):
            gather_recv(2 * j + 1).wait_recv()
            outer_update(given(j), size)
        for k in range(count):
            gather_send(k).wait_send()
        for j in range(pieces):
            deliver_send(j).wait_send()
        for copy in sends:
            copy.wait_send()


def write_back(*refs):
    arrays = len(refs) // 2
    sems = refs[-1]
    copies = []
    for index in range(arrays):
        part = refs[index].shape[0] // 2
        for piece in range(2):
            place = pl.ds(piece * part, part)
            copies.append(pltpu.make_async_copy(
                refs[index].at[place], refs[arrays + index].at[place], sems.at[index, piece]))
    for copy in copies:
        copy.start()
    for copy in copies:
        copy.wait()


def fused(pieces, local_weights, adam_first, adam_second, global_weights, outer_momentum, inputs,
          key_cotangent):
    arrays = (local_weights[0], adam_first[0], adam_second[0], global_weights, outer_momentum,
              inputs[0], key_cotangent[0])
    rows, width = arrays[0].shape
    count, depth = arrays[5].shape
    islands = lax.axis_size("island")
    splits = token_splits(count)
    size = rows // (2 * pieces)
    bf16, f32 = jnp.bfloat16, jnp.float32
    dma, vmem = pltpu.SemaphoreType.DMA, pltpu.VMEM
    out_shape = [jax.ShapeDtypeStruct((rows, width), bf16)] * 3 + [
        jax.ShapeDtypeStruct((rows, width), f32)] * 2
    steps = len(splits)
    scratch = [
        vmem((2 * rows, width), bf16),
        vmem((2 * count, 2 * rows), bf16),
        vmem((2 * count, 2 * rows), bf16),
        vmem((2 * count, width), bf16),
        vmem((2 * count, width), f32),
        vmem((2 * count, width), bf16),
        vmem((2 * count, width), bf16),
        vmem((2 * count, width), bf16),
        vmem((2 * count, width), bf16),
        vmem((rows, width), f32),
        vmem((rows, width), f32),
        vmem((rows, width), bf16),
        vmem((rows, width), bf16),
        vmem((rows, width), f32),
        vmem((rows, width), f32),
        vmem((rows, width), bf16),
    ] + [vmem((2 * pieces, size, width), bf16)] * 5 + [
        dma((5,)),
        dma((steps,)),
        dma((steps,)),
        dma((2, 2 * pieces)),
        dma((2, 1)),
        dma((2, steps)),
        dma((2, 1)),
        dma((2, steps)),
        dma((2, 2 * steps)),
        dma((2, steps)),
        dma((2, steps)),
        dma((2, steps)),
        dma((2, steps)),
        dma((2, steps)),
        dma((2, 2 * pieces)),
        dma((2, 2 * pieces)),
        dma((2, 2 * pieces)),
        dma((2, 2 * pieces)),
        dma((2, pieces)),
    ]
    in_vmem = pl.BlockSpec(memory_space=pltpu.VMEM)
    in_hbm = pl.BlockSpec(memory_space=pltpu.HBM)
    results = pl.pallas_call(
        functools.partial(window, islands, pieces, splits, float(depth) ** (-0.5)),
        out_shape=out_shape,
        in_specs=[in_hbm] * len(arrays),
        out_specs=[in_vmem] * len(out_shape),
        scratch_shapes=scratch,
        compiler_params=pltpu.CompilerParams(
            collective_id=0, has_side_effects=True, vmem_limit_bytes=40 * 1024 * 1024
        ),
    )(*(pltpu.with_memory_space_constraint(a, pltpu.HBM) for a in arrays))
    written = pl.pallas_call(
        write_back,
        out_shape=out_shape,
        in_specs=[in_vmem] * len(out_shape),
        out_specs=[in_hbm] * len(out_shape),
        scratch_shapes=[dma((len(out_shape), 2))],
        compiler_params=pltpu.CompilerParams(vmem_limit_bytes=4 * 1024 * 1024),
    )(*results)
    return tuple(a[None] for a in written[:3]) + tuple(written[3:])


def local(
    local_weights, adam_first, adam_second, global_weights, outer_momentum, inputs, key_cotangent
):
    weights = local_weights[0]
    tokens = inputs[0]
    rows, width = weights.shape
    count, depth = tokens.shape
    scale = float(depth) ** (-0.5)
    islands, shards = lax.axis_size("island"), lax.axis_size("fsdp")
    chips = shards // 2
    others = max(chips - 1, 1)
    pieces = pieces_of(rows, islands, shards)
    if pieces and width % HEAD_DIM == 0:
        return fused(pieces, local_weights, adam_first, adam_second, global_weights,
                     outer_momentum, inputs, key_cotangent)
    chunks = chunk_count(rows, islands)
    bf16, f32 = jnp.bfloat16, jnp.float32
    dma = pltpu.SemaphoreType.DMA
    out_shape = [jax.ShapeDtypeStruct((rows, width), f32)]
    scratch = [
        pltpu.VMEM((rows, width), bf16),
        pltpu.VMEM((count, depth), bf16),
        pltpu.VMEM((count, width), bf16),
        dma((3,)),
        pltpu.VMEM((rows, width), bf16),
        pltpu.VMEM((others, count, 2 * rows), bf16),
        pltpu.VMEM((chips, count, rows), bf16),
        pltpu.VMEM((others, count, width), bf16),
        pltpu.VMEM((others, count, width), bf16),
        pltpu.VMEM((others, count, width), bf16),
        pltpu.VMEM((chips, count, width), bf16),
        pltpu.VMEM((count, width), bf16),
        pltpu.VMEM((count, width), f32),
        dma((2, others)),
        dma((2, others)),
        dma((2, others)),
        dma((2, chips + 1)),
        dma((2, chips)),
    ]
    if chunks:
        levels = islands.bit_length() - 1
        out_shape.append(jax.ShapeDtypeStruct((rows, width), bf16))
        scratch += [
            pltpu.VMEM((chunks, rows // chunks, width), bf16),
            pltpu.VMEM((rows, width), bf16),
            pltpu.VMEM((rows, width), bf16),
            dma((2, chunks, 2 * levels)),
        ]
    vmem = pl.BlockSpec(memory_space=pltpu.VMEM)
    results = pl.pallas_call(
        functools.partial(exchange, islands, shards, chunks, scale),
        out_shape=out_shape,
        in_specs=[pl.BlockSpec(memory_space=pltpu.HBM)] * 3,
        out_specs=[vmem] * len(out_shape),
        scratch_shapes=scratch,
        compiler_params=pltpu.CompilerParams(
            collective_id=0, has_side_effects=True, vmem_limit_bytes=40 * 1024 * 1024
        ),
    )(*(pltpu.with_memory_space_constraint(a, pltpu.HBM) for a in (weights, tokens, key_cotangent[0])))
    gradient = results[0]
    if chunks:
        mean_local = results[1].astype(jnp.float32)
    else:
        mean_local = lax.psum(weights.astype(jnp.float32), "island") / islands
    outer_grad = global_weights - mean_local
    new_momentum = outer_beta * outer_momentum + outer_grad
    new_global = global_weights - outer_rate * (outer_grad + outer_beta * new_momentum)
    first_new = beta_one * adam_first[0].astype(jnp.float32) + (1.0 - beta_one) * gradient
    second_new = (
        beta_two * adam_second[0].astype(jnp.float32) + (1.0 - beta_two) * gradient * gradient
    )
    current = weights.astype(jnp.float32)
    inner = current - inner_rate * (
        first_new / (jnp.sqrt(second_new) + adam_epsilon) + weight_decay * current
    )
    merged = merge_weight * inner + (1.0 - merge_weight) * new_global
    return (
        merged.astype(jnp.bfloat16)[None],
        first_new.astype(jnp.bfloat16)[None],
        second_new.astype(jnp.bfloat16)[None],
        new_global,
        new_momentum,
    )


def solution(mesh):
    placed = (
        P("island", "fsdp", None),
        P("island", "fsdp", None),
        P("island", "fsdp", None),
        P("fsdp", None),
        P("fsdp", None),
        P("island", "fsdp", None),
        P("island", "fsdp", None),
    )
    return jax.shard_map(
        local,
        mesh=mesh,
        in_specs=placed,
        out_specs=(
            P("island", "fsdp", None),
            P("island", "fsdp", None),
            P("island", "fsdp", None),
            P("fsdp", None),
            P("fsdp", None),
        ),
        check_vma=False,
    )
```

```python
import functools

import jax
import jax.numpy as jnp
from jax import lax
from jax.experimental import pallas as pl
from jax.experimental.pallas import tpu as pltpu
from jax.sharding import PartitionSpec as P

HEAD_DIM = 128
MESH = pl.DeviceIdType.MESH

beta_one = 0.9
beta_two = 0.95
inner_rate = 0.02
weight_decay = 0.1
adam_epsilon = 1e-08
norm_epsilon = 1e-06
outer_rate = 0.7
outer_beta = 0.9
merge_weight = 0.5


def chunk_count(rows, islands):
    for chunks in (8, 4, 2, 1):
        if islands & (islands - 1) == 0 and rows % (islands * chunks * 16) == 0:
            return chunks
    return 0


def head_backward(keys, upstream, scale):
    squares = jnp.mean(keys * keys, axis=-1, keepdims=True)
    inverse = lax.rsqrt(squares + norm_epsilon)
    normed = keys * inverse
    projected = jnp.mean(upstream * normed, axis=-1, keepdims=True)
    return (inverse * (upstream - normed * projected) * scale).astype(jnp.bfloat16)


def exchange(islands, shards, chunks, scale, *refs):
    w_hbm, x_hbm, cot_hbm = refs[:3]
    if chunks:
        (grad, mean, w, x, cot, lsem, wp, xin, xp, psend, precv, kgin, kgp, kg, own,
         ysem, psem, ksem, csem, fsem, landed, part, gathered, hsem) = refs[3:]
    else:
        (grad, w, x, cot, lsem, wp, xin, xp, psend, precv, kgin, kgp, kg, own,
         ysem, psem, ksem, csem, fsem) = refs[3:]
    rows, width = w.shape
    chips = shards // 2
    island = lax.axis_index("island")
    shard = lax.axis_index("fsdp")
    core = lax.rem(shard, 2)
    chip = shard // 2
    partner = (island, chip * 2 + 1 - core)

    def peer(step):
        return (island, lax.rem(chip + step, chips) * 2 + core)

    def back(step):
        return (island, lax.rem(chip + chips - step, chips) * 2 + core)

    targets = [partner] + [peer(step) for step in range(1, chips)]
    if chunks:
        levels = islands.bit_length() - 1
        sides = [lax.rem(island // 2**bit, 2) for bit in range(levels)]
        mates = [(island + (1 - 2 * sides[bit]) * 2**bit, shard) for bit in range(levels)]
        targets += mates

    loads = [
        pltpu.make_async_copy(source, place, lsem.at[index])
        for index, (source, place) in enumerate(((w_hbm, w), (x_hbm, x), (cot_hbm, cot)))
    ]
    for load in loads:
        load.start()

    barrier = pltpu.get_barrier_semaphore()
    for target in targets:
        pl.semaphore_signal(barrier, inc=1, device_id=target, device_id_type=MESH)
    pl.semaphore_wait(barrier, len(targets))

    def remote(src, dst, sems, where, target):
        return pltpu.make_async_remote_copy(
            src_ref=src,
            dst_ref=dst,
            send_sem=sems.at[(0,) + where],
            recv_sem=sems.at[(1,) + where],
            device_id=target,
            device_id_type=MESH,
        )

    def columns(start):
        return pl.ds(pl.multiple_of(start, rows), rows)

    copies = []

    def begin(copy):
        copy.start()
        copies.append(copy)
        return copy

    y1 = []
    for step in range(1, chips):
        there = lax.rem(chip + step, chips)
        y1.append(begin(remote(
            x_hbm.at[:, pl.ds(pl.multiple_of(there * 2 * rows, 2 * rows), 2 * rows)],
            xin.at[step - 1], ysem, (step - 1,), peer(step))))
    halves, returns = {}, {}
    if chunks:
        span = rows // chunks
        orders = [
            [1, 0] + list(range(2, levels)) if levels > 1 and q % 2 == 1 else list(range(levels))
            for q in range(chunks)
        ]
        starts = []
        for q in range(chunks):
            begins = [q * span]
            for level, bit in enumerate(orders[q]):
                begins.append(begins[level] + sides[bit] * (span >> (level + 1)))
            starts.append(begins)

    def segment(q, level):
        return pl.ds(pl.multiple_of(starts[q][level], span >> level), span >> level)

    def landing(level):
        return pl.ds(span - (span >> level), span >> (level + 1))

    def send_half(q, level):
        bit, size = orders[q][level], span >> (level + 1)
        away = starts[q][level] + (1 - sides[bit]) * size
        source = part if level else w_hbm
        halves[q, level] = begin(remote(
            source.at[pl.ds(pl.multiple_of(away, size), size)],
            landed.at[q, landing(level)], hsem, (q, level), mates[bit]))

    def send_back(q, level):
        place = segment(q, level + 1)
        returns[q, level] = begin(remote(
            gathered.at[place], gathered.at[place], hsem, (q, levels + level),
            mates[orders[q][level]]))

    for q in range(chunks):
        send_half(q, 0)
    wcopy = begin(remote(w_hbm, wp, csem, (0,), partner))
    xcopy = [begin(remote(
        x_hbm.at[:, columns((chip * 2 + 1 - core) * rows)], xp.at[0], csem, (1,), partner))]

    def step_of(q, stage):
        if stage < levels:
            halves[q, stage].wait_recv()
            place = segment(q, stage + 1)
            held = (part if stage else w)[place, :].astype(jnp.float32)
            total = held + landed[q, landing(stage), :].astype(jnp.float32)
            if stage + 1 < levels:
                part[place, :] = total.astype(jnp.bfloat16)
                send_half(q, stage + 1)
            else:
                gathered[place, :] = (total / islands).astype(jnp.bfloat16)
                send_back(q, levels - 1)
        else:
            level = 2 * levels - 1 - stage
            returns[q, level].wait_recv()
            if level:
                send_back(q, level - 1)

    def product(left, right):
        return jnp.dot(left, right, preferred_element_type=jnp.float32)

    stages = []
    for q in range(chunks):
        for stage in range(2 * levels):
            late = (q // 2) * 6.0 / chunks
            stages.append((stage + late, q, stage))
    stages.sort()

    def advance(until):
        while stages and stages[0][0] <= until:
            step_of(*stages.pop(0)[1:])

    for load in loads:
        load.wait()
    advance(0.5)
    wcopy.wait_recv()
    own[...] = product(x[:, columns(shard * rows)], w[...]) + product(
        x[:, columns((chip * 2 + 1 - core) * rows)], wp[...])
    advance(3.3)

    y3 = []
    for step in range(1, chips):
        y1[step - 1].wait_recv()
        xcopy.append(begin(remote(
            xin.at[step - 1, :, columns((1 - core) * rows)], xp.at[step], csem, (step + 1,), partner)))
        psend[step - 1] = (product(xin[step - 1, :, columns(core * rows)], w[...]) + product(
            xin[step - 1, :, columns((1 - core) * rows)], wp[...])).astype(jnp.bfloat16)
        y3.append(begin(remote(
            psend.at[step - 1], precv.at[step - 1], psem, (step - 1,), back(step))))
    advance(5.1)

    keys = own[...]
    for step in range(1, chips):
        y3[step - 1].wait_recv()
        keys += precv[step - 1].astype(jnp.float32)
    keys = keys * scale
    for head in range(width // HEAD_DIM):
        lanes = slice(head * HEAD_DIM, (head + 1) * HEAD_DIM)
        kg[:, lanes] = head_backward(keys[:, lanes], cot[:, lanes].astype(jnp.float32), scale)
    y4 = [
        begin(remote(kg, kgin.at[step - 1], ksem, (step - 1,), peer(step)))
        for step in range(1, chips)
    ]
    forwards = [begin(remote(kg, kgp.at[0], fsem, (0,), partner))]

    tile = min(256, rows)

    def add_block(read, upstream, first=False):
        @pl.loop(0, rows // tile)
        def _(t):
            start = pl.multiple_of(t * tile, tile)
            term = lax.dot_general(
                read(start), upstream[...], (((0,), (0,)), ((), ())),
                preferred_element_type=jnp.float32,
            ).astype(jnp.bfloat16).astype(jnp.float32)
            place = pl.ds(start, tile)
            grad[place, :] = term if first else grad[place, :] + term

    def lane(base):
        def at(start):
            return pl.ds(pl.multiple_of(base + start, tile), tile)
        return at

    mine = lane(shard * rows)
    add_block(lambda start: x[:, mine(start)], kg, first=True)
    forwards[0].wait_recv()
    xcopy[0].wait_recv()
    add_block(lambda start: xp[0, :, pl.ds(start, tile)], kgp.at[0])
    advance(6.4)
    inner = lane(core * rows)
    for step in range(1, chips):
        y4[step - 1].wait_recv()
        forwards.append(begin(remote(
            kgin.at[step - 1], kgp.at[step], fsem, (step,), partner)))
        add_block(lambda start: xin[step - 1, :, inner(start)], kgin.at[step - 1])
    advance(6.9)
    for step in range(1, chips):
        xcopy[step].wait_recv()
        forwards[step].wait_recv()
        add_block(lambda start: xp[step, :, pl.ds(start, tile)], kgp.at[step])
    advance(1000)
    if chunks:
        mean[...] = gathered[...]
    for copy in copies:
        copy.wait_send()


def token_splits(count):
    if count % 64 == 0:
        return (count // 2, count // 4, count // 4)
    return (count,)


def pieces_of(rows, islands, shards):
    if shards != 4 or islands != 2 * shards:
        return ()
    for grades in ((1,) * 8, (1,) * 4, (1,)):
        unit, rest = divmod(rows // 2, sum(grades))
        if rest == 0 and unit % 16 == 0:
            return tuple(unit * grade for grade in grades)
    return ()


def window(islands, pieces, splits, scale, *refs):
    w_hbm, m_hbm, s_hbm, gw_hbm, om_hbm, x_hbm, cot_hbm = refs[:7]
    nl, nf, ns, ng, nm = refs[7:12]
    (wc, xc, xin, cot, own, psend, precv, kg, kgin, grad, half_inner, m, s, gw, om, mean,
     rsin, pin, qin, pout, res,
     load_sem, sent, first, rail, cross, gathered, kept_sem, passed) = refs[12:]
    rows, width = mean.shape
    half = rows // 2
    groups = range(len(pieces))
    token_count = x_hbm.shape[0]
    count = 2 * len(pieces)
    begins = [sum(pieces[:j]) for j in groups]
    f32, bf16 = jnp.float32, jnp.bfloat16

    island = lax.axis_index("island")
    shard = lax.axis_index("fsdp")
    core = lax.rem(shard, 2)
    chip = shard // 2
    side = lax.rem(island, 2)
    level = island // 2
    inside = level * (3 - level) // 2

    partner = (island, chip * 2 + 1 - core)

    def across(c):
        return (island, (1 - chip) * 2 + c)

    def beside(c):
        return (island + 1 - 2 * side, chip * 2 + c)

    pair = ((level + 1 - 2 * lax.rem(level, 2)) * 2 + side, shard)
    middle = ((3 - level) * 2 + side, shard)

    offsets = [sum(splits[:i]) for i in range(len(splits))]

    def block(c, i):
        return pl.ds(2 * offsets[i] + c * splits[i], splits[i])

    def both(i):
        return pl.ds(2 * offsets[i], 2 * splits[i])

    def source(i):
        return pl.ds(offsets[i], splits[i])

    def lanes(start, extent):
        return pl.ds(pl.multiple_of(start, rows), extent)

    my_lanes = lanes(chip * 2 * rows, 2 * rows)
    core_rows = core * rows

    barrier = pltpu.get_barrier_semaphore()

    def greet(target):
        pl.semaphore_signal(barrier, inc=1, device_id=target, device_id_type=MESH)

    greet(partner)
    greet(beside(1))
    greet(across(0))

    @pl.when(core == 0)
    def _():
        greet(across(1))

    @pl.when(core == 1)
    def _():
        greet(beside(0))
        greet(pair)

    @pl.when((core == 1) & (inside == 1))
    def _():
        greet(middle)

    tokens = []
    wload = pltpu.make_async_copy(
        w_hbm, wc.at[pl.ds(pl.multiple_of(core_rows, rows), rows)], load_sem.at[0])
    wload.start()
    for i in range(len(splits)):
        place = pl.ds(pl.multiple_of(2 * offsets[i] + core * splits[i], splits[i]), splits[i])
        tokens.append(pltpu.make_async_copy(
            x_hbm.at[source(i), my_lanes], xc.at[place], load_sem.at[1]))
        tokens.append(pltpu.make_async_copy(
            cot_hbm.at[source(i)], cot.at[place], load_sem.at[2]))
    for load in tokens:
        load.start()

    pl.semaphore_wait(barrier, 4 + core * (1 + inside))

    def remote(src, dst, kind, into, target):
        return pltpu.make_async_remote_copy(
            src_ref=src, dst_ref=dst, send_sem=sent.at[kind], recv_sem=into,
            device_id=target, device_id_type=MESH)

    def all_tokens(ref):
        return ref.at[pl.ds(0, token_count)]

    def tokens_loaded():
        for ref, dst, index in ((x_hbm.at[:, my_lanes], xc, 1), (cot_hbm, cot, 2)):
            pltpu.make_async_copy(ref, all_tokens(dst), load_sem.at[index]).wait()

    def kept(j):
        return pl.multiple_of(side * half + begins[j], 16)

    def given(j):
        return pl.multiple_of((1 - side) * half + begins[j], 16)

    def kept_rows(j):
        return pl.ds(kept(j), pieces[j])

    def given_rows(j):
        return pl.ds(given(j), pieces[j])

    def slot(k):
        return pl.ds(2 * begins[k // 2] + (k % 2) * pieces[k // 2], pieces[k // 2])

    group = len(pieces)
    parts = len(splits)

    def scatter_send(c, j):
        k = 2 * j + c
        return remote(w_hbm.at[given_rows(j)], rsin.at[slot(k)], 0, first.at[k], beside(1))

    def scatter_total():
        return remote(
            w_hbm.at[pl.ds(0, half)], rsin.at[pl.ds(0, half)], 0, first.at[0], beside(1))

    def token_send(c, i):
        return remote(
            x_hbm.at[source(i), lanes((1 - chip) * 2 * rows, 2 * rows)],
            xin.at[block(c, i)], 1, first.at[group + 2 * i + c], across(0))

    def token_total():
        return remote(
            x_hbm.at[:, lanes((1 - chip) * 2 * rows, 2 * rows)],
            all_tokens(xin), 1, first.at[group], across(0))

    def keep_send(j):
        extent = pieces[j] if j < 2 else half - begins[j]
        place = pl.ds(kept(j), extent)
        return remote(w_hbm.at[place], wc.at[place], 2, kept_sem.at[j], partner)

    def keep_total():
        return remote(
            w_hbm.at[pl.ds(0, half)], wc.at[pl.ds(0, half)], 2, kept_sem.at[0], partner)

    weight_send = remote(w_hbm, wc.at[pl.ds(rows, rows)], 2, cross.at[0], partner)

    def own_tokens_up(i):
        return remote(
            x_hbm.at[source(i), lanes((chip * 2 + 1) * rows, rows)],
            xc.at[block(0, i), pl.ds(rows, rows)], 3, passed.at[0], partner)

    def own_tokens_up_total():
        return remote(
            x_hbm.at[:, lanes((chip * 2 + 1) * rows, rows)],
            xc.at[pl.ds(0, token_count), pl.ds(rows, rows)], 3, passed.at[0], partner)

    def own_tokens_down(i):
        return remote(
            x_hbm.at[source(i), my_lanes], xc.at[block(1, i)], 3, passed.at[0], partner)

    def own_tokens_down_total():
        return remote(x_hbm.at[:, my_lanes], all_tokens(xc), 3, passed.at[0], partner)

    def cotangent_down(i):
        return remote(cot_hbm.at[source(i)], cot.at[block(1, i)], 4, passed.at[1], partner)

    def cotangent_total():
        return remote(cot_hbm, all_tokens(cot), 4, passed.at[1], partner)

    def tokens_forward(place):
        part = xin.at[place, pl.ds(rows, rows)]
        return remote(part, part, 4, passed.at[1], partner)

    def partial_send(place, i):
        return remote(psend.at[place], precv.at[place], 5, rail.at[i], across(0))

    def upstream_across(place, i):
        return remote(kg.at[place], kgin.at[place], 6, rail.at[parts + i], across(0))

    def upstream_down(place):
        return remote(kg.at[place], kg.at[place], 7, passed.at[2], partner)

    def upstream_forward(place):
        return remote(kgin.at[place], kgin.at[place], 8, passed.at[3], partner)

    def gather_send(k):
        return remote(
            res.at[slot(k)], mean.at[kept_rows(k // 2)], 5, gathered.at[k // 2], beside(k % 2))

    def gather_total():
        return remote(res, mean, 5, gathered.at[0], beside(0))

    def gather_recv(j):
        return remote(
            res.at[slot(2 * j)], mean.at[given_rows(j)], 5, gathered.at[j], beside(0))

    def deliver_send(j):
        return remote(res.at[slot(2 * j)], mean.at[kept_rows(j)], 6, first.at[j], partner)

    def deliver_total():
        return remote(
            res.at[pl.ds(0, half)], mean.at[pl.ds(0, half)], 6, first.at[0], partner)

    def outer_send(k):
        return remote(pout.at[slot(k)], pin.at[slot(k)], 7, rail.at[k], pair)

    def middle_send(k):
        return remote(pout.at[slot(k)], qin.at[slot(k)], 7, cross.at[k], middle)

    def part_total():
        return remote(pout, pin, 7, rail.at[0], pair)

    def result_send(k):
        return remote(res.at[slot(k)], res.at[slot(k)], 8, rail.at[k], pair)

    def result_total():
        return remote(res, res, 8, rail.at[0], pair)

    state_loads = [
        pltpu.make_async_copy(place, dst, load_sem.at[3 + index])
        for index, (place, dst) in enumerate(((m_hbm, m), (s_hbm, s), (gw_hbm, gw), (om_hbm, om)))
    ]

    def own_gradient(base):
        tile = min(256, rows)

        @pl.loop(0, rows // tile)
        def _(t):
            start = pl.multiple_of(t * tile, tile)
            grad[pl.ds(start, tile), :] = lax.dot_general(
                xc[:, pl.ds(pl.multiple_of(base + start, tile), tile)], kg[...],
                (((0,), (0,)), ((), ())), preferred_element_type=f32)

    def gradient_tile(base, start, tile):
        grad[pl.ds(start, tile), :] += lax.dot_general(
            xin[:, pl.ds(pl.multiple_of(base + start, tile), tile)], kgin[...],
            (((0,), (0,)), ((), ())), preferred_element_type=f32)
        step = min(32, tile)

        @pl.loop(0, tile // step)
        def _(u):
            place = pl.ds(pl.multiple_of(start + u * step, step), step)
            gradient = grad[place, :]
            first_new = beta_one * m[place, :].astype(f32) + (1.0 - beta_one) * gradient
            second_new = (
                beta_two * s[place, :].astype(f32) + (1.0 - beta_two) * gradient * gradient)
            nf[place, :] = first_new.astype(bf16)
            ns[place, :] = second_new.astype(bf16)
            current = wc[pl.ds(pl.multiple_of(base + start + u * step, step), step), :].astype(f32)
            inner = current - inner_rate * (
                first_new / (jnp.sqrt(second_new) + adam_epsilon) + weight_decay * current)
            half_inner[place, :] = merge_weight * inner

    def inner_update(base):
        tile = min(256, rows)

        @pl.loop(0, rows // tile)
        def _(t):
            gradient_tile(base, pl.multiple_of(t * tile, tile), tile)

    def outer_update(start, extent):
        step = 32 if extent % 32 == 0 else 16

        @pl.loop(0, extent // step)
        def _(u):
            place = pl.ds(pl.multiple_of(start + u * step, step), step)
            weights = gw[place, :]
            outer_grad = weights - mean[place, :].astype(f32)
            momentum = outer_beta * om[place, :] + outer_grad
            updated = weights - outer_rate * (outer_grad + outer_beta * momentum)
            nm[place, :] = momentum
            ng[place, :] = updated

    def merge(start, extent):
        step = 32 if extent % 32 == 0 else 16

        @pl.loop(0, extent // step)
        def _(u):
            place = pl.ds(pl.multiple_of(start + u * step, step), step)
            nl[place, :] = (
                half_inner[place, :] + (1.0 - merge_weight) * ng[place, :]).astype(bf16)

    def matmul(out, place, left, convert):
        part = min(256, width)

        @pl.loop(0, width // part)
        def _(n):
            columns = pl.ds(pl.multiple_of(n * part, part), part)
            value = jnp.dot(left[...], wc[:, columns], preferred_element_type=f32)
            out[place, columns] = value.astype(bf16) if convert else value

    steps = range(len(splits))

    every = slice(None)

    @pl.when(core == 0)
    def _():
        for j in groups:
            scatter_send(0, j).start()
            if j < 3:
                keep_send(j).start()
            if j < 2 and j < parts:
                token_send(0, j).start()
        for i in steps:
            own_tokens_up(i).start()
        for load in state_loads:
            load.start()
        wload.wait()
        tokens_loaded()
        weight_send.wait_recv()
        own_tokens_down_total().wait_recv()
        matmul(own, every, xc, False)
        for i in steps:
            token_send(0, i).wait_recv()
            token_send(1, i).wait_recv()
            tokens_forward(both(i)).start()
            matmul(psend, both(i), xin.at[both(i)], True)
            partial_send(both(i), i).start()
            if i == 0:
                for later in steps[2:]:
                    token_send(0, later).start()
        cotangent_total().wait_recv()
        for i in steps:
            partial_send(both(i), i).wait_recv()
            for head in range(width // HEAD_DIM):
                columns = slice(head * HEAD_DIM, (head + 1) * HEAD_DIM)
                keys = (own[both(i), columns] + precv[both(i), columns].astype(f32)) * scale
                kg[both(i), columns] = head_backward(
                    keys, cot[both(i), columns].astype(f32), scale)
            upstream_across(both(i), i).start()
            upstream_down(both(i)).start()
        own_gradient(0)
        for i in steps:
            upstream_across(both(i), i).wait_recv()
            upstream_forward(both(i)).start()
        for load in state_loads:
            load.wait()
        inner_update(0)
        for j in groups:
            deliver_send(j).wait_recv()
            outer_update(kept(j), pieces[j])
            merge(kept(j), pieces[j])
            gather_recv(j).wait_recv()
            outer_update(given(j), pieces[j])
            merge(given(j), pieces[j])
        for total in (scatter_total(), token_total(), keep_total(), own_tokens_up_total(),
                      tokens_forward(every), partial_send(every, 0), upstream_across(every, 0),
                      upstream_down(every), upstream_forward(every)):
            total.wait_send()

    @pl.when(core == 1)
    def _():
        def held(k):
            j = k // 2
            place = pl.ds(pl.multiple_of((k % 2) * rows + kept(j), 16), pieces[j])
            return wc[place, :].astype(f32) + rsin[slot(k), :].astype(f32)

        def hand_out(k):
            gather_send(k).start()
            j = k // 2
            if k % 2:
                mean[kept_rows(j), :] = res[slot(k), :]
                outer_update(kept(j), pieces[j])
            else:
                deliver_send(j).start()

        for j in groups:
            scatter_send(1, j).start()
            if j < parts:
                token_send(1, j).start()
        weight_send.start()
        for i in steps:
            own_tokens_down(i).start()
            cotangent_down(i).start()
        for load in state_loads:
            load.start()
        wload.wait()
        state_loads[2].wait()
        state_loads[3].wait()

        def arrived(k):
            scatter_send(k % 2, k // 2).wait_recv()
            if k % 2 == 0 and k < 6:
                keep_send(k // 2).wait_recv()

        def outer_part(k):
            arrived(k)
            pout[slot(k), :] = held(k).astype(bf16)
            outer_send(k).start()

        def outer_result(k):
            result_send(k).wait_recv()
            hand_out(k)

        def middle_part(k):
            arrived(k)
            outer_send(k).wait_recv()
            pout[slot(k), :] = (held(k) + pin[slot(k), :].astype(f32)).astype(bf16)
            middle_send(k).start()

        def middle_result(k):
            middle_send(k).wait_recv()
            total = pout[slot(k), :].astype(f32) + qin[slot(k), :].astype(f32)
            res[slot(k), :] = (total / islands).astype(bf16)
            result_send(k).start()
            hand_out(k)

        tile = min(256, rows)
        tiles = rows // tile

        def gradient_start():
            tokens_loaded()
            own_tokens_up_total().wait_recv()
            upstream_down(every).wait_recv()
            own_gradient(rows)

        def gradient_ready():
            tokens_forward(every).wait_recv()
            upstream_forward(every).wait_recv()
            for load in state_loads[:2]:
                load.wait()

        def interleave(first, second, lag, own_at, tiles_at):
            work = {}
            work.setdefault(min(own_at, count - 1), []).append(gradient_start)
            for t in range(tiles):
                place = work.setdefault(min(tiles_at + t, count - 1), [])
                if t == 0:
                    place.append(gradient_ready)
                place.append(functools.partial(gradient_tile, rows, t * tile, tile))
            done = 0
            for k in range(count + lag):
                if k < count:
                    first(k)
                if k >= lag:
                    second(k - lag)
                    for item in work.get(k - lag, ()):
                        item()

        @pl.when(inside == 0)
        def _():
            interleave(outer_part, outer_result, count, count * 10 // 16, count * 14 // 16)

        @pl.when(inside == 1)
        def _():
            interleave(middle_part, middle_result, min(4, count), count, count)

        merge(pl.multiple_of(side * half, half), half)
        for j in groups:
            gather_recv(j).wait_recv()
            outer_update(given(j), pieces[j])
            merge(given(j), pieces[j])

        @pl.when(inside == 1)
        def _():
            result_total().wait_send()

        for total in (scatter_total(), token_total(), weight_send, own_tokens_down_total(),
                      cotangent_total(), gather_total(), deliver_total(), part_total()):
            total.wait_send()


def write_back(*refs):
    arrays = len(refs) // 2
    sems = refs[-1]
    copies = []
    for index in range(arrays):
        part = refs[index].shape[0] // 2
        for piece in range(2):
            place = pl.ds(piece * part, part)
            copies.append(pltpu.make_async_copy(
                refs[index].at[place], refs[arrays + index].at[place], sems.at[index, piece]))
    for copy in copies:
        copy.start()
    for copy in copies:
        copy.wait()


def fused(pieces, local_weights, adam_first, adam_second, global_weights, outer_momentum, inputs,
          key_cotangent):
    arrays = (local_weights[0], adam_first[0], adam_second[0], global_weights, outer_momentum,
              inputs[0], key_cotangent[0])
    rows, width = arrays[0].shape
    count, depth = arrays[5].shape
    islands = lax.axis_size("island")
    splits = token_splits(count)
    groups = len(pieces)
    bf16, f32 = jnp.bfloat16, jnp.float32
    dma, vmem = pltpu.SemaphoreType.DMA, pltpu.VMEM
    out_shape = [jax.ShapeDtypeStruct((rows, width), bf16)] * 3 + [
        jax.ShapeDtypeStruct((rows, width), f32)] * 2
    steps = len(splits)
    scratch = [
        vmem((2 * rows, width), bf16),
        vmem((2 * count, 2 * rows), bf16),
        vmem((2 * count, 2 * rows), bf16),
        vmem((2 * count, width), bf16),
        vmem((2 * count, width), f32),
        vmem((2 * count, width), bf16),
        vmem((2 * count, width), bf16),
        vmem((2 * count, width), bf16),
        vmem((2 * count, width), bf16),
        vmem((rows, width), f32),
        vmem((rows, width), f32),
        vmem((rows, width), bf16),
        vmem((rows, width), bf16),
        vmem((rows, width), f32),
        vmem((rows, width), f32),
        vmem((rows, width), bf16),
    ] + [vmem((rows, width), bf16)] * 5 + [
        dma((7,)),
        dma((9,)),
        dma((max(2 * groups, groups + 2 * steps),)),
        dma((max(2 * groups, 2 * steps),)),
        dma((2 * groups,)),
        dma((groups,)),
        dma((min(groups, 3),)),
        dma((4,)),
    ]
    in_vmem = pl.BlockSpec(memory_space=pltpu.VMEM)
    in_hbm = pl.BlockSpec(memory_space=pltpu.HBM)
    results = pl.pallas_call(
        functools.partial(window, islands, pieces, splits, float(depth) ** (-0.5)),
        out_shape=out_shape,
        in_specs=[in_hbm] * len(arrays),
        out_specs=[in_vmem] * len(out_shape),
        scratch_shapes=scratch,
        compiler_params=pltpu.CompilerParams(
            collective_id=0, has_side_effects=True, vmem_limit_bytes=40 * 1024 * 1024
        ),
    )(*(pltpu.with_memory_space_constraint(a, pltpu.HBM) for a in arrays))
    written = pl.pallas_call(
        write_back,
        out_shape=out_shape,
        in_specs=[in_vmem] * len(out_shape),
        out_specs=[in_hbm] * len(out_shape),
        scratch_shapes=[dma((len(out_shape), 2))],
        compiler_params=pltpu.CompilerParams(vmem_limit_bytes=4 * 1024 * 1024),
    )(*results)
    return tuple(a[None] for a in written[:3]) + tuple(written[3:])


def local(
    local_weights, adam_first, adam_second, global_weights, outer_momentum, inputs, key_cotangent
):
    weights = local_weights[0]
    tokens = inputs[0]
    rows, width = weights.shape
    count, depth = tokens.shape
    scale = float(depth) ** (-0.5)
    islands, shards = lax.axis_size("island"), lax.axis_size("fsdp")
    chips = shards // 2
    others = max(chips - 1, 1)
    pieces = pieces_of(rows, islands, shards)
    if pieces and width % HEAD_DIM == 0:
        return fused(pieces, local_weights, adam_first, adam_second, global_weights,
                     outer_momentum, inputs, key_cotangent)
    chunks = chunk_count(rows, islands)
    bf16, f32 = jnp.bfloat16, jnp.float32
    dma = pltpu.SemaphoreType.DMA
    out_shape = [jax.ShapeDtypeStruct((rows, width), f32)]
    scratch = [
        pltpu.VMEM((rows, width), bf16),
        pltpu.VMEM((count, depth), bf16),
        pltpu.VMEM((count, width), bf16),
        dma((3,)),
        pltpu.VMEM((rows, width), bf16),
        pltpu.VMEM((others, count, 2 * rows), bf16),
        pltpu.VMEM((chips, count, rows), bf16),
        pltpu.VMEM((others, count, width), bf16),
        pltpu.VMEM((others, count, width), bf16),
        pltpu.VMEM((others, count, width), bf16),
        pltpu.VMEM((chips, count, width), bf16),
        pltpu.VMEM((count, width), bf16),
        pltpu.VMEM((count, width), f32),
        dma((2, others)),
        dma((2, others)),
        dma((2, others)),
        dma((2, chips + 1)),
        dma((2, chips)),
    ]
    if chunks:
        levels = islands.bit_length() - 1
        out_shape.append(jax.ShapeDtypeStruct((rows, width), bf16))
        scratch += [
            pltpu.VMEM((chunks, rows // chunks, width), bf16),
            pltpu.VMEM((rows, width), bf16),
            pltpu.VMEM((rows, width), bf16),
            dma((2, chunks, 2 * levels)),
        ]
    vmem = pl.BlockSpec(memory_space=pltpu.VMEM)
    results = pl.pallas_call(
        functools.partial(exchange, islands, shards, chunks, scale),
        out_shape=out_shape,
        in_specs=[pl.BlockSpec(memory_space=pltpu.HBM)] * 3,
        out_specs=[vmem] * len(out_shape),
        scratch_shapes=scratch,
        compiler_params=pltpu.CompilerParams(
            collective_id=0, has_side_effects=True, vmem_limit_bytes=40 * 1024 * 1024
        ),
    )(*(pltpu.with_memory_space_constraint(a, pltpu.HBM) for a in (weights, tokens, key_cotangent[0])))
    gradient = results[0]
    if chunks:
        mean_local = results[1].astype(jnp.float32)
    else:
        mean_local = lax.psum(weights.astype(jnp.float32), "island") / islands
    outer_grad = global_weights - mean_local
    new_momentum = outer_beta * outer_momentum + outer_grad
    new_global = global_weights - outer_rate * (outer_grad + outer_beta * new_momentum)
    first_new = beta_one * adam_first[0].astype(jnp.float32) + (1.0 - beta_one) * gradient
    second_new = (
        beta_two * adam_second[0].astype(jnp.float32) + (1.0 - beta_two) * gradient * gradient
    )
    current = weights.astype(jnp.float32)
    inner = current - inner_rate * (
        first_new / (jnp.sqrt(second_new) + adam_epsilon) + weight_decay * current
    )
    merged = merge_weight * inner + (1.0 - merge_weight) * new_global
    return (
        merged.astype(jnp.bfloat16)[None],
        first_new.astype(jnp.bfloat16)[None],
        second_new.astype(jnp.bfloat16)[None],
        new_global,
        new_momentum,
    )


def solution(mesh):
    placed = (
        P("island", "fsdp", None),
        P("island", "fsdp", None),
        P("island", "fsdp", None),
        P("fsdp", None),
        P("fsdp", None),
        P("island", "fsdp", None),
        P("island", "fsdp", None),
    )
    return jax.shard_map(
        local,
        mesh=mesh,
        in_specs=placed,
        out_specs=(
            P("island", "fsdp", None),
            P("island", "fsdp", None),
            P("island", "fsdp", None),
            P("fsdp", None),
            P("fsdp", None),
        ),
        check_vma=False,
    )
```

```python
import functools

import jax
import jax.numpy as jnp
from jax import lax
from jax.experimental import pallas as pl
from jax.experimental.pallas import tpu as pltpu
from jax.sharding import PartitionSpec as P

HEAD_DIM = 128
MESH = pl.DeviceIdType.MESH

beta_one = 0.9
beta_two = 0.95
inner_rate = 0.02
weight_decay = 0.1
adam_epsilon = 1e-08
norm_epsilon = 1e-06
outer_rate = 0.7
outer_beta = 0.9
merge_weight = 0.5


def chunk_count(rows, islands):
    for chunks in (8, 4, 2, 1):
        if islands & (islands - 1) == 0 and rows % (islands * chunks * 16) == 0:
            return chunks
    return 0


def head_backward(keys, upstream, scale):
    squares = jnp.mean(keys * keys, axis=-1, keepdims=True)
    inverse = lax.rsqrt(squares + norm_epsilon)
    normed = keys * inverse
    projected = jnp.mean(upstream * normed, axis=-1, keepdims=True)
    return (inverse * (upstream - normed * projected) * scale).astype(jnp.bfloat16)


def exchange(islands, shards, chunks, scale, *refs):
    w_hbm, x_hbm, cot_hbm = refs[:3]
    if chunks:
        (grad, mean, w, x, cot, lsem, wp, xin, xp, psend, precv, kgin, kgp, kg, own,
         ysem, psem, ksem, csem, fsem, landed, part, gathered, hsem) = refs[3:]
    else:
        (grad, w, x, cot, lsem, wp, xin, xp, psend, precv, kgin, kgp, kg, own,
         ysem, psem, ksem, csem, fsem) = refs[3:]
    rows, width = w.shape
    chips = shards // 2
    island = lax.axis_index("island")
    shard = lax.axis_index("fsdp")
    core = lax.rem(shard, 2)
    chip = shard // 2
    partner = (island, chip * 2 + 1 - core)

    def peer(step):
        return (island, lax.rem(chip + step, chips) * 2 + core)

    def back(step):
        return (island, lax.rem(chip + chips - step, chips) * 2 + core)

    targets = [partner] + [peer(step) for step in range(1, chips)]
    if chunks:
        levels = islands.bit_length() - 1
        sides = [lax.rem(island // 2**bit, 2) for bit in range(levels)]
        mates = [(island + (1 - 2 * sides[bit]) * 2**bit, shard) for bit in range(levels)]
        targets += mates

    loads = [
        pltpu.make_async_copy(source, place, lsem.at[index])
        for index, (source, place) in enumerate(((w_hbm, w), (x_hbm, x), (cot_hbm, cot)))
    ]
    for load in loads:
        load.start()

    barrier = pltpu.get_barrier_semaphore()
    for target in targets:
        pl.semaphore_signal(barrier, inc=1, device_id=target, device_id_type=MESH)
    pl.semaphore_wait(barrier, len(targets))

    def remote(src, dst, sems, where, target):
        return pltpu.make_async_remote_copy(
            src_ref=src,
            dst_ref=dst,
            send_sem=sems.at[(0,) + where],
            recv_sem=sems.at[(1,) + where],
            device_id=target,
            device_id_type=MESH,
        )

    def columns(start):
        return pl.ds(pl.multiple_of(start, rows), rows)

    copies = []

    def begin(copy):
        copy.start()
        copies.append(copy)
        return copy

    y1 = []
    for step in range(1, chips):
        there = lax.rem(chip + step, chips)
        y1.append(begin(remote(
            x_hbm.at[:, pl.ds(pl.multiple_of(there * 2 * rows, 2 * rows), 2 * rows)],
            xin.at[step - 1], ysem, (step - 1,), peer(step))))
    halves, returns = {}, {}
    if chunks:
        span = rows // chunks
        orders = [
            [1, 0] + list(range(2, levels)) if levels > 1 and q % 2 == 1 else list(range(levels))
            for q in range(chunks)
        ]
        starts = []
        for q in range(chunks):
            begins = [q * span]
            for level, bit in enumerate(orders[q]):
                begins.append(begins[level] + sides[bit] * (span >> (level + 1)))
            starts.append(begins)

    def segment(q, level):
        return pl.ds(pl.multiple_of(starts[q][level], span >> level), span >> level)

    def landing(level):
        return pl.ds(span - (span >> level), span >> (level + 1))

    def send_half(q, level):
        bit, size = orders[q][level], span >> (level + 1)
        away = starts[q][level] + (1 - sides[bit]) * size
        source = part if level else w_hbm
        halves[q, level] = begin(remote(
            source.at[pl.ds(pl.multiple_of(away, size), size)],
            landed.at[q, landing(level)], hsem, (q, level), mates[bit]))

    def send_back(q, level):
        place = segment(q, level + 1)
        returns[q, level] = begin(remote(
            gathered.at[place], gathered.at[place], hsem, (q, levels + level),
            mates[orders[q][level]]))

    for q in range(chunks):
        send_half(q, 0)
    wcopy = begin(remote(w_hbm, wp, csem, (0,), partner))
    xcopy = [begin(remote(
        x_hbm.at[:, columns((chip * 2 + 1 - core) * rows)], xp.at[0], csem, (1,), partner))]

    def step_of(q, stage):
        if stage < levels:
            halves[q, stage].wait_recv()
            place = segment(q, stage + 1)
            held = (part if stage else w)[place, :].astype(jnp.float32)
            total = held + landed[q, landing(stage), :].astype(jnp.float32)
            if stage + 1 < levels:
                part[place, :] = total.astype(jnp.bfloat16)
                send_half(q, stage + 1)
            else:
                gathered[place, :] = (total / islands).astype(jnp.bfloat16)
                send_back(q, levels - 1)
        else:
            level = 2 * levels - 1 - stage
            returns[q, level].wait_recv()
            if level:
                send_back(q, level - 1)

    def product(left, right):
        return jnp.dot(left, right, preferred_element_type=jnp.float32)

    stages = []
    for q in range(chunks):
        for stage in range(2 * levels):
            late = (q // 2) * 6.0 / chunks
            stages.append((stage + late, q, stage))
    stages.sort()

    def advance(until):
        while stages and stages[0][0] <= until:
            step_of(*stages.pop(0)[1:])

    for load in loads:
        load.wait()
    advance(0.5)
    wcopy.wait_recv()
    own[...] = product(x[:, columns(shard * rows)], w[...]) + product(
        x[:, columns((chip * 2 + 1 - core) * rows)], wp[...])
    advance(3.3)

    y3 = []
    for step in range(1, chips):
        y1[step - 1].wait_recv()
        xcopy.append(begin(remote(
            xin.at[step - 1, :, columns((1 - core) * rows)], xp.at[step], csem, (step + 1,), partner)))
        psend[step - 1] = (product(xin[step - 1, :, columns(core * rows)], w[...]) + product(
            xin[step - 1, :, columns((1 - core) * rows)], wp[...])).astype(jnp.bfloat16)
        y3.append(begin(remote(
            psend.at[step - 1], precv.at[step - 1], psem, (step - 1,), back(step))))
    advance(5.1)

    keys = own[...]
    for step in range(1, chips):
        y3[step - 1].wait_recv()
        keys += precv[step - 1].astype(jnp.float32)
    keys = keys * scale
    for head in range(width // HEAD_DIM):
        lanes = slice(head * HEAD_DIM, (head + 1) * HEAD_DIM)
        kg[:, lanes] = head_backward(keys[:, lanes], cot[:, lanes].astype(jnp.float32), scale)
    y4 = [
        begin(remote(kg, kgin.at[step - 1], ksem, (step - 1,), peer(step)))
        for step in range(1, chips)
    ]
    forwards = [begin(remote(kg, kgp.at[0], fsem, (0,), partner))]

    tile = min(256, rows)

    def add_block(read, upstream, first=False):
        @pl.loop(0, rows // tile)
        def _(t):
            start = pl.multiple_of(t * tile, tile)
            term = lax.dot_general(
                read(start), upstream[...], (((0,), (0,)), ((), ())),
                preferred_element_type=jnp.float32,
            ).astype(jnp.bfloat16).astype(jnp.float32)
            place = pl.ds(start, tile)
            grad[place, :] = term if first else grad[place, :] + term

    def lane(base):
        def at(start):
            return pl.ds(pl.multiple_of(base + start, tile), tile)
        return at

    mine = lane(shard * rows)
    add_block(lambda start: x[:, mine(start)], kg, first=True)
    forwards[0].wait_recv()
    xcopy[0].wait_recv()
    add_block(lambda start: xp[0, :, pl.ds(start, tile)], kgp.at[0])
    advance(6.4)
    inner = lane(core * rows)
    for step in range(1, chips):
        y4[step - 1].wait_recv()
        forwards.append(begin(remote(
            kgin.at[step - 1], kgp.at[step], fsem, (step,), partner)))
        add_block(lambda start: xin[step - 1, :, inner(start)], kgin.at[step - 1])
    advance(6.9)
    for step in range(1, chips):
        xcopy[step].wait_recv()
        forwards[step].wait_recv()
        add_block(lambda start: xp[step, :, pl.ds(start, tile)], kgp.at[step])
    advance(1000)
    if chunks:
        mean[...] = gathered[...]
    for copy in copies:
        copy.wait_send()


def token_splits(count):
    if count % 64 == 0:
        return (count // 2, count // 4, count // 4)
    return (count,)


def pieces_of(rows, islands, shards):
    if shards != 4 or islands != 2 * shards:
        return ()
    for grades in ((1,) * 8, (1,) * 4, (1,)):
        unit, rest = divmod(rows // 2, sum(grades))
        if rest == 0 and unit % 16 == 0:
            return tuple(unit * grade for grade in grades)
    return ()


def window(islands, pieces, splits, scale, *refs):
    w_hbm, m_hbm, s_hbm, gw_hbm, om_hbm, x_hbm, cot_hbm = refs[:7]
    nf, ns, half_inner, mean, gw, om = refs[7:13]
    (wc, xc, xin, cot, own, psend, precv, kg, kgin, grad, m, s,
     rsin, pin, qin, pout, res,
     load_sem, sent, first, rail, cross, gathered, kept_sem, passed) = refs[13:]
    rows, width = mean.shape
    half = rows // 2
    groups = range(len(pieces))
    token_count = x_hbm.shape[0]
    count = 2 * len(pieces)
    begins = [sum(pieces[:j]) for j in groups]
    f32, bf16 = jnp.float32, jnp.bfloat16

    island = lax.axis_index("island")
    shard = lax.axis_index("fsdp")
    core = lax.rem(shard, 2)
    chip = shard // 2
    side = lax.rem(island, 2)
    level = island // 2
    inside = level * (3 - level) // 2

    partner = (island, chip * 2 + 1 - core)

    def across(c):
        return (island, (1 - chip) * 2 + c)

    def beside(c):
        return (island + 1 - 2 * side, chip * 2 + c)

    pair = ((level + 1 - 2 * lax.rem(level, 2)) * 2 + side, shard)
    middle = ((3 - level) * 2 + side, shard)

    offsets = [sum(splits[:i]) for i in range(len(splits))]

    def block(c, i):
        return pl.ds(2 * offsets[i] + c * splits[i], splits[i])

    def both(i):
        return pl.ds(2 * offsets[i], 2 * splits[i])

    def source(i):
        return pl.ds(offsets[i], splits[i])

    def lanes(start, extent):
        return pl.ds(pl.multiple_of(start, rows), extent)

    my_lanes = lanes(chip * 2 * rows, 2 * rows)
    core_rows = core * rows

    barrier = pltpu.get_barrier_semaphore()

    def greet(target):
        pl.semaphore_signal(barrier, inc=1, device_id=target, device_id_type=MESH)

    greet(partner)
    greet(beside(1))
    greet(across(0))

    @pl.when(core == 0)
    def _():
        greet(across(1))

    @pl.when(core == 1)
    def _():
        greet(beside(0))
        greet(pair)

    @pl.when((core == 1) & (inside == 1))
    def _():
        greet(middle)

    tokens = []
    wload = pltpu.make_async_copy(
        w_hbm, wc.at[pl.ds(pl.multiple_of(core_rows, rows), rows)], load_sem.at[0])
    wload.start()
    for i in range(len(splits)):
        place = pl.ds(pl.multiple_of(2 * offsets[i] + core * splits[i], splits[i]), splits[i])
        tokens.append(pltpu.make_async_copy(
            x_hbm.at[source(i), my_lanes], xc.at[place], load_sem.at[1]))
        tokens.append(pltpu.make_async_copy(
            cot_hbm.at[source(i)], cot.at[place], load_sem.at[2]))
    for load in tokens:
        load.start()

    pl.semaphore_wait(barrier, 4 + core * (1 + inside))

    def remote(src, dst, kind, into, target):
        return pltpu.make_async_remote_copy(
            src_ref=src, dst_ref=dst, send_sem=sent.at[kind], recv_sem=into,
            device_id=target, device_id_type=MESH)

    def all_tokens(ref):
        return ref.at[pl.ds(0, token_count)]

    def tokens_loaded():
        for ref, dst, index in ((x_hbm.at[:, my_lanes], xc, 1), (cot_hbm, cot, 2)):
            pltpu.make_async_copy(ref, all_tokens(dst), load_sem.at[index]).wait()

    def kept(j):
        return pl.multiple_of(side * half + begins[j], 16)

    def given(j):
        return pl.multiple_of((1 - side) * half + begins[j], 16)

    def kept_rows(j):
        return pl.ds(kept(j), pieces[j])

    def given_rows(j):
        return pl.ds(given(j), pieces[j])

    def slot(k):
        return pl.ds(2 * begins[k // 2] + (k % 2) * pieces[k // 2], pieces[k // 2])

    group = len(pieces)
    parts = len(splits)

    def scatter_send(c, j):
        k = 2 * j + c
        return remote(w_hbm.at[given_rows(j)], rsin.at[slot(k)], 0, first.at[k], beside(1))

    def scatter_total():
        return remote(
            w_hbm.at[pl.ds(0, half)], rsin.at[pl.ds(0, half)], 0, first.at[0], beside(1))

    def token_send(c, i):
        return remote(
            x_hbm.at[source(i), lanes((1 - chip) * 2 * rows, 2 * rows)],
            xin.at[block(c, i)], 1, first.at[group + 2 * i + c], across(0))

    def token_total():
        return remote(
            x_hbm.at[:, lanes((1 - chip) * 2 * rows, 2 * rows)],
            all_tokens(xin), 1, first.at[group], across(0))

    def keep_send(j):
        extent = pieces[j] if j < 2 else half - begins[j]
        place = pl.ds(kept(j), extent)
        return remote(w_hbm.at[place], wc.at[place], 2, kept_sem.at[j], partner)

    def keep_total():
        return remote(
            w_hbm.at[pl.ds(0, half)], wc.at[pl.ds(0, half)], 2, kept_sem.at[0], partner)

    weight_send = remote(w_hbm, wc.at[pl.ds(rows, rows)], 2, cross.at[0], partner)

    def own_tokens_up(i):
        return remote(
            x_hbm.at[source(i), lanes((chip * 2 + 1) * rows, rows)],
            xc.at[block(0, i), pl.ds(rows, rows)], 3, passed.at[0], partner)

    def own_tokens_up_total():
        return remote(
            x_hbm.at[:, lanes((chip * 2 + 1) * rows, rows)],
            xc.at[pl.ds(0, token_count), pl.ds(rows, rows)], 3, passed.at[0], partner)

    def own_tokens_down(i):
        return remote(
            x_hbm.at[source(i), my_lanes], xc.at[block(1, i)], 3, passed.at[0], partner)

    def own_tokens_down_total():
        return remote(x_hbm.at[:, my_lanes], all_tokens(xc), 3, passed.at[0], partner)

    def cotangent_down(i):
        return remote(cot_hbm.at[source(i)], cot.at[block(1, i)], 4, passed.at[1], partner)

    def cotangent_total():
        return remote(cot_hbm, all_tokens(cot), 4, passed.at[1], partner)

    def tokens_forward(place):
        part = xin.at[place, pl.ds(rows, rows)]
        return remote(part, part, 4, passed.at[1], partner)

    def partial_send(place, i):
        return remote(psend.at[place], precv.at[place], 5, rail.at[i], across(0))

    def upstream_across(place, i):
        return remote(kg.at[place], kgin.at[place], 6, rail.at[parts + i], across(0))

    def upstream_down(place):
        return remote(kg.at[place], kg.at[place], 7, passed.at[2], partner)

    def upstream_forward(place):
        return remote(kgin.at[place], kgin.at[place], 8, passed.at[3], partner)

    def gather_send(k):
        return remote(
            res.at[slot(k)], mean.at[kept_rows(k // 2)], 5, gathered.at[k // 2], beside(k % 2))

    def gather_total():
        return remote(res, mean, 5, gathered.at[0], beside(0))

    def gather_recv(j):
        return remote(
            res.at[slot(2 * j)], mean.at[given_rows(j)], 5, gathered.at[j], beside(0))

    def deliver_send(j):
        return remote(res.at[slot(2 * j)], mean.at[kept_rows(j)], 6, first.at[j], partner)

    def deliver_total():
        return remote(
            res.at[pl.ds(0, half)], mean.at[pl.ds(0, half)], 6, first.at[0], partner)

    def outer_send(k):
        return remote(pout.at[slot(k)], pin.at[slot(k)], 7, rail.at[k], pair)

    def middle_send(k):
        return remote(pout.at[slot(k)], qin.at[slot(k)], 7, cross.at[k], middle)

    def part_total():
        return remote(pout, pin, 7, rail.at[0], pair)

    def result_send(k):
        return remote(res.at[slot(k)], res.at[slot(k)], 8, rail.at[k], pair)

    def result_total():
        return remote(res, res, 8, rail.at[0], pair)

    state_loads = [
        pltpu.make_async_copy(place, dst, load_sem.at[3 + index])
        for index, (place, dst) in enumerate(((m_hbm, m), (s_hbm, s), (gw_hbm, gw), (om_hbm, om)))
    ]

    def own_gradient(base):
        tile = min(256, rows)

        @pl.loop(0, rows // tile)
        def _(t):
            start = pl.multiple_of(t * tile, tile)
            grad[pl.ds(start, tile), :] = lax.dot_general(
                xc[:, pl.ds(pl.multiple_of(base + start, tile), tile)], kg[...],
                (((0,), (0,)), ((), ())), preferred_element_type=f32)

    def gradient_tile(base, start, tile):
        grad[pl.ds(start, tile), :] += lax.dot_general(
            xin[:, pl.ds(pl.multiple_of(base + start, tile), tile)], kgin[...],
            (((0,), (0,)), ((), ())), preferred_element_type=f32)
        step = min(32, tile)

        @pl.loop(0, tile // step)
        def _(u):
            place = pl.ds(pl.multiple_of(start + u * step, step), step)
            gradient = grad[place, :]
            first_new = beta_one * m[place, :].astype(f32) + (1.0 - beta_one) * gradient
            second_new = (
                beta_two * s[place, :].astype(f32) + (1.0 - beta_two) * gradient * gradient)
            nf[place, :] = first_new.astype(bf16)
            ns[place, :] = second_new.astype(bf16)
            current = wc[pl.ds(pl.multiple_of(base + start + u * step, step), step), :].astype(f32)
            inner = current - inner_rate * (
                first_new / (jnp.sqrt(second_new) + adam_epsilon) + weight_decay * current)
            half_inner[place, :] = merge_weight * inner

    def inner_update(base):
        tile = min(256, rows)

        @pl.loop(0, rows // tile)
        def _(t):
            gradient_tile(base, pl.multiple_of(t * tile, tile), tile)

    def matmul(out, place, left, convert):
        part = min(256, width)

        @pl.loop(0, width // part)
        def _(n):
            columns = pl.ds(pl.multiple_of(n * part, part), part)
            value = jnp.dot(left[...], wc[:, columns], preferred_element_type=f32)
            out[place, columns] = value.astype(bf16) if convert else value

    steps = range(len(splits))

    every = slice(None)

    @pl.when(core == 0)
    def _():
        for j in groups:
            scatter_send(0, j).start()
            if j < 3:
                keep_send(j).start()
            if j < 2 and j < parts:
                token_send(0, j).start()
        for i in steps:
            own_tokens_up(i).start()
        for load in state_loads:
            load.start()
        wload.wait()
        tokens_loaded()
        weight_send.wait_recv()
        own_tokens_down_total().wait_recv()
        matmul(own, every, xc, False)
        for i in steps:
            token_send(0, i).wait_recv()
            token_send(1, i).wait_recv()
            tokens_forward(both(i)).start()
            matmul(psend, both(i), xin.at[both(i)], True)
            partial_send(both(i), i).start()
            if i == 0:
                for later in steps[2:]:
                    token_send(0, later).start()
        cotangent_total().wait_recv()
        for i in steps:
            partial_send(both(i), i).wait_recv()
            for head in range(width // HEAD_DIM):
                columns = slice(head * HEAD_DIM, (head + 1) * HEAD_DIM)
                keys = (own[both(i), columns] + precv[both(i), columns].astype(f32)) * scale
                kg[both(i), columns] = head_backward(
                    keys, cot[both(i), columns].astype(f32), scale)
            upstream_across(both(i), i).start()
            upstream_down(both(i)).start()
        own_gradient(0)
        for i in steps:
            upstream_across(both(i), i).wait_recv()
            upstream_forward(both(i)).start()
        for load in state_loads:
            load.wait()
        inner_update(0)
        for j in groups:
            deliver_send(j).wait_recv()
            gather_recv(j).wait_recv()
        for total in (scatter_total(), token_total(), keep_total(), own_tokens_up_total(),
                      tokens_forward(every), partial_send(every, 0), upstream_across(every, 0),
                      upstream_down(every), upstream_forward(every)):
            total.wait_send()

    @pl.when(core == 1)
    def _():
        def held(k):
            j = k // 2
            place = pl.ds(pl.multiple_of((k % 2) * rows + kept(j), 16), pieces[j])
            return wc[place, :].astype(f32) + rsin[slot(k), :].astype(f32)

        def hand_out(k):
            gather_send(k).start()
            j = k // 2
            if k % 2:
                mean[kept_rows(j), :] = res[slot(k), :]
            else:
                deliver_send(j).start()

        for j in groups:
            scatter_send(1, j).start()
            if j < parts:
                token_send(1, j).start()
        weight_send.start()
        for i in steps:
            own_tokens_down(i).start()
            cotangent_down(i).start()
        for load in state_loads:
            load.start()
        wload.wait()

        def arrived(k):
            scatter_send(k % 2, k // 2).wait_recv()
            if k % 2 == 0 and k < 6:
                keep_send(k // 2).wait_recv()

        def outer_part(k):
            arrived(k)
            pout[slot(k), :] = held(k).astype(bf16)
            outer_send(k).start()

        def outer_result(k):
            result_send(k).wait_recv()
            hand_out(k)

        def middle_part(k):
            arrived(k)
            outer_send(k).wait_recv()
            pout[slot(k), :] = (held(k) + pin[slot(k), :].astype(f32)).astype(bf16)
            middle_send(k).start()

        def middle_result(k):
            middle_send(k).wait_recv()
            total = pout[slot(k), :].astype(f32) + qin[slot(k), :].astype(f32)
            res[slot(k), :] = (total / islands).astype(bf16)
            result_send(k).start()
            hand_out(k)

        tile = min(256, rows)
        tiles = rows // tile

        def gradient_start():
            tokens_loaded()
            own_tokens_up_total().wait_recv()
            upstream_down(every).wait_recv()
            own_gradient(rows)

        def gradient_ready():
            tokens_forward(every).wait_recv()
            upstream_forward(every).wait_recv()
            for load in state_loads:
                load.wait()

        ends = [2 * begins[k // 2] + (1 + k % 2) * pieces[k // 2] for k in range(count)]

        def interleave(first, second, lag, own_at, tiles_at):
            work = []
            if own_at < 16:
                work.append((own_at * rows // 16, gradient_start))
                work.append((tiles_at * rows // 16, gradient_ready))
                for t in range(tiles):
                    work.append(((tiles_at + t) * rows // 16, functools.partial(
                        gradient_tile, rows, t * tile, tile)))
            done = 0
            for k in range(count + 1):
                if k < count:
                    first(k)
                limit = rows * 2 if k == count else ends[k] - lag * rows // 16
                while done < count and ends[done] <= limit:
                    second(done)
                    while work and work[0][0] <= ends[done]:
                        work.pop(0)[1]()
                    done += 1
            for item in work:
                item[1]()

        @pl.when(inside == 0)
        def _():
            interleave(outer_part, outer_result, 16, 11, 15)

        @pl.when(level == 1)
        def _():
            interleave(middle_part, middle_result, 4, 16, 16)

        @pl.when(level == 2)
        def _():
            interleave(middle_part, middle_result, 4, 16, 16)

        @pl.when(inside == 1)
        def _():
            gradient_start()
            gradient_ready()
            inner_update(rows)

        for j in groups:
            gather_recv(j).wait_recv()

        @pl.when(inside == 1)
        def _():
            result_total().wait_send()

        for total in (scatter_total(), token_total(), weight_send, own_tokens_down_total(),
                      cotangent_total(), gather_total(), deliver_total(), part_total()):
            total.wait_send()


def finish(first, second, half_inner, mean, gw, om, nl, nf, ns, ng, nm, local, weights, momenta,
           sems):
    rows = mean.shape[0]
    tile = min(128, rows)
    step = min(32, tile)
    f32 = jnp.float32
    pltpu.make_async_copy(first, nf, sems.at[0]).start()
    pltpu.make_async_copy(second, ns, sems.at[1]).start()
    results = ((local, nl, sems.at[2]), (weights, ng, sems.at[3]), (momenta, nm, sems.at[4]))
    for t in range(rows // tile):
        @pl.loop(0, tile // step)
        def _(u):
            place = pl.ds(pl.multiple_of(t * tile + u * step, step), step)
            current = gw[place, :]
            outer_grad = current - mean[place, :].astype(f32)
            momentum = outer_beta * om[place, :] + outer_grad
            updated = current - outer_rate * (outer_grad + outer_beta * momentum)
            momenta[place, :] = momentum
            weights[place, :] = updated
            local[place, :] = (
                half_inner[place, :] + (1.0 - merge_weight) * updated).astype(jnp.bfloat16)

        part = pl.ds(t * tile, tile)
        for source, target, sem in results:
            pltpu.make_async_copy(source.at[part], target.at[part], sem).start()
    pltpu.make_async_copy(first, nf, sems.at[0]).wait()
    pltpu.make_async_copy(second, ns, sems.at[1]).wait()
    for source, target, sem in results:
        pltpu.make_async_copy(source, target, sem).wait()


def fused(pieces, local_weights, adam_first, adam_second, global_weights, outer_momentum, inputs,
          key_cotangent):
    arrays = (local_weights[0], adam_first[0], adam_second[0], global_weights, outer_momentum,
              inputs[0], key_cotangent[0])
    rows, width = arrays[0].shape
    count, depth = arrays[5].shape
    islands = lax.axis_size("island")
    splits = token_splits(count)
    groups = len(pieces)
    bf16, f32 = jnp.bfloat16, jnp.float32
    dma, vmem = pltpu.SemaphoreType.DMA, pltpu.VMEM
    narrow = jax.ShapeDtypeStruct((rows, width), bf16)
    wide = jax.ShapeDtypeStruct((rows, width), f32)
    carried = [narrow, narrow, wide, narrow, wide, wide]
    out_shape = [narrow] * 3 + [wide] * 2
    steps = len(splits)
    scratch = [
        vmem((2 * rows, width), bf16),
        vmem((2 * count, 2 * rows), bf16),
        vmem((2 * count, 2 * rows), bf16),
        vmem((2 * count, width), bf16),
        vmem((2 * count, width), f32),
        vmem((2 * count, width), bf16),
        vmem((2 * count, width), bf16),
        vmem((2 * count, width), bf16),
        vmem((2 * count, width), bf16),
        vmem((rows, width), f32),
        vmem((rows, width), bf16),
        vmem((rows, width), bf16),
    ] + [vmem((rows, width), bf16)] * 5 + [
        dma((7,)),
        dma((9,)),
        dma((max(2 * groups, groups + 2 * steps),)),
        dma((max(2 * groups, 2 * steps),)),
        dma((2 * groups,)),
        dma((groups,)),
        dma((min(groups, 3),)),
        dma((4,)),
    ]
    in_vmem = pl.BlockSpec(memory_space=pltpu.VMEM)
    in_hbm = pl.BlockSpec(memory_space=pltpu.HBM)
    results = pl.pallas_call(
        functools.partial(window, islands, pieces, splits, float(depth) ** (-0.5)),
        out_shape=carried,
        in_specs=[in_hbm] * len(arrays),
        out_specs=[in_vmem] * len(carried),
        scratch_shapes=scratch,
        compiler_params=pltpu.CompilerParams(
            collective_id=0, has_side_effects=True, vmem_limit_bytes=40 * 1024 * 1024
        ),
    )(*(pltpu.with_memory_space_constraint(a, pltpu.HBM) for a in arrays))
    written = pl.pallas_call(
        finish,
        out_shape=out_shape,
        in_specs=[in_vmem] * len(carried),
        out_specs=[in_hbm] * len(out_shape),
        scratch_shapes=[
            vmem((rows, width), bf16),
            vmem((rows, width), f32),
            vmem((rows, width), f32),
            dma((len(out_shape),)),
        ],
        compiler_params=pltpu.CompilerParams(vmem_limit_bytes=8 * 1024 * 1024),
    )(*results)
    return tuple(a[None] for a in written[:3]) + tuple(written[3:])


def local(
    local_weights, adam_first, adam_second, global_weights, outer_momentum, inputs, key_cotangent
):
    weights = local_weights[0]
    tokens = inputs[0]
    rows, width = weights.shape
    count, depth = tokens.shape
    scale = float(depth) ** (-0.5)
    islands, shards = lax.axis_size("island"), lax.axis_size("fsdp")
    chips = shards // 2
    others = max(chips - 1, 1)
    pieces = pieces_of(rows, islands, shards)
    if pieces and width % HEAD_DIM == 0:
        return fused(pieces, local_weights, adam_first, adam_second, global_weights,
                     outer_momentum, inputs, key_cotangent)
    chunks = chunk_count(rows, islands)
    bf16, f32 = jnp.bfloat16, jnp.float32
    dma = pltpu.SemaphoreType.DMA
    out_shape = [jax.ShapeDtypeStruct((rows, width), f32)]
    scratch = [
        pltpu.VMEM((rows, width), bf16),
        pltpu.VMEM((count, depth), bf16),
        pltpu.VMEM((count, width), bf16),
        dma((3,)),
        pltpu.VMEM((rows, width), bf16),
        pltpu.VMEM((others, count, 2 * rows), bf16),
        pltpu.VMEM((chips, count, rows), bf16),
        pltpu.VMEM((others, count, width), bf16),
        pltpu.VMEM((others, count, width), bf16),
        pltpu.VMEM((others, count, width), bf16),
        pltpu.VMEM((chips, count, width), bf16),
        pltpu.VMEM((count, width), bf16),
        pltpu.VMEM((count, width), f32),
        dma((2, others)),
        dma((2, others)),
        dma((2, others)),
        dma((2, chips + 1)),
        dma((2, chips)),
    ]
    if chunks:
        levels = islands.bit_length() - 1
        out_shape.append(jax.ShapeDtypeStruct((rows, width), bf16))
        scratch += [
            pltpu.VMEM((chunks, rows // chunks, width), bf16),
            pltpu.VMEM((rows, width), bf16),
            pltpu.VMEM((rows, width), bf16),
            dma((2, chunks, 2 * levels)),
        ]
    vmem = pl.BlockSpec(memory_space=pltpu.VMEM)
    results = pl.pallas_call(
        functools.partial(exchange, islands, shards, chunks, scale),
        out_shape=out_shape,
        in_specs=[pl.BlockSpec(memory_space=pltpu.HBM)] * 3,
        out_specs=[vmem] * len(out_shape),
        scratch_shapes=scratch,
        compiler_params=pltpu.CompilerParams(
            collective_id=0, has_side_effects=True, vmem_limit_bytes=40 * 1024 * 1024
        ),
    )(*(pltpu.with_memory_space_constraint(a, pltpu.HBM) for a in (weights, tokens, key_cotangent[0])))
    gradient = results[0]
    if chunks:
        mean_local = results[1].astype(jnp.float32)
    else:
        mean_local = lax.psum(weights.astype(jnp.float32), "island") / islands
    outer_grad = global_weights - mean_local
    new_momentum = outer_beta * outer_momentum + outer_grad
    new_global = global_weights - outer_rate * (outer_grad + outer_beta * new_momentum)
    first_new = beta_one * adam_first[0].astype(jnp.float32) + (1.0 - beta_one) * gradient
    second_new = (
        beta_two * adam_second[0].astype(jnp.float32) + (1.0 - beta_two) * gradient * gradient
    )
    current = weights.astype(jnp.float32)
    inner = current - inner_rate * (
        first_new / (jnp.sqrt(second_new) + adam_epsilon) + weight_decay * current
    )
    merged = merge_weight * inner + (1.0 - merge_weight) * new_global
    return (
        merged.astype(jnp.bfloat16)[None],
        first_new.astype(jnp.bfloat16)[None],
        second_new.astype(jnp.bfloat16)[None],
        new_global,
        new_momentum,
    )


def solution(mesh):
    placed = (
        P("island", "fsdp", None),
        P("island", "fsdp", None),
        P("island", "fsdp", None),
        P("fsdp", None),
        P("fsdp", None),
        P("island", "fsdp", None),
        P("island", "fsdp", None),
    )
    return jax.shard_map(
        local,
        mesh=mesh,
        in_specs=placed,
        out_specs=(
            P("island", "fsdp", None),
            P("island", "fsdp", None),
            P("island", "fsdp", None),
            P("fsdp", None),
            P("fsdp", None),
        ),
        check_vma=False,
    )
```

```python
import functools

import jax
import jax.numpy as jnp
from jax import lax
from jax.experimental import pallas as pl
from jax.experimental.pallas import tpu as pltpu
from jax.sharding import PartitionSpec as P

HEAD_DIM = 128
MESH = pl.DeviceIdType.MESH

beta_one = 0.9
beta_two = 0.95
inner_rate = 0.02
weight_decay = 0.1
adam_epsilon = 1e-08
norm_epsilon = 1e-06
outer_rate = 0.7
outer_beta = 0.9
merge_weight = 0.5


def chunk_count(rows, islands):
    for chunks in (8, 4, 2, 1):
        if islands & (islands - 1) == 0 and rows % (islands * chunks * 16) == 0:
            return chunks
    return 0


def head_backward(keys, upstream, scale):
    squares = jnp.mean(keys * keys, axis=-1, keepdims=True)
    inverse = lax.rsqrt(squares + norm_epsilon)
    normed = keys * inverse
    projected = jnp.mean(upstream * normed, axis=-1, keepdims=True)
    return (inverse * (upstream - normed * projected) * scale).astype(jnp.bfloat16)


def exchange(islands, shards, chunks, scale, *refs):
    w_hbm, x_hbm, cot_hbm = refs[:3]
    if chunks:
        (grad, mean, w, x, cot, lsem, wp, xin, xp, psend, precv, kgin, kgp, kg, own,
         ysem, psem, ksem, csem, fsem, landed, part, gathered, hsem) = refs[3:]
    else:
        (grad, w, x, cot, lsem, wp, xin, xp, psend, precv, kgin, kgp, kg, own,
         ysem, psem, ksem, csem, fsem) = refs[3:]
    rows, width = w.shape
    chips = shards // 2
    island = lax.axis_index("island")
    shard = lax.axis_index("fsdp")
    core = lax.rem(shard, 2)
    chip = shard // 2
    partner = (island, chip * 2 + 1 - core)

    def peer(step):
        return (island, lax.rem(chip + step, chips) * 2 + core)

    def back(step):
        return (island, lax.rem(chip + chips - step, chips) * 2 + core)

    targets = [partner] + [peer(step) for step in range(1, chips)]
    if chunks:
        levels = islands.bit_length() - 1
        sides = [lax.rem(island // 2**bit, 2) for bit in range(levels)]
        mates = [(island + (1 - 2 * sides[bit]) * 2**bit, shard) for bit in range(levels)]
        targets += mates

    loads = [
        pltpu.make_async_copy(source, place, lsem.at[index])
        for index, (source, place) in enumerate(((w_hbm, w), (x_hbm, x), (cot_hbm, cot)))
    ]
    for load in loads:
        load.start()

    barrier = pltpu.get_barrier_semaphore()
    for target in targets:
        pl.semaphore_signal(barrier, inc=1, device_id=target, device_id_type=MESH)
    pl.semaphore_wait(barrier, len(targets))

    def remote(src, dst, sems, where, target):
        return pltpu.make_async_remote_copy(
            src_ref=src,
            dst_ref=dst,
            send_sem=sems.at[(0,) + where],
            recv_sem=sems.at[(1,) + where],
            device_id=target,
            device_id_type=MESH,
        )

    def columns(start):
        return pl.ds(pl.multiple_of(start, rows), rows)

    copies = []

    def begin(copy):
        copy.start()
        copies.append(copy)
        return copy

    y1 = []
    for step in range(1, chips):
        there = lax.rem(chip + step, chips)
        y1.append(begin(remote(
            x_hbm.at[:, pl.ds(pl.multiple_of(there * 2 * rows, 2 * rows), 2 * rows)],
            xin.at[step - 1], ysem, (step - 1,), peer(step))))
    halves, returns = {}, {}
    if chunks:
        span = rows // chunks
        orders = [
            [1, 0] + list(range(2, levels)) if levels > 1 and q % 2 == 1 else list(range(levels))
            for q in range(chunks)
        ]
        starts = []
        for q in range(chunks):
            begins = [q * span]
            for level, bit in enumerate(orders[q]):
                begins.append(begins[level] + sides[bit] * (span >> (level + 1)))
            starts.append(begins)

    def segment(q, level):
        return pl.ds(pl.multiple_of(starts[q][level], span >> level), span >> level)

    def landing(level):
        return pl.ds(span - (span >> level), span >> (level + 1))

    def send_half(q, level):
        bit, size = orders[q][level], span >> (level + 1)
        away = starts[q][level] + (1 - sides[bit]) * size
        source = part if level else w_hbm
        halves[q, level] = begin(remote(
            source.at[pl.ds(pl.multiple_of(away, size), size)],
            landed.at[q, landing(level)], hsem, (q, level), mates[bit]))

    def send_back(q, level):
        place = segment(q, level + 1)
        returns[q, level] = begin(remote(
            gathered.at[place], gathered.at[place], hsem, (q, levels + level),
            mates[orders[q][level]]))

    for q in range(chunks):
        send_half(q, 0)
    wcopy = begin(remote(w_hbm, wp, csem, (0,), partner))
    xcopy = [begin(remote(
        x_hbm.at[:, columns((chip * 2 + 1 - core) * rows)], xp.at[0], csem, (1,), partner))]

    def step_of(q, stage):
        if stage < levels:
            halves[q, stage].wait_recv()
            place = segment(q, stage + 1)
            held = (part if stage else w)[place, :].astype(jnp.float32)
            total = held + landed[q, landing(stage), :].astype(jnp.float32)
            if stage + 1 < levels:
                part[place, :] = total.astype(jnp.bfloat16)
                send_half(q, stage + 1)
            else:
                gathered[place, :] = (total / islands).astype(jnp.bfloat16)
                send_back(q, levels - 1)
        else:
            level = 2 * levels - 1 - stage
            returns[q, level].wait_recv()
            if level:
                send_back(q, level - 1)

    def product(left, right):
        return jnp.dot(left, right, preferred_element_type=jnp.float32)

    stages = []
    for q in range(chunks):
        for stage in range(2 * levels):
            late = (q // 2) * 6.0 / chunks
            stages.append((stage + late, q, stage))
    stages.sort()

    def advance(until):
        while stages and stages[0][0] <= until:
            step_of(*stages.pop(0)[1:])

    for load in loads:
        load.wait()
    advance(0.5)
    wcopy.wait_recv()
    own[...] = product(x[:, columns(shard * rows)], w[...]) + product(
        x[:, columns((chip * 2 + 1 - core) * rows)], wp[...])
    advance(3.3)

    y3 = []
    for step in range(1, chips):
        y1[step - 1].wait_recv()
        xcopy.append(begin(remote(
            xin.at[step - 1, :, columns((1 - core) * rows)], xp.at[step], csem, (step + 1,), partner)))
        psend[step - 1] = (product(xin[step - 1, :, columns(core * rows)], w[...]) + product(
            xin[step - 1, :, columns((1 - core) * rows)], wp[...])).astype(jnp.bfloat16)
        y3.append(begin(remote(
            psend.at[step - 1], precv.at[step - 1], psem, (step - 1,), back(step))))
    advance(5.1)

    keys = own[...]
    for step in range(1, chips):
        y3[step - 1].wait_recv()
        keys += precv[step - 1].astype(jnp.float32)
    keys = keys * scale
    for head in range(width // HEAD_DIM):
        lanes = slice(head * HEAD_DIM, (head + 1) * HEAD_DIM)
        kg[:, lanes] = head_backward(keys[:, lanes], cot[:, lanes].astype(jnp.float32), scale)
    y4 = [
        begin(remote(kg, kgin.at[step - 1], ksem, (step - 1,), peer(step)))
        for step in range(1, chips)
    ]
    forwards = [begin(remote(kg, kgp.at[0], fsem, (0,), partner))]

    tile = min(256, rows)

    def add_block(read, upstream, first=False):
        @pl.loop(0, rows // tile)
        def _(t):
            start = pl.multiple_of(t * tile, tile)
            term = lax.dot_general(
                read(start), upstream[...], (((0,), (0,)), ((), ())),
                preferred_element_type=jnp.float32,
            ).astype(jnp.bfloat16).astype(jnp.float32)
            place = pl.ds(start, tile)
            grad[place, :] = term if first else grad[place, :] + term

    def lane(base):
        def at(start):
            return pl.ds(pl.multiple_of(base + start, tile), tile)
        return at

    mine = lane(shard * rows)
    add_block(lambda start: x[:, mine(start)], kg, first=True)
    forwards[0].wait_recv()
    xcopy[0].wait_recv()
    add_block(lambda start: xp[0, :, pl.ds(start, tile)], kgp.at[0])
    advance(6.4)
    inner = lane(core * rows)
    for step in range(1, chips):
        y4[step - 1].wait_recv()
        forwards.append(begin(remote(
            kgin.at[step - 1], kgp.at[step], fsem, (step,), partner)))
        add_block(lambda start: xin[step - 1, :, inner(start)], kgin.at[step - 1])
    advance(6.9)
    for step in range(1, chips):
        xcopy[step].wait_recv()
        forwards[step].wait_recv()
        add_block(lambda start: xp[step, :, pl.ds(start, tile)], kgp.at[step])
    advance(1000)
    if chunks:
        mean[...] = gathered[...]
    for copy in copies:
        copy.wait_send()


def token_splits(count):
    if count % 64 == 0:
        return (count // 2, count // 4, count // 4)
    return (count,)


def pieces_of(rows, islands, shards):
    if shards != 4 or islands != 2 * shards:
        return ()
    for grades in ((1,) * 8, (1,) * 4, (1,)):
        unit, rest = divmod(rows // 2, sum(grades))
        if rest == 0 and unit % 16 == 0:
            return tuple(unit * grade for grade in grades)
    return ()


def inner_step(gradient, first, second, current):
    first_new = beta_one * first.astype(jnp.float32) + (1.0 - beta_one) * gradient
    second_new = beta_two * second.astype(jnp.float32) + (1.0 - beta_two) * gradient * gradient
    current = current.astype(jnp.float32)
    inner = current - inner_rate * (
        first_new / (jnp.sqrt(second_new) + adam_epsilon) + weight_decay * current)
    return first_new.astype(jnp.bfloat16), second_new.astype(jnp.bfloat16), merge_weight * inner


def window(islands, pieces, splits, scale, *refs):
    w_hbm, m_hbm, s_hbm, gw_hbm, om_hbm, x_hbm, cot_hbm = refs[:7]
    nf, ns, half_inner, mean, gw, om, grad, m, s, late = refs[7:17]
    (wc, xc, xin, cot, own, psend, precv, kg, kgin, xct, xint,
     rsin, pin, qin, pout, res,
     load_sem, sent, first, rail, cross, gathered, kept_sem, passed, ready) = refs[17:]
    rows, width = mean.shape
    half = rows // 2
    groups = range(len(pieces))
    token_count = x_hbm.shape[0]
    count = 2 * len(pieces)
    begins = [sum(pieces[:j]) for j in groups]
    f32, bf16 = jnp.float32, jnp.bfloat16

    island = lax.axis_index("island")
    shard = lax.axis_index("fsdp")
    core = lax.rem(shard, 2)
    chip = shard // 2
    side = lax.rem(island, 2)
    level = island // 2
    inside = level * (3 - level) // 2

    partner = (island, chip * 2 + 1 - core)

    def across(c):
        return (island, (1 - chip) * 2 + c)

    def beside(c):
        return (island + 1 - 2 * side, chip * 2 + c)

    pair = ((level + 1 - 2 * lax.rem(level, 2)) * 2 + side, shard)
    middle = ((3 - level) * 2 + side, shard)

    offsets = [sum(splits[:i]) for i in range(len(splits))]

    def block(c, i):
        return pl.ds(2 * offsets[i] + c * splits[i], splits[i])

    def both(i):
        return pl.ds(2 * offsets[i], 2 * splits[i])

    def source(i):
        return pl.ds(offsets[i], splits[i])

    def lanes(start, extent):
        return pl.ds(pl.multiple_of(start, rows), extent)

    my_lanes = lanes(chip * 2 * rows, 2 * rows)
    core_rows = core * rows

    barrier = pltpu.get_barrier_semaphore()

    def greet(target):
        pl.semaphore_signal(barrier, inc=1, device_id=target, device_id_type=MESH)

    greet(partner)
    greet(beside(1))

    @pl.when(chip == 0)
    def _():
        greet(across(0))

    @pl.when((core == 0) & (chip == 0))
    def _():
        greet(across(1))

    @pl.when(core == 1)
    def _():
        greet(beside(0))
        greet(pair)

    @pl.when((core == 1) & (inside == 1))
    def _():
        greet(middle)

    tokens = []
    wload = pltpu.make_async_copy(
        w_hbm, wc.at[pl.ds(pl.multiple_of(core_rows, rows), rows)], load_sem.at[0])
    wload.start()
    for i in range(len(splits)):
        place = pl.ds(pl.multiple_of(2 * offsets[i] + core * splits[i], splits[i]), splits[i])
        tokens.append(pltpu.make_async_copy(
            x_hbm.at[source(i), my_lanes], xc.at[place], load_sem.at[1]))
        tokens.append(pltpu.make_async_copy(
            cot_hbm.at[source(i)], cot.at[place], load_sem.at[2]))
    for load in tokens:
        load.start()

    pl.semaphore_wait(barrier, 4 + core * (1 + inside) - (1 - chip) * (2 - core))

    @pl.when((core == 0) & (chip == 1))
    def _():
        for c in range(2):
            pl.semaphore_signal(ready, inc=1, device_id=across(c), device_id_type=MESH)

    def reach_across():
        @pl.when(chip == 0)
        def _():
            pl.semaphore_wait(ready, 1)

    def remote(src, dst, kind, into, target):
        return pltpu.make_async_remote_copy(
            src_ref=src, dst_ref=dst, send_sem=sent.at[kind], recv_sem=into,
            device_id=target, device_id_type=MESH)

    def all_tokens(ref):
        return ref.at[pl.ds(0, token_count)]

    def tokens_loaded():
        for ref, dst, index in ((x_hbm.at[:, my_lanes], xc, 1), (cot_hbm, cot, 2)):
            pltpu.make_async_copy(ref, all_tokens(dst), load_sem.at[index]).wait()

    def kept(j):
        return pl.multiple_of(side * half + begins[j], 16)

    def given(j):
        return pl.multiple_of((1 - side) * half + begins[j], 16)

    def kept_rows(j):
        return pl.ds(kept(j), pieces[j])

    def given_rows(j):
        return pl.ds(given(j), pieces[j])

    def slot(k):
        return pl.ds(2 * begins[k // 2] + (k % 2) * pieces[k // 2], pieces[k // 2])

    group = len(pieces)
    parts = len(splits)

    def scatter_send(c, j):
        k = 2 * j + c
        return remote(w_hbm.at[given_rows(j)], rsin.at[slot(k)], 0, first.at[k], beside(1))

    def scatter_total():
        return remote(
            w_hbm.at[pl.ds(0, half)], rsin.at[pl.ds(0, half)], 0, first.at[0], beside(1))

    def token_send(c, i):
        return remote(
            x_hbm.at[source(i), lanes((1 - chip) * 2 * rows, 2 * rows)],
            xin.at[block(c, i)], 1, first.at[group + 2 * i + c], across(0))

    def token_total():
        return remote(
            x_hbm.at[:, lanes((1 - chip) * 2 * rows, 2 * rows)],
            all_tokens(xin), 1, first.at[group], across(0))

    def keep_send(j):
        extent = pieces[j] if j < 2 else half - begins[j]
        place = pl.ds(kept(j), extent)
        return remote(w_hbm.at[place], wc.at[place], 2, kept_sem.at[j], partner)

    def keep_total():
        return remote(
            w_hbm.at[pl.ds(0, half)], wc.at[pl.ds(0, half)], 2, kept_sem.at[0], partner)

    weight_send = remote(w_hbm, wc.at[pl.ds(rows, rows)], 2, cross.at[0], partner)

    def own_tokens_up(i):
        return remote(
            x_hbm.at[source(i), lanes((chip * 2 + 1) * rows, rows)],
            xc.at[block(0, i), pl.ds(rows, rows)], 3, passed.at[0], partner)

    def own_tokens_up_total():
        return remote(
            x_hbm.at[:, lanes((chip * 2 + 1) * rows, rows)],
            xc.at[pl.ds(0, token_count), pl.ds(rows, rows)], 3, passed.at[0], partner)

    def own_tokens_down(i):
        return remote(
            x_hbm.at[source(i), my_lanes], xc.at[block(1, i)], 3, passed.at[0], partner)

    def own_tokens_down_total():
        return remote(x_hbm.at[:, my_lanes], all_tokens(xc), 3, passed.at[0], partner)

    def cotangent_down(i):
        return remote(cot_hbm.at[source(i)], cot.at[block(1, i)], 4, passed.at[1], partner)

    def cotangent_total():
        return remote(cot_hbm, all_tokens(cot), 4, passed.at[1], partner)

    def tokens_forward(place):
        part = xin.at[place, pl.ds(rows, rows)]
        return remote(part, part, 4, passed.at[1], partner)

    def partial_send(place, i):
        return remote(psend.at[place], precv.at[place], 5, rail.at[i], across(0))

    def upstream_across(place, i):
        return remote(kg.at[place], kgin.at[place], 6, rail.at[parts + i], across(0))

    def upstream_down(place):
        return remote(kg.at[place], kg.at[place], 7, passed.at[2], partner)

    def upstream_forward(place):
        return remote(kgin.at[place], kgin.at[place], 8, passed.at[3], partner)

    def gather_send(k):
        return remote(
            res.at[slot(k)], mean.at[kept_rows(k // 2)], 5, gathered.at[k // 2], beside(k % 2))

    def gather_total():
        return remote(res, mean, 5, gathered.at[0], beside(0))

    def gather_recv(j):
        return remote(
            res.at[slot(2 * j)], mean.at[given_rows(j)], 5, gathered.at[j], beside(0))

    def deliver_send(j):
        return remote(res.at[slot(2 * j)], mean.at[kept_rows(j)], 6, first.at[j], partner)

    def deliver_total():
        return remote(
            res.at[pl.ds(0, half)], mean.at[pl.ds(0, half)], 6, first.at[0], partner)

    def outer_send(k):
        return remote(pout.at[slot(k)], pin.at[slot(k)], 7, rail.at[k], pair)

    def middle_send(k):
        return remote(pout.at[slot(k)], qin.at[slot(k)], 7, cross.at[k], middle)

    def part_total():
        return remote(pout, pin, 7, rail.at[0], pair)

    def result_send(k):
        return remote(res.at[slot(k)], res.at[slot(k)], 8, rail.at[k], pair)

    def result_total():
        return remote(res, res, 8, rail.at[0], pair)

    state_loads = [
        pltpu.make_async_copy(place, dst, load_sem.at[3 + index])
        for index, (place, dst) in enumerate((
            (m_hbm, m), (s_hbm, s), (gw_hbm, gw), (om_hbm, om),
            (w_hbm.at[pl.ds(rows - late.shape[0], late.shape[0])], late)))
    ]

    def turn(out, tokens_by_width, base, start, tile):
        columns = pl.ds(pl.multiple_of(base + start, tile), tile)
        out[pl.ds(start, tile), :] = tokens_by_width[:, columns].T

    def turn_all(out, tokens_by_width, base):
        tile = min(256, rows)

        @pl.loop(0, rows // tile)
        def _(t):
            turn(out, tokens_by_width, base, pl.multiple_of(t * tile, tile), tile)

    def own_gradient():
        tile = min(256, rows)

        @pl.loop(0, rows // tile)
        def _(t):
            place = pl.ds(pl.multiple_of(t * tile, tile), tile)
            grad[place, :] = jnp.dot(xct[place, :], kg[...], preferred_element_type=f32)

    def gradient_tile(base, start, tile):
        place = pl.ds(start, tile)
        grad[place, :] += jnp.dot(xint[place, :], kgin[...], preferred_element_type=f32)
        if start >= nf.shape[0]:
            return
        step = min(32, tile)

        @pl.loop(0, tile // step)
        def _(u):
            place = pl.ds(pl.multiple_of(start + u * step, step), step)
            current = wc[pl.ds(pl.multiple_of(base + start + u * step, step), step), :]
            first_new, second_new, inner = inner_step(
                grad[place, :], m[place, :], s[place, :], current)
            nf[place, :] = first_new
            ns[place, :] = second_new
            half_inner[place, :] = inner

    def inner_update(base):
        tile = min(256, rows)
        for t in range(rows // tile):
            gradient_tile(base, t * tile, tile)

    def matmul(out, place, left, convert):
        part = min(256, width)

        @pl.loop(0, width // part)
        def _(n):
            columns = pl.ds(pl.multiple_of(n * part, part), part)
            value = jnp.dot(left[...], wc[:, columns], preferred_element_type=f32)
            out[place, columns] = value.astype(bf16) if convert else value

    steps = range(len(splits))

    every = slice(None)

    @pl.when(core == 0)
    def _():
        for j in groups:
            scatter_send(0, j).start()
            if j < 3:
                keep_send(j).start()
        for i in steps:
            own_tokens_up(i).start()
        for load in state_loads:
            load.start()
        reach_across()
        for i in steps[:2]:
            token_send(0, i).start()
        wload.wait()
        tokens_loaded()
        weight_send.wait_recv()
        own_tokens_down_total().wait_recv()
        matmul(own, every, xc, False)
        turn_all(xct, xc, 0)
        for i in steps:
            token_send(0, i).wait_recv()
            token_send(1, i).wait_recv()
            tokens_forward(both(i)).start()
            matmul(psend, both(i), xin.at[both(i)], True)
            partial_send(both(i), i).start()
            if i == 0:
                for later in steps[2:]:
                    token_send(0, later).start()
        cotangent_total().wait_recv()
        for i in steps:
            partial_send(both(i), i).wait_recv()
            for head in range(width // HEAD_DIM):
                columns = slice(head * HEAD_DIM, (head + 1) * HEAD_DIM)
                keys = (own[both(i), columns] + precv[both(i), columns].astype(f32)) * scale
                kg[both(i), columns] = head_backward(
                    keys, cot[both(i), columns].astype(f32), scale)
            upstream_across(both(i), i).start()
            upstream_down(both(i)).start()
        own_gradient()
        turn_all(xint, xin, 0)
        for i in steps:
            upstream_across(both(i), i).wait_recv()
            upstream_forward(both(i)).start()
        for load in state_loads:
            load.wait()
        inner_update(0)
        for j in groups:
            deliver_send(j).wait_recv()
            gather_recv(j).wait_recv()
        for total in (scatter_total(), token_total(), keep_total(), own_tokens_up_total(),
                      tokens_forward(every), partial_send(every, 0), upstream_across(every, 0),
                      upstream_down(every), upstream_forward(every)):
            total.wait_send()

    @pl.when(core == 1)
    def _():
        def held(k):
            j = k // 2
            place = pl.ds(pl.multiple_of((k % 2) * rows + kept(j), 16), pieces[j])
            return wc[place, :].astype(f32) + rsin[slot(k), :].astype(f32)

        def hand_out(k):
            gather_send(k).start()
            j = k // 2
            if k % 2:
                mean[kept_rows(j), :] = res[slot(k), :]
            else:
                deliver_send(j).start()

        for j in groups:
            scatter_send(1, j).start()
        weight_send.start()
        for i in steps:
            own_tokens_down(i).start()
            cotangent_down(i).start()
        for load in state_loads:
            load.start()
        reach_across()
        for i in steps:
            token_send(1, i).start()
        wload.wait()

        def arrived(k):
            scatter_send(k % 2, k // 2).wait_recv()
            if k % 2 == 0 and k < 6:
                keep_send(k // 2).wait_recv()

        def outer_part(k):
            arrived(k)
            pout[slot(k), :] = held(k).astype(bf16)
            outer_send(k).start()

        def outer_result(k):
            result_send(k).wait_recv()
            hand_out(k)

        def middle_part(k):
            arrived(k)
            outer_send(k).wait_recv()
            pout[slot(k), :] = (held(k) + pin[slot(k), :].astype(f32)).astype(bf16)
            middle_send(k).start()

        def middle_result(k):
            middle_send(k).wait_recv()
            total = pout[slot(k), :].astype(f32) + qin[slot(k), :].astype(f32)
            res[slot(k), :] = (total / islands).astype(bf16)
            result_send(k).start()
            hand_out(k)

        tile = min(256, rows)
        tiles = rows // tile

        def own_tokens_ready():
            tokens_loaded()
            own_tokens_up_total().wait_recv()

        def gradient_start():
            upstream_down(every).wait_recv()
            own_gradient()

        def gradient_ready():
            upstream_forward(every).wait_recv()
            for load in state_loads:
                load.wait()

        ends = [2 * begins[k // 2] + (1 + k % 2) * pieces[k // 2] for k in range(count)]

        def interleave(first, second, lag, turn_at, own_at, tiles_at):
            unit = rows // 16
            work = []
            work.append((turn_at * unit, tokens_forward(every).wait_recv))
            for t in range(tiles):
                work.append(((turn_at + t) * unit, functools.partial(
                    turn, xint, xin, rows, t * tile, tile)))
            work.append((own_at * unit, gradient_start))
            work.append((tiles_at * unit, gradient_ready))
            for t in range(tiles):
                work.append(((tiles_at + t) * unit, functools.partial(
                    gradient_tile, rows, t * tile, tile)))
            done = 0
            for k in range(count + 1):
                if k < count:
                    first(k)
                limit = rows * 2 if k == count else ends[k] - lag * rows // 16
                while done < count and ends[done] <= limit:
                    second(done)
                    while work and work[0][0] <= ends[done]:
                        work.pop(0)[1]()
                    done += 1
            for item in work:
                item[1]()

        own_tokens_ready()
        turn_all(xct, xc, rows)

        @pl.when(inside == 0)
        def _():
            interleave(outer_part, outer_result, 16, 14, 14, 16)

        @pl.when(inside == 1)
        def _():
            interleave(middle_part, middle_result, 4, 16, 16, 16)

        for j in groups:
            gather_recv(j).wait_recv()

        @pl.when(inside == 1)
        def _():
            result_total().wait_send()

        for total in (scatter_total(), token_total(), weight_send, own_tokens_down_total(),
                      cotangent_total(), gather_total(), deliver_total(), part_total()):
            total.wait_send()


def finish(first, second, half_inner, mean, gw, om, grad, m, s, late, nl, nf, ns, ng, nm, local,
           weights, momenta, first_late, second_late, sems):
    rows = mean.shape[0]
    early = first.shape[0]
    tile = min(128, early)
    step = min(32, tile)
    f32 = jnp.float32
    begin = pl.ds(0, early)
    rest = pl.ds(early, rows - early)
    pltpu.make_async_copy(first, nf.at[begin], sems.at[0]).start()
    pltpu.make_async_copy(second, ns.at[begin], sems.at[1]).start()
    for t in range(rows // tile):
        after = t * tile - early

        @pl.loop(0, tile // step)
        def _(u):
            place = pl.ds(pl.multiple_of(t * tile + u * step, step), step)
            if after < 0:
                inner = half_inner[place, :]
            else:
                behind = pl.ds(pl.multiple_of(after + u * step, step), step)
                first_new, second_new, inner = inner_step(
                    grad[place, :], m[place, :], s[place, :], late[behind, :])
                first_late[behind, :] = first_new
                second_late[behind, :] = second_new
            current = gw[place, :]
            outer_grad = current - mean[place, :].astype(f32)
            momentum = outer_beta * om[place, :] + outer_grad
            updated = current - outer_rate * (outer_grad + outer_beta * momentum)
            momenta[place, :] = momentum
            weights[place, :] = updated
            local[place, :] = (inner + (1.0 - merge_weight) * updated).astype(jnp.bfloat16)

        part = pl.ds(t * tile, tile)
        if after >= 0:
            behind = pl.ds(after, tile)
            pltpu.make_async_copy(first_late.at[behind], nf.at[part], sems.at[5]).start()
            pltpu.make_async_copy(second_late.at[behind], ns.at[part], sems.at[6]).start()
        pltpu.make_async_copy(local.at[part], nl.at[part], sems.at[2]).start()
        pltpu.make_async_copy(weights.at[part], ng.at[part], sems.at[3]).start()
        pltpu.make_async_copy(momenta.at[part], nm.at[part], sems.at[4]).start()
    pltpu.make_async_copy(first, nf.at[begin], sems.at[0]).wait()
    pltpu.make_async_copy(second, ns.at[begin], sems.at[1]).wait()
    pltpu.make_async_copy(local, nl, sems.at[2]).wait()
    pltpu.make_async_copy(weights, ng, sems.at[3]).wait()
    pltpu.make_async_copy(momenta, nm, sems.at[4]).wait()
    pltpu.make_async_copy(first_late, nf.at[rest], sems.at[5]).wait()
    pltpu.make_async_copy(second_late, ns.at[rest], sems.at[6]).wait()


def fused(pieces, local_weights, adam_first, adam_second, global_weights, outer_momentum, inputs,
          key_cotangent):
    arrays = (local_weights[0], adam_first[0], adam_second[0], global_weights, outer_momentum,
              inputs[0], key_cotangent[0])
    rows, width = arrays[0].shape
    count, depth = arrays[5].shape
    islands = lax.axis_size("island")
    splits = token_splits(count)
    groups = len(pieces)
    bf16, f32 = jnp.bfloat16, jnp.float32
    dma, vmem = pltpu.SemaphoreType.DMA, pltpu.VMEM
    narrow = jax.ShapeDtypeStruct((rows, width), bf16)
    wide = jax.ShapeDtypeStruct((rows, width), f32)
    early = rows // 2
    part = jax.ShapeDtypeStruct((early, width), bf16)
    carried = [part, part, jax.ShapeDtypeStruct((early, width), f32), narrow, wide, wide, wide,
               narrow, narrow, jax.ShapeDtypeStruct((rows - early, width), bf16)]
    out_shape = [narrow] * 3 + [wide] * 2
    steps = len(splits)
    scratch = [
        vmem((2 * rows, width), bf16),
        vmem((2 * count, 2 * rows), bf16),
        vmem((2 * count, 2 * rows), bf16),
        vmem((2 * count, width), bf16),
        vmem((2 * count, width), f32),
        vmem((2 * count, width), bf16),
        vmem((2 * count, width), bf16),
        vmem((2 * count, width), bf16),
        vmem((2 * count, width), bf16),
        vmem((rows, 2 * count), bf16),
        vmem((rows, 2 * count), bf16),
    ] + [vmem((rows, width), bf16)] * 5 + [
        dma((8,)),
        dma((9,)),
        dma((max(2 * groups, groups + 2 * steps),)),
        dma((max(2 * groups, 2 * steps),)),
        dma((2 * groups,)),
        dma((groups,)),
        dma((min(groups, 3),)),
        dma((4,)),
        pltpu.SemaphoreType.REGULAR,
    ]
    in_vmem = pl.BlockSpec(memory_space=pltpu.VMEM)
    in_hbm = pl.BlockSpec(memory_space=pltpu.HBM)
    results = pl.pallas_call(
        functools.partial(window, islands, pieces, splits, float(depth) ** (-0.5)),
        out_shape=carried,
        in_specs=[in_hbm] * len(arrays),
        out_specs=[in_vmem] * len(carried),
        scratch_shapes=scratch,
        compiler_params=pltpu.CompilerParams(
            collective_id=0, has_side_effects=True, vmem_limit_bytes=40 * 1024 * 1024
        ),
    )(*(pltpu.with_memory_space_constraint(a, pltpu.HBM) for a in arrays))
    written = pl.pallas_call(
        finish,
        out_shape=out_shape,
        in_specs=[in_vmem] * len(carried),
        out_specs=[in_hbm] * len(out_shape),
        scratch_shapes=[
            vmem((rows, width), bf16),
            vmem((rows, width), f32),
            vmem((rows, width), f32),
            vmem((rows - early, width), bf16),
            vmem((rows - early, width), bf16),
            dma((7,)),
        ],
        compiler_params=pltpu.CompilerParams(vmem_limit_bytes=8 * 1024 * 1024),
    )(*results)
    return tuple(a[None] for a in written[:3]) + tuple(written[3:])


def local(
    local_weights, adam_first, adam_second, global_weights, outer_momentum, inputs, key_cotangent
):
    weights = local_weights[0]
    tokens = inputs[0]
    rows, width = weights.shape
    count, depth = tokens.shape
    scale = float(depth) ** (-0.5)
    islands, shards = lax.axis_size("island"), lax.axis_size("fsdp")
    chips = shards // 2
    others = max(chips - 1, 1)
    pieces = pieces_of(rows, islands, shards)
    if pieces and width % HEAD_DIM == 0:
        return fused(pieces, local_weights, adam_first, adam_second, global_weights,
                     outer_momentum, inputs, key_cotangent)
    chunks = chunk_count(rows, islands)
    bf16, f32 = jnp.bfloat16, jnp.float32
    dma = pltpu.SemaphoreType.DMA
    out_shape = [jax.ShapeDtypeStruct((rows, width), f32)]
    scratch = [
        pltpu.VMEM((rows, width), bf16),
        pltpu.VMEM((count, depth), bf16),
        pltpu.VMEM((count, width), bf16),
        dma((3,)),
        pltpu.VMEM((rows, width), bf16),
        pltpu.VMEM((others, count, 2 * rows), bf16),
        pltpu.VMEM((chips, count, rows), bf16),
        pltpu.VMEM((others, count, width), bf16),
        pltpu.VMEM((others, count, width), bf16),
        pltpu.VMEM((others, count, width), bf16),
        pltpu.VMEM((chips, count, width), bf16),
        pltpu.VMEM((count, width), bf16),
        pltpu.VMEM((count, width), f32),
        dma((2, others)),
        dma((2, others)),
        dma((2, others)),
        dma((2, chips + 1)),
        dma((2, chips)),
    ]
    if chunks:
        levels = islands.bit_length() - 1
        out_shape.append(jax.ShapeDtypeStruct((rows, width), bf16))
        scratch += [
            pltpu.VMEM((chunks, rows // chunks, width), bf16),
            pltpu.VMEM((rows, width), bf16),
            pltpu.VMEM((rows, width), bf16),
            dma((2, chunks, 2 * levels)),
        ]
    vmem = pl.BlockSpec(memory_space=pltpu.VMEM)
    results = pl.pallas_call(
        functools.partial(exchange, islands, shards, chunks, scale),
        out_shape=out_shape,
        in_specs=[pl.BlockSpec(memory_space=pltpu.HBM)] * 3,
        out_specs=[vmem] * len(out_shape),
        scratch_shapes=scratch,
        compiler_params=pltpu.CompilerParams(
            collective_id=0, has_side_effects=True, vmem_limit_bytes=40 * 1024 * 1024
        ),
    )(*(pltpu.with_memory_space_constraint(a, pltpu.HBM) for a in (weights, tokens, key_cotangent[0])))
    gradient = results[0]
    if chunks:
        mean_local = results[1].astype(jnp.float32)
    else:
        mean_local = lax.psum(weights.astype(jnp.float32), "island") / islands
    outer_grad = global_weights - mean_local
    new_momentum = outer_beta * outer_momentum + outer_grad
    new_global = global_weights - outer_rate * (outer_grad + outer_beta * new_momentum)
    first_new = beta_one * adam_first[0].astype(jnp.float32) + (1.0 - beta_one) * gradient
    second_new = (
        beta_two * adam_second[0].astype(jnp.float32) + (1.0 - beta_two) * gradient * gradient
    )
    current = weights.astype(jnp.float32)
    inner = current - inner_rate * (
        first_new / (jnp.sqrt(second_new) + adam_epsilon) + weight_decay * current
    )
    merged = merge_weight * inner + (1.0 - merge_weight) * new_global
    return (
        merged.astype(jnp.bfloat16)[None],
        first_new.astype(jnp.bfloat16)[None],
        second_new.astype(jnp.bfloat16)[None],
        new_global,
        new_momentum,
    )


def solution(mesh):
    placed = (
        P("island", "fsdp", None),
        P("island", "fsdp", None),
        P("island", "fsdp", None),
        P("fsdp", None),
        P("fsdp", None),
        P("island", "fsdp", None),
        P("island", "fsdp", None),
    )
    return jax.shard_map(
        local,
        mesh=mesh,
        in_specs=placed,
        out_specs=(
            P("island", "fsdp", None),
            P("island", "fsdp", None),
            P("island", "fsdp", None),
            P("fsdp", None),
            P("fsdp", None),
        ),
        check_vma=False,
    )
```

```python
import functools

import jax
import jax.numpy as jnp
from jax import lax
from jax.experimental import pallas as pl
from jax.experimental.pallas import tpu as pltpu
from jax.sharding import PartitionSpec as P

HEAD_DIM = 128
MESH = pl.DeviceIdType.MESH

beta_one = 0.9
beta_two = 0.95
inner_rate = 0.02
weight_decay = 0.1
adam_epsilon = 1e-08
norm_epsilon = 1e-06
outer_rate = 0.7
outer_beta = 0.9
merge_weight = 0.5


def chunk_count(rows, islands):
    for chunks in (8, 4, 2, 1):
        if islands & (islands - 1) == 0 and rows % (islands * chunks * 16) == 0:
            return chunks
    return 0


def head_backward(keys, upstream, scale):
    squares = jnp.mean(keys * keys, axis=-1, keepdims=True)
    inverse = lax.rsqrt(squares + norm_epsilon)
    normed = keys * inverse
    projected = jnp.mean(upstream * normed, axis=-1, keepdims=True)
    return (inverse * (upstream - normed * projected) * scale).astype(jnp.bfloat16)


def exchange(islands, shards, chunks, scale, *refs):
    w_hbm, x_hbm, cot_hbm = refs[:3]
    if chunks:
        (grad, mean, w, x, cot, lsem, wp, xin, xp, psend, precv, kgin, kgp, kg, own,
         ysem, psem, ksem, csem, fsem, landed, part, gathered, hsem) = refs[3:]
    else:
        (grad, w, x, cot, lsem, wp, xin, xp, psend, precv, kgin, kgp, kg, own,
         ysem, psem, ksem, csem, fsem) = refs[3:]
    rows, width = w.shape
    chips = shards // 2
    island = lax.axis_index("island")
    shard = lax.axis_index("fsdp")
    core = lax.rem(shard, 2)
    chip = shard // 2
    partner = (island, chip * 2 + 1 - core)

    def peer(step):
        return (island, lax.rem(chip + step, chips) * 2 + core)

    def back(step):
        return (island, lax.rem(chip + chips - step, chips) * 2 + core)

    targets = [partner] + [peer(step) for step in range(1, chips)]
    if chunks:
        levels = islands.bit_length() - 1
        sides = [lax.rem(island // 2**bit, 2) for bit in range(levels)]
        mates = [(island + (1 - 2 * sides[bit]) * 2**bit, shard) for bit in range(levels)]
        targets += mates

    loads = [
        pltpu.make_async_copy(source, place, lsem.at[index])
        for index, (source, place) in enumerate(((w_hbm, w), (x_hbm, x), (cot_hbm, cot)))
    ]
    for load in loads:
        load.start()

    barrier = pltpu.get_barrier_semaphore()
    for target in targets:
        pl.semaphore_signal(barrier, inc=1, device_id=target, device_id_type=MESH)
    pl.semaphore_wait(barrier, len(targets))

    def remote(src, dst, sems, where, target):
        return pltpu.make_async_remote_copy(
            src_ref=src,
            dst_ref=dst,
            send_sem=sems.at[(0,) + where],
            recv_sem=sems.at[(1,) + where],
            device_id=target,
            device_id_type=MESH,
        )

    def columns(start):
        return pl.ds(pl.multiple_of(start, rows), rows)

    copies = []

    def begin(copy):
        copy.start()
        copies.append(copy)
        return copy

    y1 = []
    for step in range(1, chips):
        there = lax.rem(chip + step, chips)
        y1.append(begin(remote(
            x_hbm.at[:, pl.ds(pl.multiple_of(there * 2 * rows, 2 * rows), 2 * rows)],
            xin.at[step - 1], ysem, (step - 1,), peer(step))))
    halves, returns = {}, {}
    if chunks:
        span = rows // chunks
        orders = [
            [1, 0] + list(range(2, levels)) if levels > 1 and q % 2 == 1 else list(range(levels))
            for q in range(chunks)
        ]
        starts = []
        for q in range(chunks):
            begins = [q * span]
            for level, bit in enumerate(orders[q]):
                begins.append(begins[level] + sides[bit] * (span >> (level + 1)))
            starts.append(begins)

    def segment(q, level):
        return pl.ds(pl.multiple_of(starts[q][level], span >> level), span >> level)

    def landing(level):
        return pl.ds(span - (span >> level), span >> (level + 1))

    def send_half(q, level):
        bit, size = orders[q][level], span >> (level + 1)
        away = starts[q][level] + (1 - sides[bit]) * size
        source = part if level else w_hbm
        halves[q, level] = begin(remote(
            source.at[pl.ds(pl.multiple_of(away, size), size)],
            landed.at[q, landing(level)], hsem, (q, level), mates[bit]))

    def send_back(q, level):
        place = segment(q, level + 1)
        returns[q, level] = begin(remote(
            gathered.at[place], gathered.at[place], hsem, (q, levels + level),
            mates[orders[q][level]]))

    for q in range(chunks):
        send_half(q, 0)
    wcopy = begin(remote(w_hbm, wp, csem, (0,), partner))
    xcopy = [begin(remote(
        x_hbm.at[:, columns((chip * 2 + 1 - core) * rows)], xp.at[0], csem, (1,), partner))]

    def step_of(q, stage):
        if stage < levels:
            halves[q, stage].wait_recv()
            place = segment(q, stage + 1)
            held = (part if stage else w)[place, :].astype(jnp.float32)
            total = held + landed[q, landing(stage), :].astype(jnp.float32)
            if stage + 1 < levels:
                part[place, :] = total.astype(jnp.bfloat16)
                send_half(q, stage + 1)
            else:
                gathered[place, :] = (total / islands).astype(jnp.bfloat16)
                send_back(q, levels - 1)
        else:
            level = 2 * levels - 1 - stage
            returns[q, level].wait_recv()
            if level:
                send_back(q, level - 1)

    def product(left, right):
        return jnp.dot(left, right, preferred_element_type=jnp.float32)

    stages = []
    for q in range(chunks):
        for stage in range(2 * levels):
            late = (q // 2) * 6.0 / chunks
            stages.append((stage + late, q, stage))
    stages.sort()

    def advance(until):
        while stages and stages[0][0] <= until:
            step_of(*stages.pop(0)[1:])

    for load in loads:
        load.wait()
    advance(0.5)
    wcopy.wait_recv()
    own[...] = product(x[:, columns(shard * rows)], w[...]) + product(
        x[:, columns((chip * 2 + 1 - core) * rows)], wp[...])
    advance(3.3)

    y3 = []
    for step in range(1, chips):
        y1[step - 1].wait_recv()
        xcopy.append(begin(remote(
            xin.at[step - 1, :, columns((1 - core) * rows)], xp.at[step], csem, (step + 1,), partner)))
        psend[step - 1] = (product(xin[step - 1, :, columns(core * rows)], w[...]) + product(
            xin[step - 1, :, columns((1 - core) * rows)], wp[...])).astype(jnp.bfloat16)
        y3.append(begin(remote(
            psend.at[step - 1], precv.at[step - 1], psem, (step - 1,), back(step))))
    advance(5.1)

    keys = own[...]
    for step in range(1, chips):
        y3[step - 1].wait_recv()
        keys += precv[step - 1].astype(jnp.float32)
    keys = keys * scale
    for head in range(width // HEAD_DIM):
        lanes = slice(head * HEAD_DIM, (head + 1) * HEAD_DIM)
        kg[:, lanes] = head_backward(keys[:, lanes], cot[:, lanes].astype(jnp.float32), scale)
    y4 = [
        begin(remote(kg, kgin.at[step - 1], ksem, (step - 1,), peer(step)))
        for step in range(1, chips)
    ]
    forwards = [begin(remote(kg, kgp.at[0], fsem, (0,), partner))]

    tile = min(256, rows)

    def add_block(read, upstream, first=False):
        @pl.loop(0, rows // tile)
        def _(t):
            start = pl.multiple_of(t * tile, tile)
            term = lax.dot_general(
                read(start), upstream[...], (((0,), (0,)), ((), ())),
                preferred_element_type=jnp.float32,
            ).astype(jnp.bfloat16).astype(jnp.float32)
            place = pl.ds(start, tile)
            grad[place, :] = term if first else grad[place, :] + term

    def lane(base):
        def at(start):
            return pl.ds(pl.multiple_of(base + start, tile), tile)
        return at

    mine = lane(shard * rows)
    add_block(lambda start: x[:, mine(start)], kg, first=True)
    forwards[0].wait_recv()
    xcopy[0].wait_recv()
    add_block(lambda start: xp[0, :, pl.ds(start, tile)], kgp.at[0])
    advance(6.4)
    inner = lane(core * rows)
    for step in range(1, chips):
        y4[step - 1].wait_recv()
        forwards.append(begin(remote(
            kgin.at[step - 1], kgp.at[step], fsem, (step,), partner)))
        add_block(lambda start: xin[step - 1, :, inner(start)], kgin.at[step - 1])
    advance(6.9)
    for step in range(1, chips):
        xcopy[step].wait_recv()
        forwards[step].wait_recv()
        add_block(lambda start: xp[step, :, pl.ds(start, tile)], kgp.at[step])
    advance(1000)
    if chunks:
        mean[...] = gathered[...]
    for copy in copies:
        copy.wait_send()


def token_splits(count):
    if count % 64 == 0:
        return (count // 2, count // 4, count // 4)
    return (count,)


def pieces_of(rows, islands, shards):
    if shards != 4 or islands != 2 * shards:
        return ()
    for grades in ((1,) * 8, (1,) * 4, (1,)):
        unit, rest = divmod(rows // 2, sum(grades))
        if rest == 0 and unit % 16 == 0:
            return tuple(unit * grade for grade in grades)
    return ()


def inner_step(gradient, first, second, current):
    first_new = beta_one * first.astype(jnp.float32) + (1.0 - beta_one) * gradient
    second_new = beta_two * second.astype(jnp.float32) + (1.0 - beta_two) * gradient * gradient
    current = current.astype(jnp.float32)
    inner = current - inner_rate * (
        first_new / (jnp.sqrt(second_new) + adam_epsilon) + weight_decay * current)
    return first_new.astype(jnp.bfloat16), second_new.astype(jnp.bfloat16), merge_weight * inner


def window(islands, pieces, splits, scale, *refs):
    w_hbm, m_hbm, s_hbm, gw_hbm, om_hbm, x_hbm, cot_hbm = refs[:7]
    nf, ns, half_inner, mean, gw, om, grad, m, s, late = refs[7:17]
    (wc, xc, xin, cot, own, psend, precv, kg, kgin, xct, xint,
     rsin, pin, qin, pout, res,
     load_sem, sent, first, rail, cross, gathered, kept_sem, passed, ready) = refs[17:]
    rows, width = mean.shape
    half = rows // 2
    groups = range(len(pieces))
    token_count = x_hbm.shape[0]
    count = 2 * len(pieces)
    begins = [sum(pieces[:j]) for j in groups]
    f32, bf16 = jnp.float32, jnp.bfloat16

    island = lax.axis_index("island")
    shard = lax.axis_index("fsdp")
    core = lax.rem(shard, 2)
    chip = shard // 2
    side = lax.rem(island, 2)
    level = island // 2
    inside = level * (3 - level) // 2

    partner = (island, chip * 2 + 1 - core)

    def across(c):
        return (island, (1 - chip) * 2 + c)

    def beside(c):
        return (island + 1 - 2 * side, chip * 2 + c)

    pair = ((level + 1 - 2 * lax.rem(level, 2)) * 2 + side, shard)
    middle = ((3 - level) * 2 + side, shard)

    offsets = [sum(splits[:i]) for i in range(len(splits))]

    def block(c, i):
        return pl.ds(2 * offsets[i] + c * splits[i], splits[i])

    def both(i):
        return pl.ds(2 * offsets[i], 2 * splits[i])

    def source(i):
        return pl.ds(offsets[i], splits[i])

    def lanes(start, extent):
        return pl.ds(pl.multiple_of(start, rows), extent)

    my_lanes = lanes(chip * 2 * rows, 2 * rows)
    core_rows = core * rows

    barrier = pltpu.get_barrier_semaphore()

    def greet(target):
        pl.semaphore_signal(barrier, inc=1, device_id=target, device_id_type=MESH)

    greet(partner)
    greet(beside(1))

    @pl.when(chip == 0)
    def _():
        greet(across(0))

    @pl.when((core == 0) & (chip == 0))
    def _():
        greet(across(1))

    @pl.when(core == 1)
    def _():
        greet(beside(0))
        greet(pair)

    @pl.when((core == 1) & (inside == 1))
    def _():
        greet(middle)

    tokens = []
    wload = pltpu.make_async_copy(
        w_hbm, wc.at[pl.ds(pl.multiple_of(core_rows, rows), rows)], load_sem.at[0])
    wload.start()
    for i in range(len(splits)):
        place = pl.ds(pl.multiple_of(2 * offsets[i] + core * splits[i], splits[i]), splits[i])
        tokens.append(pltpu.make_async_copy(
            x_hbm.at[source(i), my_lanes], xc.at[place], load_sem.at[1]))
        tokens.append(pltpu.make_async_copy(
            cot_hbm.at[source(i)], cot.at[place], load_sem.at[2]))
    for load in tokens:
        load.start()

    pl.semaphore_wait(barrier, 4 + core * (1 + inside) - (1 - chip) * (2 - core))

    @pl.when((core == 0) & (chip == 1))
    def _():
        for c in range(2):
            pl.semaphore_signal(ready, inc=1, device_id=across(c), device_id_type=MESH)

    def reach_across():
        @pl.when(chip == 0)
        def _():
            pl.semaphore_wait(ready, 1)

    def remote(src, dst, kind, into, target):
        return pltpu.make_async_remote_copy(
            src_ref=src, dst_ref=dst, send_sem=sent.at[kind], recv_sem=into,
            device_id=target, device_id_type=MESH)

    def all_tokens(ref):
        return ref.at[pl.ds(0, token_count)]

    def tokens_loaded():
        for ref, dst, index in ((x_hbm.at[:, my_lanes], xc, 1), (cot_hbm, cot, 2)):
            pltpu.make_async_copy(ref, all_tokens(dst), load_sem.at[index]).wait()

    def kept(j):
        return pl.multiple_of(side * half + begins[j], 16)

    def given(j):
        return pl.multiple_of((1 - side) * half + begins[j], 16)

    def kept_rows(j):
        return pl.ds(kept(j), pieces[j])

    def given_rows(j):
        return pl.ds(given(j), pieces[j])

    def slot(k):
        return pl.ds(2 * begins[k // 2] + (k % 2) * pieces[k // 2], pieces[k // 2])

    group = len(pieces)
    parts = len(splits)

    def scatter_send(c, j):
        k = 2 * j + c
        return remote(w_hbm.at[given_rows(j)], rsin.at[slot(k)], 0, first.at[k], beside(1))

    def scatter_total():
        return remote(
            w_hbm.at[pl.ds(0, half)], rsin.at[pl.ds(0, half)], 0, first.at[0], beside(1))

    def token_send(c, i):
        return remote(
            x_hbm.at[source(i), lanes((1 - chip) * 2 * rows, 2 * rows)],
            xin.at[block(c, i)], 1, first.at[group + 2 * i + c], across(0))

    def token_total():
        return remote(
            x_hbm.at[:, lanes((1 - chip) * 2 * rows, 2 * rows)],
            all_tokens(xin), 1, first.at[group], across(0))

    def keep_send(j):
        extent = pieces[j] if j < 2 else half - begins[j]
        place = pl.ds(kept(j), extent)
        return remote(w_hbm.at[place], wc.at[place], 2, kept_sem.at[j], partner)

    def keep_total():
        return remote(
            w_hbm.at[pl.ds(0, half)], wc.at[pl.ds(0, half)], 2, kept_sem.at[0], partner)

    weight_send = remote(w_hbm, wc.at[pl.ds(rows, rows)], 2, cross.at[0], partner)

    def own_tokens_up(i):
        return remote(
            x_hbm.at[source(i), lanes((chip * 2 + 1) * rows, rows)],
            xc.at[block(0, i), pl.ds(rows, rows)], 3, passed.at[0], partner)

    def own_tokens_up_total():
        return remote(
            x_hbm.at[:, lanes((chip * 2 + 1) * rows, rows)],
            xc.at[pl.ds(0, token_count), pl.ds(rows, rows)], 3, passed.at[0], partner)

    def own_tokens_down(i):
        return remote(
            x_hbm.at[source(i), my_lanes], xc.at[block(1, i)], 3, passed.at[0], partner)

    def own_tokens_down_total():
        return remote(x_hbm.at[:, my_lanes], all_tokens(xc), 3, passed.at[0], partner)

    def cotangent_down(i):
        return remote(cot_hbm.at[source(i)], cot.at[block(1, i)], 4, passed.at[1], partner)

    def cotangent_total():
        return remote(cot_hbm, all_tokens(cot), 4, passed.at[1], partner)

    def tokens_forward(place):
        part = xin.at[place, pl.ds(rows, rows)]
        return remote(part, part, 4, passed.at[1], partner)

    def partial_send(place, i):
        return remote(psend.at[place], precv.at[place], 5, rail.at[i], across(0))

    def upstream_across(place, i):
        return remote(kg.at[place], kgin.at[place], 6, rail.at[parts + i], across(0))

    def upstream_down(place):
        return remote(kg.at[place], kg.at[place], 7, passed.at[2], partner)

    def upstream_forward(place):
        return remote(kgin.at[place], kgin.at[place], 8, passed.at[3], partner)

    def gather_send(k):
        return remote(
            res.at[slot(k)], mean.at[kept_rows(k // 2)], 5, gathered.at[k // 2], beside(k % 2))

    def gather_total():
        return remote(res, mean, 5, gathered.at[0], beside(0))

    def gather_recv(j):
        return remote(
            res.at[slot(2 * j)], mean.at[given_rows(j)], 5, gathered.at[j], beside(0))

    def deliver_send(j):
        return remote(res.at[slot(2 * j)], mean.at[kept_rows(j)], 6, first.at[j], partner)

    def deliver_total():
        return remote(
            res.at[pl.ds(0, half)], mean.at[pl.ds(0, half)], 6, first.at[0], partner)

    def outer_send(k):
        return remote(pout.at[slot(k)], pin.at[slot(k)], 7, rail.at[k], pair)

    def middle_send(k):
        return remote(pout.at[slot(k)], qin.at[slot(k)], 7, cross.at[k], middle)

    def part_total():
        return remote(pout, pin, 7, rail.at[0], pair)

    def result_send(k):
        return remote(res.at[slot(k)], res.at[slot(k)], 8, rail.at[k], pair)

    def result_total():
        return remote(res, res, 8, rail.at[0], pair)

    state_loads = [
        pltpu.make_async_copy(place, dst, load_sem.at[3 + index])
        for index, (place, dst) in enumerate((
            (m_hbm, m), (s_hbm, s), (gw_hbm, gw), (om_hbm, om),
            (w_hbm.at[pl.ds(rows - late.shape[0], late.shape[0])], late)))
    ]

    def turn(out, tokens_by_width, base, start, tile):
        columns = pl.ds(pl.multiple_of(base + start, tile), tile)
        out[pl.ds(start, tile), :] = tokens_by_width[:, columns].T

    def turn_all(out, tokens_by_width, base):
        tile = min(256, rows)

        @pl.loop(0, rows // tile)
        def _(t):
            turn(out, tokens_by_width, base, pl.multiple_of(t * tile, tile), tile)

    def own_gradient():
        tile = min(256, rows)

        @pl.loop(0, rows // tile)
        def _(t):
            place = pl.ds(pl.multiple_of(t * tile, tile), tile)
            grad[place, :] = jnp.dot(xct[place, :], kg[...], preferred_element_type=f32)

    def gradient_tile(base, start, tile):
        place = pl.ds(start, tile)
        grad[place, :] += jnp.dot(xint[place, :], kgin[...], preferred_element_type=f32)
        if start >= nf.shape[0]:
            return
        step = min(32, tile)

        @pl.loop(0, tile // step)
        def _(u):
            place = pl.ds(pl.multiple_of(start + u * step, step), step)
            current = wc[pl.ds(pl.multiple_of(base + start + u * step, step), step), :]
            first_new, second_new, inner = inner_step(
                grad[place, :], m[place, :], s[place, :], current)
            nf[place, :] = first_new
            ns[place, :] = second_new
            half_inner[place, :] = inner

    def inner_update(base):
        tile = min(256, rows)
        for t in range(rows // tile):
            gradient_tile(base, t * tile, tile)

    def matmul(out, place, left, convert):
        part = min(256, width)

        @pl.loop(0, width // part)
        def _(n):
            columns = pl.ds(pl.multiple_of(n * part, part), part)
            value = jnp.dot(left[...], wc[:, columns], preferred_element_type=f32)
            out[place, columns] = value.astype(bf16) if convert else value

    steps = range(len(splits))

    every = slice(None)

    @pl.when(core == 0)
    def _():
        for j in groups:
            scatter_send(0, j).start()
            if j < 3:
                keep_send(j).start()
        for i in steps:
            own_tokens_up(i).start()
        for load in state_loads:
            load.start()
        reach_across()
        for i in steps[:2]:
            token_send(0, i).start()
        wload.wait()
        tokens_loaded()
        weight_send.wait_recv()
        own_tokens_down_total().wait_recv()
        matmul(own, every, xc, False)
        turn_all(xct, xc, 0)
        for i in steps:
            token_send(0, i).wait_recv()
            token_send(1, i).wait_recv()
            tokens_forward(both(i)).start()
            matmul(psend, both(i), xin.at[both(i)], True)
            partial_send(both(i), i).start()
            if i == 0:
                for later in steps[2:]:
                    token_send(0, later).start()
        cotangent_total().wait_recv()
        for i in steps:
            partial_send(both(i), i).wait_recv()
            for head in range(width // HEAD_DIM):
                columns = slice(head * HEAD_DIM, (head + 1) * HEAD_DIM)
                keys = (own[both(i), columns] + precv[both(i), columns].astype(f32)) * scale
                kg[both(i), columns] = head_backward(
                    keys, cot[both(i), columns].astype(f32), scale)
            upstream_across(both(i), i).start()
            upstream_down(both(i)).start()
        own_gradient()
        turn_all(xint, xin, 0)
        for i in steps:
            upstream_across(both(i), i).wait_recv()
            upstream_forward(both(i)).start()
        for load in state_loads:
            load.wait()
        inner_update(0)
        for j in groups:
            deliver_send(j).wait_recv()
            gather_recv(j).wait_recv()
        for total in (scatter_total(), token_total(), keep_total(), own_tokens_up_total(),
                      tokens_forward(every), partial_send(every, 0), upstream_across(every, 0),
                      upstream_down(every), upstream_forward(every)):
            total.wait_send()

    @pl.when(core == 1)
    def _():
        def held(k):
            j = k // 2
            place = pl.ds(pl.multiple_of((k % 2) * rows + kept(j), 16), pieces[j])
            return wc[place, :].astype(f32) + rsin[slot(k), :].astype(f32)

        def hand_out(k):
            gather_send(k).start()
            j = k // 2
            if k % 2:
                mean[kept_rows(j), :] = res[slot(k), :]
            else:
                deliver_send(j).start()

        for j in groups:
            scatter_send(1, j).start()
        weight_send.start()
        for i in steps:
            own_tokens_down(i).start()
            cotangent_down(i).start()
        for load in state_loads:
            load.start()
        reach_across()
        for i in steps:
            token_send(1, i).start()
        wload.wait()

        def arrived(k):
            scatter_send(k % 2, k // 2).wait_recv()
            if k % 2 == 0 and k < 6:
                keep_send(k // 2).wait_recv()

        def outer_part(k):
            arrived(k)
            pout[slot(k), :] = held(k).astype(bf16)
            outer_send(k).start()

        def outer_result(k):
            result_send(k).wait_recv()
            hand_out(k)

        def middle_part(k):
            arrived(k)
            outer_send(k).wait_recv()
            pout[slot(k), :] = (held(k) + pin[slot(k), :].astype(f32)).astype(bf16)
            middle_send(k).start()

        def middle_result(k):
            middle_send(k).wait_recv()
            total = pout[slot(k), :].astype(f32) + qin[slot(k), :].astype(f32)
            res[slot(k), :] = (total / islands).astype(bf16)
            result_send(k).start()
            hand_out(k)

        tile = min(256, rows)
        tiles = rows // tile

        def own_tokens_ready():
            tokens_loaded()
            own_tokens_up_total().wait_recv()

        def gradient_start():
            upstream_down(every).wait_recv()
            own_gradient()

        def gradient_ready():
            upstream_forward(every).wait_recv()
            for load in state_loads:
                load.wait()

        ends = [2 * begins[k // 2] + (1 + k % 2) * pieces[k // 2] for k in range(count)]

        def interleave(first, second, lag, turn_at, own_at, tiles_at):
            unit = rows // 16
            work = []
            work.append((turn_at * unit, tokens_forward(every).wait_recv))
            for t in range(tiles):
                work.append(((turn_at + t) * unit, functools.partial(
                    turn, xint, xin, rows, t * tile, tile)))
            work.append((turn_at * unit, own_tokens_ready))
            for t in range(tiles):
                work.append(((turn_at + t) * unit, functools.partial(
                    turn, xct, xc, rows, t * tile, tile)))
            work.append((own_at * unit, gradient_start))
            work.append((tiles_at * unit, gradient_ready))
            for t in range(tiles):
                work.append(((tiles_at + t) * unit, functools.partial(
                    gradient_tile, rows, t * tile, tile)))
            done = 0
            for k in range(count + 1):
                if k < count:
                    first(k)
                limit = rows * 2 if k == count else ends[k] - lag * rows // 16
                while done < count and ends[done] <= limit:
                    second(done)
                    while work and work[0][0] <= ends[done]:
                        work.pop(0)[1]()
                    done += 1
            for item in work:
                item[1]()

        @pl.when(inside == 0)
        def _():
            interleave(outer_part, outer_result, 16, 14, 14, 16)

        @pl.when(inside == 1)
        def _():
            interleave(middle_part, middle_result, 4, 16, 16, 16)

        for j in groups:
            gather_recv(j).wait_recv()

        @pl.when(inside == 1)
        def _():
            result_total().wait_send()

        for total in (scatter_total(), token_total(), weight_send, own_tokens_down_total(),
                      cotangent_total(), gather_total(), deliver_total(), part_total()):
            total.wait_send()


def finish(first, second, half_inner, mean, gw, om, grad, m, s, late, nl, nf, ns, ng, nm, local,
           weights, momenta, first_late, second_late, sems):
    rows = mean.shape[0]
    early = first.shape[0]
    tile = min(128, early)
    step = min(32, tile)
    f32 = jnp.float32
    begin = pl.ds(0, early)
    rest = pl.ds(early, rows - early)
    pltpu.make_async_copy(first, nf.at[begin], sems.at[0]).start()
    pltpu.make_async_copy(second, ns.at[begin], sems.at[1]).start()
    for t in range(rows // tile):
        after = t * tile - early

        @pl.loop(0, tile // step)
        def _(u):
            place = pl.ds(pl.multiple_of(t * tile + u * step, step), step)
            if after < 0:
                inner = half_inner[place, :]
            else:
                behind = pl.ds(pl.multiple_of(after + u * step, step), step)
                first_new, second_new, inner = inner_step(
                    grad[place, :], m[place, :], s[place, :], late[behind, :])
                first_late[behind, :] = first_new
                second_late[behind, :] = second_new
            current = gw[place, :]
            outer_grad = current - mean[place, :].astype(f32)
            momentum = outer_beta * om[place, :] + outer_grad
            updated = current - outer_rate * (outer_grad + outer_beta * momentum)
            momenta[place, :] = momentum
            weights[place, :] = updated
            local[place, :] = (inner + (1.0 - merge_weight) * updated).astype(jnp.bfloat16)

        part = pl.ds(t * tile, tile)
        if after >= 0:
            behind = pl.ds(after, tile)
            pltpu.make_async_copy(first_late.at[behind], nf.at[part], sems.at[5]).start()
            pltpu.make_async_copy(second_late.at[behind], ns.at[part], sems.at[6]).start()
        pltpu.make_async_copy(local.at[part], nl.at[part], sems.at[2]).start()
        pltpu.make_async_copy(weights.at[part], ng.at[part], sems.at[3]).start()
        pltpu.make_async_copy(momenta.at[part], nm.at[part], sems.at[4]).start()
    pltpu.make_async_copy(first, nf.at[begin], sems.at[0]).wait()
    pltpu.make_async_copy(second, ns.at[begin], sems.at[1]).wait()
    pltpu.make_async_copy(local, nl, sems.at[2]).wait()
    pltpu.make_async_copy(weights, ng, sems.at[3]).wait()
    pltpu.make_async_copy(momenta, nm, sems.at[4]).wait()
    pltpu.make_async_copy(first_late, nf.at[rest], sems.at[5]).wait()
    pltpu.make_async_copy(second_late, ns.at[rest], sems.at[6]).wait()


def fused(pieces, local_weights, adam_first, adam_second, global_weights, outer_momentum, inputs,
          key_cotangent):
    arrays = (local_weights[0], adam_first[0], adam_second[0], global_weights, outer_momentum,
              inputs[0], key_cotangent[0])
    rows, width = arrays[0].shape
    count, depth = arrays[5].shape
    islands = lax.axis_size("island")
    splits = token_splits(count)
    groups = len(pieces)
    bf16, f32 = jnp.bfloat16, jnp.float32
    dma, vmem = pltpu.SemaphoreType.DMA, pltpu.VMEM
    narrow = jax.ShapeDtypeStruct((rows, width), bf16)
    wide = jax.ShapeDtypeStruct((rows, width), f32)
    early = rows // 2
    part = jax.ShapeDtypeStruct((early, width), bf16)
    carried = [part, part, jax.ShapeDtypeStruct((early, width), f32), narrow, wide, wide, wide,
               narrow, narrow, jax.ShapeDtypeStruct((rows - early, width), bf16)]
    out_shape = [narrow] * 3 + [wide] * 2
    steps = len(splits)
    scratch = [
        vmem((2 * rows, width), bf16),
        vmem((2 * count, 2 * rows), bf16),
        vmem((2 * count, 2 * rows), bf16),
        vmem((2 * count, width), bf16),
        vmem((2 * count, width), f32),
        vmem((2 * count, width), bf16),
        vmem((2 * count, width), bf16),
        vmem((2 * count, width), bf16),
        vmem((2 * count, width), bf16),
        vmem((rows, 2 * count), bf16),
        vmem((rows, 2 * count), bf16),
    ] + [vmem((rows, width), bf16)] * 5 + [
        dma((8,)),
        dma((9,)),
        dma((max(2 * groups, groups + 2 * steps),)),
        dma((max(2 * groups, 2 * steps),)),
        dma((2 * groups,)),
        dma((groups,)),
        dma((min(groups, 3),)),
        dma((4,)),
        pltpu.SemaphoreType.REGULAR,
    ]
    in_vmem = pl.BlockSpec(memory_space=pltpu.VMEM)
    in_hbm = pl.BlockSpec(memory_space=pltpu.HBM)
    results = pl.pallas_call(
        functools.partial(window, islands, pieces, splits, float(depth) ** (-0.5)),
        out_shape=carried,
        in_specs=[in_hbm] * len(arrays),
        out_specs=[in_vmem] * len(carried),
        scratch_shapes=scratch,
        compiler_params=pltpu.CompilerParams(
            collective_id=0, has_side_effects=True, vmem_limit_bytes=40 * 1024 * 1024
        ),
    )(*(pltpu.with_memory_space_constraint(a, pltpu.HBM) for a in arrays))
    written = pl.pallas_call(
        finish,
        out_shape=out_shape,
        in_specs=[in_vmem] * len(carried),
        out_specs=[in_hbm] * len(out_shape),
        scratch_shapes=[
            vmem((rows, width), bf16),
            vmem((rows, width), f32),
            vmem((rows, width), f32),
            vmem((rows - early, width), bf16),
            vmem((rows - early, width), bf16),
            dma((7,)),
        ],
        compiler_params=pltpu.CompilerParams(vmem_limit_bytes=8 * 1024 * 1024),
    )(*results)
    return tuple(a[None] for a in written[:3]) + tuple(written[3:])


def local(
    local_weights, adam_first, adam_second, global_weights, outer_momentum, inputs, key_cotangent
):
    weights = local_weights[0]
    tokens = inputs[0]
    rows, width = weights.shape
    count, depth = tokens.shape
    scale = float(depth) ** (-0.5)
    islands, shards = lax.axis_size("island"), lax.axis_size("fsdp")
    chips = shards // 2
    others = max(chips - 1, 1)
    pieces = pieces_of(rows, islands, shards)
    if pieces and width % HEAD_DIM == 0:
        return fused(pieces, local_weights, adam_first, adam_second, global_weights,
                     outer_momentum, inputs, key_cotangent)
    chunks = chunk_count(rows, islands)
    bf16, f32 = jnp.bfloat16, jnp.float32
    dma = pltpu.SemaphoreType.DMA
    out_shape = [jax.ShapeDtypeStruct((rows, width), f32)]
    scratch = [
        pltpu.VMEM((rows, width), bf16),
        pltpu.VMEM((count, depth), bf16),
        pltpu.VMEM((count, width), bf16),
        dma((3,)),
        pltpu.VMEM((rows, width), bf16),
        pltpu.VMEM((others, count, 2 * rows), bf16),
        pltpu.VMEM((chips, count, rows), bf16),
        pltpu.VMEM((others, count, width), bf16),
        pltpu.VMEM((others, count, width), bf16),
        pltpu.VMEM((others, count, width), bf16),
        pltpu.VMEM((chips, count, width), bf16),
        pltpu.VMEM((count, width), bf16),
        pltpu.VMEM((count, width), f32),
        dma((2, others)),
        dma((2, others)),
        dma((2, others)),
        dma((2, chips + 1)),
        dma((2, chips)),
    ]
    if chunks:
        levels = islands.bit_length() - 1
        out_shape.append(jax.ShapeDtypeStruct((rows, width), bf16))
        scratch += [
            pltpu.VMEM((chunks, rows // chunks, width), bf16),
            pltpu.VMEM((rows, width), bf16),
            pltpu.VMEM((rows, width), bf16),
            dma((2, chunks, 2 * levels)),
        ]
    vmem = pl.BlockSpec(memory_space=pltpu.VMEM)
    results = pl.pallas_call(
        functools.partial(exchange, islands, shards, chunks, scale),
        out_shape=out_shape,
        in_specs=[pl.BlockSpec(memory_space=pltpu.HBM)] * 3,
        out_specs=[vmem] * len(out_shape),
        scratch_shapes=scratch,
        compiler_params=pltpu.CompilerParams(
            collective_id=0, has_side_effects=True, vmem_limit_bytes=40 * 1024 * 1024
        ),
    )(*(pltpu.with_memory_space_constraint(a, pltpu.HBM) for a in (weights, tokens, key_cotangent[0])))
    gradient = results[0]
    if chunks:
        mean_local = results[1].astype(jnp.float32)
    else:
        mean_local = lax.psum(weights.astype(jnp.float32), "island") / islands
    outer_grad = global_weights - mean_local
    new_momentum = outer_beta * outer_momentum + outer_grad
    new_global = global_weights - outer_rate * (outer_grad + outer_beta * new_momentum)
    first_new = beta_one * adam_first[0].astype(jnp.float32) + (1.0 - beta_one) * gradient
    second_new = (
        beta_two * adam_second[0].astype(jnp.float32) + (1.0 - beta_two) * gradient * gradient
    )
    current = weights.astype(jnp.float32)
    inner = current - inner_rate * (
        first_new / (jnp.sqrt(second_new) + adam_epsilon) + weight_decay * current
    )
    merged = merge_weight * inner + (1.0 - merge_weight) * new_global
    return (
        merged.astype(jnp.bfloat16)[None],
        first_new.astype(jnp.bfloat16)[None],
        second_new.astype(jnp.bfloat16)[None],
        new_global,
        new_momentum,
    )


def solution(mesh):
    placed = (
        P("island", "fsdp", None),
        P("island", "fsdp", None),
        P("island", "fsdp", None),
        P("fsdp", None),
        P("fsdp", None),
        P("island", "fsdp", None),
        P("island", "fsdp", None),
    )
    return jax.shard_map(
        local,
        mesh=mesh,
        in_specs=placed,
        out_specs=(
            P("island", "fsdp", None),
            P("island", "fsdp", None),
            P("island", "fsdp", None),
            P("fsdp", None),
            P("fsdp", None),
        ),
        check_vma=False,
    )
```

```python
import functools

import jax
import jax.numpy as jnp
from jax import lax
from jax.experimental import pallas as pl
from jax.experimental.pallas import tpu as pltpu
from jax.sharding import PartitionSpec as P

HEAD_DIM = 128
MESH = pl.DeviceIdType.MESH

beta_one = 0.9
beta_two = 0.95
inner_rate = 0.02
weight_decay = 0.1
adam_epsilon = 1e-08
norm_epsilon = 1e-06
outer_rate = 0.7
outer_beta = 0.9
merge_weight = 0.5


def chunk_count(rows, islands):
    for chunks in (8, 4, 2, 1):
        if islands & (islands - 1) == 0 and rows % (islands * chunks * 16) == 0:
            return chunks
    return 0


def head_backward(keys, upstream, scale):
    squares = jnp.mean(keys * keys, axis=-1, keepdims=True)
    inverse = lax.rsqrt(squares + norm_epsilon)
    normed = keys * inverse
    projected = jnp.mean(upstream * normed, axis=-1, keepdims=True)
    return (inverse * (upstream - normed * projected) * scale).astype(jnp.bfloat16)


def exchange(islands, shards, chunks, scale, *refs):
    w_hbm, x_hbm, cot_hbm = refs[:3]
    if chunks:
        (grad, mean, w, x, cot, lsem, wp, xin, xp, psend, precv, kgin, kgp, kg, own,
         ysem, psem, ksem, csem, fsem, landed, part, gathered, hsem) = refs[3:]
    else:
        (grad, w, x, cot, lsem, wp, xin, xp, psend, precv, kgin, kgp, kg, own,
         ysem, psem, ksem, csem, fsem) = refs[3:]
    rows, width = w.shape
    chips = shards // 2
    island = lax.axis_index("island")
    shard = lax.axis_index("fsdp")
    core = lax.rem(shard, 2)
    chip = shard // 2
    partner = (island, chip * 2 + 1 - core)

    def peer(step):
        return (island, lax.rem(chip + step, chips) * 2 + core)

    def back(step):
        return (island, lax.rem(chip + chips - step, chips) * 2 + core)

    targets = [partner] + [peer(step) for step in range(1, chips)]
    if chunks:
        levels = islands.bit_length() - 1
        sides = [lax.rem(island // 2**bit, 2) for bit in range(levels)]
        mates = [(island + (1 - 2 * sides[bit]) * 2**bit, shard) for bit in range(levels)]
        targets += mates

    loads = [
        pltpu.make_async_copy(source, place, lsem.at[index])
        for index, (source, place) in enumerate(((w_hbm, w), (x_hbm, x), (cot_hbm, cot)))
    ]
    for load in loads:
        load.start()

    barrier = pltpu.get_barrier_semaphore()
    for target in targets:
        pl.semaphore_signal(barrier, inc=1, device_id=target, device_id_type=MESH)
    pl.semaphore_wait(barrier, len(targets))

    def remote(src, dst, sems, where, target):
        return pltpu.make_async_remote_copy(
            src_ref=src,
            dst_ref=dst,
            send_sem=sems.at[(0,) + where],
            recv_sem=sems.at[(1,) + where],
            device_id=target,
            device_id_type=MESH,
        )

    def columns(start):
        return pl.ds(pl.multiple_of(start, rows), rows)

    copies = []

    def begin(copy):
        copy.start()
        copies.append(copy)
        return copy

    y1 = []
    for step in range(1, chips):
        there = lax.rem(chip + step, chips)
        y1.append(begin(remote(
            x_hbm.at[:, pl.ds(pl.multiple_of(there * 2 * rows, 2 * rows), 2 * rows)],
            xin.at[step - 1], ysem, (step - 1,), peer(step))))
    halves, returns = {}, {}
    if chunks:
        span = rows // chunks
        orders = [
            [1, 0] + list(range(2, levels)) if levels > 1 and q % 2 == 1 else list(range(levels))
            for q in range(chunks)
        ]
        starts = []
        for q in range(chunks):
            begins = [q * span]
            for level, bit in enumerate(orders[q]):
                begins.append(begins[level] + sides[bit] * (span >> (level + 1)))
            starts.append(begins)

    def segment(q, level):
        return pl.ds(pl.multiple_of(starts[q][level], span >> level), span >> level)

    def landing(level):
        return pl.ds(span - (span >> level), span >> (level + 1))

    def send_half(q, level):
        bit, size = orders[q][level], span >> (level + 1)
        away = starts[q][level] + (1 - sides[bit]) * size
        source = part if level else w_hbm
        halves[q, level] = begin(remote(
            source.at[pl.ds(pl.multiple_of(away, size), size)],
            landed.at[q, landing(level)], hsem, (q, level), mates[bit]))

    def send_back(q, level):
        place = segment(q, level + 1)
        returns[q, level] = begin(remote(
            gathered.at[place], gathered.at[place], hsem, (q, levels + level),
            mates[orders[q][level]]))

    for q in range(chunks):
        send_half(q, 0)
    wcopy = begin(remote(w_hbm, wp, csem, (0,), partner))
    xcopy = [begin(remote(
        x_hbm.at[:, columns((chip * 2 + 1 - core) * rows)], xp.at[0], csem, (1,), partner))]

    def step_of(q, stage):
        if stage < levels:
            halves[q, stage].wait_recv()
            place = segment(q, stage + 1)
            held = (part if stage else w)[place, :].astype(jnp.float32)
            total = held + landed[q, landing(stage), :].astype(jnp.float32)
            if stage + 1 < levels:
                part[place, :] = total.astype(jnp.bfloat16)
                send_half(q, stage + 1)
            else:
                gathered[place, :] = (total / islands).astype(jnp.bfloat16)
                send_back(q, levels - 1)
        else:
            level = 2 * levels - 1 - stage
            returns[q, level].wait_recv()
            if level:
                send_back(q, level - 1)

    def product(left, right):
        return jnp.dot(left, right, preferred_element_type=jnp.float32)

    stages = []
    for q in range(chunks):
        for stage in range(2 * levels):
            late = (q // 2) * 6.0 / chunks
            stages.append((stage + late, q, stage))
    stages.sort()

    def advance(until):
        while stages and stages[0][0] <= until:
            step_of(*stages.pop(0)[1:])

    for load in loads:
        load.wait()
    advance(0.5)
    wcopy.wait_recv()
    own[...] = product(x[:, columns(shard * rows)], w[...]) + product(
        x[:, columns((chip * 2 + 1 - core) * rows)], wp[...])
    advance(3.3)

    y3 = []
    for step in range(1, chips):
        y1[step - 1].wait_recv()
        xcopy.append(begin(remote(
            xin.at[step - 1, :, columns((1 - core) * rows)], xp.at[step], csem, (step + 1,), partner)))
        psend[step - 1] = (product(xin[step - 1, :, columns(core * rows)], w[...]) + product(
            xin[step - 1, :, columns((1 - core) * rows)], wp[...])).astype(jnp.bfloat16)
        y3.append(begin(remote(
            psend.at[step - 1], precv.at[step - 1], psem, (step - 1,), back(step))))
    advance(5.1)

    keys = own[...]
    for step in range(1, chips):
        y3[step - 1].wait_recv()
        keys += precv[step - 1].astype(jnp.float32)
    keys = keys * scale
    for head in range(width // HEAD_DIM):
        lanes = slice(head * HEAD_DIM, (head + 1) * HEAD_DIM)
        kg[:, lanes] = head_backward(keys[:, lanes], cot[:, lanes].astype(jnp.float32), scale)
    y4 = [
        begin(remote(kg, kgin.at[step - 1], ksem, (step - 1,), peer(step)))
        for step in range(1, chips)
    ]
    forwards = [begin(remote(kg, kgp.at[0], fsem, (0,), partner))]

    tile = min(256, rows)

    def add_block(read, upstream, first=False):
        @pl.loop(0, rows // tile)
        def _(t):
            start = pl.multiple_of(t * tile, tile)
            term = lax.dot_general(
                read(start), upstream[...], (((0,), (0,)), ((), ())),
                preferred_element_type=jnp.float32,
            ).astype(jnp.bfloat16).astype(jnp.float32)
            place = pl.ds(start, tile)
            grad[place, :] = term if first else grad[place, :] + term

    def lane(base):
        def at(start):
            return pl.ds(pl.multiple_of(base + start, tile), tile)
        return at

    mine = lane(shard * rows)
    add_block(lambda start: x[:, mine(start)], kg, first=True)
    forwards[0].wait_recv()
    xcopy[0].wait_recv()
    add_block(lambda start: xp[0, :, pl.ds(start, tile)], kgp.at[0])
    advance(6.4)
    inner = lane(core * rows)
    for step in range(1, chips):
        y4[step - 1].wait_recv()
        forwards.append(begin(remote(
            kgin.at[step - 1], kgp.at[step], fsem, (step,), partner)))
        add_block(lambda start: xin[step - 1, :, inner(start)], kgin.at[step - 1])
    advance(6.9)
    for step in range(1, chips):
        xcopy[step].wait_recv()
        forwards[step].wait_recv()
        add_block(lambda start: xp[step, :, pl.ds(start, tile)], kgp.at[step])
    advance(1000)
    if chunks:
        mean[...] = gathered[...]
    for copy in copies:
        copy.wait_send()


def token_splits(count):
    if count % 64 == 0:
        return (count // 2, count // 4, count // 4)
    return (count,)


def pieces_of(rows, islands, shards):
    if shards != 4 or islands != 2 * shards:
        return ()
    for grades in ((1,) * 8, (1,) * 4, (1,)):
        unit, rest = divmod(rows // 2, sum(grades))
        if rest == 0 and unit % 16 == 0:
            return tuple(unit * grade for grade in grades)
    return ()


def inner_step(gradient, first, second, current):
    first_new = beta_one * first.astype(jnp.float32) + (1.0 - beta_one) * gradient
    second_new = beta_two * second.astype(jnp.float32) + (1.0 - beta_two) * gradient * gradient
    current = current.astype(jnp.float32)
    inner = current - inner_rate * (
        first_new / (jnp.sqrt(second_new) + adam_epsilon) + weight_decay * current)
    return first_new.astype(jnp.bfloat16), second_new.astype(jnp.bfloat16), merge_weight * inner


def window(islands, pieces, splits, scale, *refs):
    w_hbm, m_hbm, s_hbm, gw_hbm, om_hbm, x_hbm, cot_hbm = refs[:7]
    nf, ns, half_inner, mean, gw, om, grad, m, s, late = refs[7:17]
    (wc, xc, xin, cot, own, psend, precv, kg, kgin, xct, xint,
     rsin, pin, qin, pout, res,
     load_sem, sent, first, rail, cross, gathered, kept_sem, passed, ready) = refs[17:]
    rows, width = mean.shape
    half = rows // 2
    groups = range(len(pieces))
    token_count = x_hbm.shape[0]
    count = 2 * len(pieces)
    begins = [sum(pieces[:j]) for j in groups]
    f32, bf16 = jnp.float32, jnp.bfloat16

    island = lax.axis_index("island")
    shard = lax.axis_index("fsdp")
    core = lax.rem(shard, 2)
    chip = shard // 2
    side = lax.rem(island, 2)
    level = island // 2
    inside = level * (3 - level) // 2

    partner = (island, chip * 2 + 1 - core)

    def across(c):
        return (island, (1 - chip) * 2 + c)

    def beside(c):
        return (island + 1 - 2 * side, chip * 2 + c)

    pair = ((level + 1 - 2 * lax.rem(level, 2)) * 2 + side, shard)
    middle = ((3 - level) * 2 + side, shard)

    offsets = [sum(splits[:i]) for i in range(len(splits))]

    def block(c, i):
        return pl.ds(2 * offsets[i] + c * splits[i], splits[i])

    def both(i):
        return pl.ds(2 * offsets[i], 2 * splits[i])

    def source(i):
        return pl.ds(offsets[i], splits[i])

    def lanes(start, extent):
        return pl.ds(pl.multiple_of(start, rows), extent)

    my_lanes = lanes(chip * 2 * rows, 2 * rows)
    core_rows = core * rows

    barrier = pltpu.get_barrier_semaphore()

    def greet(target):
        pl.semaphore_signal(barrier, inc=1, device_id=target, device_id_type=MESH)

    greet(partner)
    greet(beside(1))

    @pl.when(chip == 0)
    def _():
        greet(across(0))

    @pl.when((core == 0) & (chip == 0))
    def _():
        greet(across(1))

    @pl.when(core == 1)
    def _():
        greet(beside(0))
        greet(pair)

    @pl.when((core == 1) & (inside == 1))
    def _():
        greet(middle)

    tokens = []
    wload = pltpu.make_async_copy(
        w_hbm, wc.at[pl.ds(pl.multiple_of(core_rows, rows), rows)], load_sem.at[0])
    wload.start()
    for i in range(len(splits)):
        place = pl.ds(pl.multiple_of(2 * offsets[i] + core * splits[i], splits[i]), splits[i])
        tokens.append(pltpu.make_async_copy(
            x_hbm.at[source(i), my_lanes], xc.at[place], load_sem.at[1]))
        tokens.append(pltpu.make_async_copy(
            cot_hbm.at[source(i)], cot.at[place], load_sem.at[2]))
    for load in tokens:
        load.start()

    pl.semaphore_wait(barrier, 4 + core * (1 + inside) - (1 - chip) * (2 - core))

    @pl.when((core == 0) & (chip == 1))
    def _():
        for c in range(2):
            pl.semaphore_signal(ready, inc=1, device_id=across(c), device_id_type=MESH)

    def reach_across():
        @pl.when(chip == 0)
        def _():
            pl.semaphore_wait(ready, 1)

    def remote(src, dst, kind, into, target):
        return pltpu.make_async_remote_copy(
            src_ref=src, dst_ref=dst, send_sem=sent.at[kind], recv_sem=into,
            device_id=target, device_id_type=MESH)

    def all_tokens(ref):
        return ref.at[pl.ds(0, token_count)]

    def tokens_loaded():
        for ref, dst, index in ((x_hbm.at[:, my_lanes], xc, 1), (cot_hbm, cot, 2)):
            pltpu.make_async_copy(ref, all_tokens(dst), load_sem.at[index]).wait()

    def kept(j):
        return pl.multiple_of(side * half + begins[j], 16)

    def given(j):
        return pl.multiple_of((1 - side) * half + begins[j], 16)

    def kept_rows(j):
        return pl.ds(kept(j), pieces[j])

    def given_rows(j):
        return pl.ds(given(j), pieces[j])

    def slot(k):
        return pl.ds(2 * begins[k // 2] + (k % 2) * pieces[k // 2], pieces[k // 2])

    group = len(pieces)
    parts = len(splits)

    def scatter_send(c, j):
        k = 2 * j + c
        return remote(w_hbm.at[given_rows(j)], rsin.at[slot(k)], 0, first.at[k], beside(1))

    def scatter_total():
        return remote(
            w_hbm.at[pl.ds(0, half)], rsin.at[pl.ds(0, half)], 0, first.at[0], beside(1))

    def token_send(c, i):
        return remote(
            x_hbm.at[source(i), lanes((1 - chip) * 2 * rows, 2 * rows)],
            xin.at[block(c, i)], 1, first.at[group + 2 * i + c], across(0))

    def token_total():
        return remote(
            x_hbm.at[:, lanes((1 - chip) * 2 * rows, 2 * rows)],
            all_tokens(xin), 1, first.at[group], across(0))

    def keep_send(j):
        extent = pieces[j] if j < 2 else half - begins[j]
        place = pl.ds(kept(j), extent)
        return remote(w_hbm.at[place], wc.at[place], 2, kept_sem.at[j], partner)

    def keep_total():
        return remote(
            w_hbm.at[pl.ds(0, half)], wc.at[pl.ds(0, half)], 2, kept_sem.at[0], partner)

    weight_send = remote(w_hbm, wc.at[pl.ds(rows, rows)], 2, cross.at[0], partner)

    def own_tokens_up(i):
        return remote(
            x_hbm.at[source(i), lanes((chip * 2 + 1) * rows, rows)],
            xc.at[block(0, i), pl.ds(rows, rows)], 3, passed.at[0], partner)

    def own_tokens_up_total():
        return remote(
            x_hbm.at[:, lanes((chip * 2 + 1) * rows, rows)],
            xc.at[pl.ds(0, token_count), pl.ds(rows, rows)], 3, passed.at[0], partner)

    def own_tokens_down(i):
        return remote(
            x_hbm.at[source(i), my_lanes], xc.at[block(1, i)], 3, passed.at[0], partner)

    def own_tokens_down_total():
        return remote(x_hbm.at[:, my_lanes], all_tokens(xc), 3, passed.at[0], partner)

    def cotangent_down(i):
        return remote(cot_hbm.at[source(i)], cot.at[block(1, i)], 4, passed.at[1], partner)

    def cotangent_total():
        return remote(cot_hbm, all_tokens(cot), 4, passed.at[1], partner)

    def tokens_forward(place):
        part = xin.at[place, pl.ds(rows, rows)]
        return remote(part, part, 4, passed.at[1], partner)

    def partial_send(place, i):
        return remote(psend.at[place], precv.at[place], 5, rail.at[i], across(0))

    def upstream_across(place, i):
        return remote(kg.at[place], kgin.at[place], 6, rail.at[parts + i], across(0))

    def upstream_down(place):
        return remote(kg.at[place], kg.at[place], 7, passed.at[2], partner)

    def upstream_forward(place):
        return remote(kgin.at[place], kgin.at[place], 8, passed.at[3], partner)

    def gather_send(k):
        return remote(
            res.at[slot(k)], mean.at[kept_rows(k // 2)], 5, gathered.at[k // 2], beside(k % 2))

    def gather_total():
        return remote(res, mean, 5, gathered.at[0], beside(0))

    def gather_recv(j):
        return remote(
            res.at[slot(2 * j)], mean.at[given_rows(j)], 5, gathered.at[j], beside(0))

    def deliver_send(j):
        return remote(res.at[slot(2 * j)], mean.at[kept_rows(j)], 6, first.at[j], partner)

    def deliver_total():
        return remote(
            res.at[pl.ds(0, half)], mean.at[pl.ds(0, half)], 6, first.at[0], partner)

    def outer_send(k):
        return remote(pout.at[slot(k)], pin.at[slot(k)], 7, rail.at[k], pair)

    def middle_send(k):
        return remote(pout.at[slot(k)], qin.at[slot(k)], 7, cross.at[k], middle)

    def part_total():
        return remote(pout, pin, 7, rail.at[0], pair)

    def result_send(k):
        return remote(res.at[slot(k)], res.at[slot(k)], 8, rail.at[k], pair)

    def result_total():
        return remote(res, res, 8, rail.at[0], pair)

    state_loads = [
        pltpu.make_async_copy(place, dst, load_sem.at[3 + index])
        for index, (place, dst) in enumerate((
            (m_hbm, m), (s_hbm, s), (gw_hbm, gw), (om_hbm, om),
            (w_hbm.at[pl.ds(rows - late.shape[0], late.shape[0])], late)))
    ]

    def turn(out, tokens_by_width, base, start, tile):
        columns = pl.ds(pl.multiple_of(base + start, tile), tile)
        out[pl.ds(start, tile), :] = tokens_by_width[:, columns].T

    def turn_all(out, tokens_by_width, base):
        tile = min(256, rows)

        @pl.loop(0, rows // tile)
        def _(t):
            turn(out, tokens_by_width, base, pl.multiple_of(t * tile, tile), tile)

    def own_gradient():
        tile = min(256, rows)

        @pl.loop(0, rows // tile)
        def _(t):
            place = pl.ds(pl.multiple_of(t * tile, tile), tile)
            grad[place, :] = jnp.dot(xct[place, :], kg[...], preferred_element_type=f32)

    def gradient_tile(base, start, tile):
        place = pl.ds(start, tile)
        grad[place, :] += jnp.dot(xint[place, :], kgin[...], preferred_element_type=f32)
        if start >= nf.shape[0]:
            return
        step = min(32, tile)

        @pl.loop(0, tile // step)
        def _(u):
            place = pl.ds(pl.multiple_of(start + u * step, step), step)
            current = wc[pl.ds(pl.multiple_of(base + start + u * step, step), step), :]
            first_new, second_new, inner = inner_step(
                grad[place, :], m[place, :], s[place, :], current)
            nf[place, :] = first_new
            ns[place, :] = second_new
            half_inner[place, :] = inner

    def inner_update(base):
        tile = min(256, rows)
        for t in range(rows // tile):
            gradient_tile(base, t * tile, tile)

    def matmul(out, place, left, convert):
        part = min(256, width)

        @pl.loop(0, width // part)
        def _(n):
            columns = pl.ds(pl.multiple_of(n * part, part), part)
            value = jnp.dot(left[...], wc[:, columns], preferred_element_type=f32)
            out[place, columns] = value.astype(bf16) if convert else value

    steps = range(len(splits))

    every = slice(None)

    @pl.when(core == 0)
    def _():
        for j in groups:
            scatter_send(0, j).start()
            if j < 3:
                keep_send(j).start()
        for i in steps:
            own_tokens_up(i).start()
        for load in state_loads:
            load.start()
        reach_across()
        for i in steps[:2]:
            token_send(0, i).start()
        wload.wait()
        tokens_loaded()
        weight_send.wait_recv()
        own_tokens_down_total().wait_recv()
        matmul(own, every, xc, False)
        turn_all(xct, xc, 0)
        for i in steps:
            token_send(0, i).wait_recv()
            token_send(1, i).wait_recv()
            tokens_forward(both(i)).start()
            matmul(psend, both(i), xin.at[both(i)], True)
            partial_send(both(i), i).start()
            if i == 0:
                for later in steps[2:]:
                    token_send(0, later).start()
        cotangent_total().wait_recv()
        for i in steps:
            partial_send(both(i), i).wait_recv()
            for head in range(width // HEAD_DIM):
                columns = slice(head * HEAD_DIM, (head + 1) * HEAD_DIM)
                keys = (own[both(i), columns] + precv[both(i), columns].astype(f32)) * scale
                kg[both(i), columns] = head_backward(
                    keys, cot[both(i), columns].astype(f32), scale)
            upstream_across(both(i), i).start()
            upstream_down(both(i)).start()
        own_gradient()
        turn_all(xint, xin, 0)
        for i in steps:
            upstream_across(both(i), i).wait_recv()
            upstream_forward(both(i)).start()
        for load in state_loads:
            load.wait()
        inner_update(0)
        for j in groups:
            deliver_send(j).wait_recv()
            gather_recv(j).wait_recv()
        for total in (scatter_total(), token_total(), keep_total(), own_tokens_up_total(),
                      tokens_forward(every), partial_send(every, 0), upstream_across(every, 0),
                      upstream_down(every), upstream_forward(every)):
            total.wait_send()

    @pl.when(core == 1)
    def _():
        def held(k):
            j = k // 2
            place = pl.ds(pl.multiple_of((k % 2) * rows + kept(j), 16), pieces[j])
            return wc[place, :].astype(f32) + rsin[slot(k), :].astype(f32)

        def hand_out(k):
            gather_send(k).start()
            j = k // 2
            if k % 2:
                mean[kept_rows(j), :] = res[slot(k), :]
            else:
                deliver_send(j).start()

        for j in groups:
            scatter_send(1, j).start()
        weight_send.start()
        for i in steps:
            own_tokens_down(i).start()
            cotangent_down(i).start()
        for load in state_loads:
            load.start()
        reach_across()
        for i in steps:
            token_send(1, i).start()
        wload.wait()

        def arrived(k):
            scatter_send(k % 2, k // 2).wait_recv()
            if k % 2 == 0 and k < 6:
                keep_send(k // 2).wait_recv()

        def outer_part(k):
            arrived(k)
            pout[slot(k), :] = held(k).astype(bf16)
            outer_send(k).start()

        def outer_result(k):
            result_send(k).wait_recv()
            hand_out(k)

        def middle_part(k):
            arrived(k)
            outer_send(k).wait_recv()
            pout[slot(k), :] = (held(k) + pin[slot(k), :].astype(f32)).astype(bf16)
            middle_send(k).start()

        def middle_result(k):
            middle_send(k).wait_recv()
            total = pout[slot(k), :].astype(f32) + qin[slot(k), :].astype(f32)
            res[slot(k), :] = (total / islands).astype(bf16)
            result_send(k).start()
            hand_out(k)

        tile = min(256, rows)
        tiles = rows // tile

        def own_tokens_ready():
            tokens_loaded()
            own_tokens_up_total().wait_recv()

        def gradient_start():
            upstream_down(every).wait_recv()
            own_gradient()

        def gradient_ready():
            upstream_forward(every).wait_recv()
            for load in state_loads:
                load.wait()

        ends = [2 * begins[k // 2] + (1 + k % 2) * pieces[k // 2] for k in range(count)]

        def interleave(first, second, lag, turn_at, own_at, tiles_at):
            unit = rows // 16
            work = []
            work.append((turn_at * unit, tokens_forward(every).wait_recv))
            for t in range(tiles):
                work.append(((turn_at + t) * unit, functools.partial(
                    turn, xint, xin, rows, t * tile, tile)))
            work.append((turn_at * unit, own_tokens_ready))
            for t in range(tiles):
                work.append(((turn_at + t) * unit, functools.partial(
                    turn, xct, xc, rows, t * tile, tile)))
            work.append((own_at * unit, gradient_start))
            work.append((tiles_at * unit, gradient_ready))
            for t in range(tiles):
                work.append(((tiles_at + t) * unit, functools.partial(
                    gradient_tile, rows, t * tile, tile)))
            done = 0
            for k in range(count + 1):
                if k < count:
                    first(k)
                limit = rows * 2 if k == count else ends[k] - lag * rows // 16
                while done < count and ends[done] <= limit:
                    second(done)
                    while work and work[0][0] <= ends[done]:
                        work.pop(0)[1]()
                    done += 1
            for item in work:
                item[1]()

        @pl.when(inside == 0)
        def _():
            interleave(outer_part, outer_result, 16, 14, 14, 16)

        @pl.when(inside == 1)
        def _():
            interleave(middle_part, middle_result, 4, 16, 16, 16)

        for j in groups:
            gather_recv(j).wait_recv()

        @pl.when(inside == 1)
        def _():
            result_total().wait_send()

        for total in (scatter_total(), token_total(), weight_send, own_tokens_down_total(),
                      cotangent_total(), gather_total(), deliver_total(), part_total()):
            total.wait_send()


def finish(first, second, half_inner, mean, gw, om, grad, m, s, late, nl, nf, ns, ng, nm, local,
           weights, momenta, first_late, second_late, sems):
    rows = mean.shape[0]
    early = first.shape[0]
    tile = min(128, early)
    step = min(32, tile)
    f32 = jnp.float32
    begin = pl.ds(0, early)
    rest = pl.ds(early, rows - early)
    pltpu.make_async_copy(first, nf.at[begin], sems.at[0]).start()
    pltpu.make_async_copy(second, ns.at[begin], sems.at[1]).start()
    for t in range(rows // tile):
        after = t * tile - early

        @pl.loop(0, tile // step)
        def _(u):
            place = pl.ds(pl.multiple_of(t * tile + u * step, step), step)
            if after < 0:
                inner = half_inner[place, :]
            else:
                behind = pl.ds(pl.multiple_of(after + u * step, step), step)
                first_new, second_new, inner = inner_step(
                    grad[place, :], m[place, :], s[place, :], late[behind, :])
                first_late[behind, :] = first_new
                second_late[behind, :] = second_new
            current = gw[place, :]
            outer_grad = current - mean[place, :].astype(f32)
            momentum = outer_beta * om[place, :] + outer_grad
            updated = current - outer_rate * (outer_grad + outer_beta * momentum)
            momenta[place, :] = momentum
            weights[place, :] = updated
            local[place, :] = (inner + (1.0 - merge_weight) * updated).astype(jnp.bfloat16)

        part = pl.ds(t * tile, tile)
        if after >= 0:
            behind = pl.ds(after, tile)
            pltpu.make_async_copy(first_late.at[behind], nf.at[part], sems.at[5]).start()
            pltpu.make_async_copy(second_late.at[behind], ns.at[part], sems.at[6]).start()
        pltpu.make_async_copy(local.at[part], nl.at[part], sems.at[2]).start()
        pltpu.make_async_copy(weights.at[part], ng.at[part], sems.at[3]).start()
        pltpu.make_async_copy(momenta.at[part], nm.at[part], sems.at[4]).start()
    pltpu.make_async_copy(first, nf.at[begin], sems.at[0]).wait()
    pltpu.make_async_copy(second, ns.at[begin], sems.at[1]).wait()
    pltpu.make_async_copy(local, nl, sems.at[2]).wait()
    pltpu.make_async_copy(weights, ng, sems.at[3]).wait()
    pltpu.make_async_copy(momenta, nm, sems.at[4]).wait()
    pltpu.make_async_copy(first_late, nf.at[rest], sems.at[5]).wait()
    pltpu.make_async_copy(second_late, ns.at[rest], sems.at[6]).wait()


def fused(pieces, local_weights, adam_first, adam_second, global_weights, outer_momentum, inputs,
          key_cotangent):
    arrays = (local_weights[0], adam_first[0], adam_second[0], global_weights, outer_momentum,
              inputs[0], key_cotangent[0])
    rows, width = arrays[0].shape
    count, depth = arrays[5].shape
    islands = lax.axis_size("island")
    splits = token_splits(count)
    groups = len(pieces)
    bf16, f32 = jnp.bfloat16, jnp.float32
    dma, vmem = pltpu.SemaphoreType.DMA, pltpu.VMEM
    narrow = jax.ShapeDtypeStruct((rows, width), bf16)
    wide = jax.ShapeDtypeStruct((rows, width), f32)
    early = rows // 4
    part = jax.ShapeDtypeStruct((early, width), bf16)
    carried = [part, part, jax.ShapeDtypeStruct((early, width), f32), narrow, wide, wide, wide,
               narrow, narrow, jax.ShapeDtypeStruct((rows - early, width), bf16)]
    out_shape = [narrow] * 3 + [wide] * 2
    steps = len(splits)
    scratch = [
        vmem((2 * rows, width), bf16),
        vmem((2 * count, 2 * rows), bf16),
        vmem((2 * count, 2 * rows), bf16),
        vmem((2 * count, width), bf16),
        vmem((2 * count, width), f32),
        vmem((2 * count, width), bf16),
        vmem((2 * count, width), bf16),
        vmem((2 * count, width), bf16),
        vmem((2 * count, width), bf16),
        vmem((rows, 2 * count), bf16),
        vmem((rows, 2 * count), bf16),
    ] + [vmem((rows, width), bf16)] * 5 + [
        dma((8,)),
        dma((9,)),
        dma((max(2 * groups, groups + 2 * steps),)),
        dma((max(2 * groups, 2 * steps),)),
        dma((2 * groups,)),
        dma((groups,)),
        dma((min(groups, 3),)),
        dma((4,)),
        pltpu.SemaphoreType.REGULAR,
    ]
    in_vmem = pl.BlockSpec(memory_space=pltpu.VMEM)
    in_hbm = pl.BlockSpec(memory_space=pltpu.HBM)
    results = pl.pallas_call(
        functools.partial(window, islands, pieces, splits, float(depth) ** (-0.5)),
        out_shape=carried,
        in_specs=[in_hbm] * len(arrays),
        out_specs=[in_vmem] * len(carried),
        scratch_shapes=scratch,
        compiler_params=pltpu.CompilerParams(
            collective_id=0, has_side_effects=True, vmem_limit_bytes=40 * 1024 * 1024
        ),
    )(*(pltpu.with_memory_space_constraint(a, pltpu.HBM) for a in arrays))
    written = pl.pallas_call(
        finish,
        out_shape=out_shape,
        in_specs=[in_vmem] * len(carried),
        out_specs=[in_hbm] * len(out_shape),
        scratch_shapes=[
            vmem((rows, width), bf16),
            vmem((rows, width), f32),
            vmem((rows, width), f32),
            vmem((rows - early, width), bf16),
            vmem((rows - early, width), bf16),
            dma((7,)),
        ],
        compiler_params=pltpu.CompilerParams(vmem_limit_bytes=8 * 1024 * 1024),
    )(*results)
    return tuple(a[None] for a in written[:3]) + tuple(written[3:])


def local(
    local_weights, adam_first, adam_second, global_weights, outer_momentum, inputs, key_cotangent
):
    weights = local_weights[0]
    tokens = inputs[0]
    rows, width = weights.shape
    count, depth = tokens.shape
    scale = float(depth) ** (-0.5)
    islands, shards = lax.axis_size("island"), lax.axis_size("fsdp")
    chips = shards // 2
    others = max(chips - 1, 1)
    pieces = pieces_of(rows, islands, shards)
    if pieces and width % HEAD_DIM == 0:
        return fused(pieces, local_weights, adam_first, adam_second, global_weights,
                     outer_momentum, inputs, key_cotangent)
    chunks = chunk_count(rows, islands)
    bf16, f32 = jnp.bfloat16, jnp.float32
    dma = pltpu.SemaphoreType.DMA
    out_shape = [jax.ShapeDtypeStruct((rows, width), f32)]
    scratch = [
        pltpu.VMEM((rows, width), bf16),
        pltpu.VMEM((count, depth), bf16),
        pltpu.VMEM((count, width), bf16),
        dma((3,)),
        pltpu.VMEM((rows, width), bf16),
        pltpu.VMEM((others, count, 2 * rows), bf16),
        pltpu.VMEM((chips, count, rows), bf16),
        pltpu.VMEM((others, count, width), bf16),
        pltpu.VMEM((others, count, width), bf16),
        pltpu.VMEM((others, count, width), bf16),
        pltpu.VMEM((chips, count, width), bf16),
        pltpu.VMEM((count, width), bf16),
        pltpu.VMEM((count, width), f32),
        dma((2, others)),
        dma((2, others)),
        dma((2, others)),
        dma((2, chips + 1)),
        dma((2, chips)),
    ]
    if chunks:
        levels = islands.bit_length() - 1
        out_shape.append(jax.ShapeDtypeStruct((rows, width), bf16))
        scratch += [
            pltpu.VMEM((chunks, rows // chunks, width), bf16),
            pltpu.VMEM((rows, width), bf16),
            pltpu.VMEM((rows, width), bf16),
            dma((2, chunks, 2 * levels)),
        ]
    vmem = pl.BlockSpec(memory_space=pltpu.VMEM)
    results = pl.pallas_call(
        functools.partial(exchange, islands, shards, chunks, scale),
        out_shape=out_shape,
        in_specs=[pl.BlockSpec(memory_space=pltpu.HBM)] * 3,
        out_specs=[vmem] * len(out_shape),
        scratch_shapes=scratch,
        compiler_params=pltpu.CompilerParams(
            collective_id=0, has_side_effects=True, vmem_limit_bytes=40 * 1024 * 1024
        ),
    )(*(pltpu.with_memory_space_constraint(a, pltpu.HBM) for a in (weights, tokens, key_cotangent[0])))
    gradient = results[0]
    if chunks:
        mean_local = results[1].astype(jnp.float32)
    else:
        mean_local = lax.psum(weights.astype(jnp.float32), "island") / islands
    outer_grad = global_weights - mean_local
    new_momentum = outer_beta * outer_momentum + outer_grad
    new_global = global_weights - outer_rate * (outer_grad + outer_beta * new_momentum)
    first_new = beta_one * adam_first[0].astype(jnp.float32) + (1.0 - beta_one) * gradient
    second_new = (
        beta_two * adam_second[0].astype(jnp.float32) + (1.0 - beta_two) * gradient * gradient
    )
    current = weights.astype(jnp.float32)
    inner = current - inner_rate * (
        first_new / (jnp.sqrt(second_new) + adam_epsilon) + weight_decay * current
    )
    merged = merge_weight * inner + (1.0 - merge_weight) * new_global
    return (
        merged.astype(jnp.bfloat16)[None],
        first_new.astype(jnp.bfloat16)[None],
        second_new.astype(jnp.bfloat16)[None],
        new_global,
        new_momentum,
    )


def solution(mesh):
    placed = (
        P("island", "fsdp", None),
        P("island", "fsdp", None),
        P("island", "fsdp", None),
        P("fsdp", None),
        P("fsdp", None),
        P("island", "fsdp", None),
        P("island", "fsdp", None),
    )
    return jax.shard_map(
        local,
        mesh=mesh,
        in_specs=placed,
        out_specs=(
            P("island", "fsdp", None),
            P("island", "fsdp", None),
            P("island", "fsdp", None),
            P("fsdp", None),
            P("fsdp", None),
        ),
        check_vma=False,
    )
```
